32 devices in a mesh: row: 8 (over z, y), col: 4 (over x, core).
Axes of the slice: x: 2, y: 2, z: 4, core: 2. Of those that a mesh axis runs over, the one named last changes fastest.
Arguments:
- ancestor_inverse: float32 [12288, 12288], P('row', 'col'), may hold values from -5 to 320, as said below
- panel_one: float32 [12288, 256], P(('row', 'col')), may hold values from -0.015625 to 0.015625
- struct_one: int32 [10752], replicated, may hold values from 0 to 12287, as said below
- lower_one: float32 [256, 256], replicated, may hold values from -1 to 2, as said below
- panel_two: float32 [12288, 256], P(('row', 'col')), may hold values from -0.015625 to 0.015625
- struct_two: int32 [9216], replicated, may hold values from 0 to 12287, as said below
- panel_above: float32 [256, 256], replicated, may hold values from -0.375 to 0.375
- lower_two: float32 [256, 256], replicated, may hold values from -1 to 2, as said below
- tile_owner: int32 [192, 1], P(('col', 'row')), may hold values from 0 to 3; in each aligned block of 6 rows (0 to 5, 6 to 11, ...) at most 2 rows name the same one
Outputs:
- inverse_one: float32 [12288, 256], P(('col', 'row'))
- diag_one: float32 [256, 256], replicated
- cross_two: float32 [256, 256], replicated
- diag_two: float32 [256, 256], replicated
- delivered: float32 [256, 64, 256], P(('row', 'col'))
The draws below stay inside these ranges and needn't reach their ends.
Inputs may be any that keep to these rules, and one draw needn't show every extreme that they name: ancestor_inverse is exactly symmetric and positive definite. `struct_one`: 10752 distinct row numbers of the ancestor block. `struct_two`: 9216 distinct entries of struct_one. `lower_one`: lower triangular with a positive diagonal. `lower_two`: lower triangular with a positive diagonal. `tile_owner`: within each aligned block of 6 entries (the tiles of one device) no value appears more than 2 times; in some block a value appears exactly 2 times.
All inputs are finite; a program needn't handle non-finite values.
Results may differ from the reference program's by a relative error of at most 0.00007.
Values sent between devices are 32-bit elements; how exact they have to be, the bound alone decides.
A program may use at most 64 MiB of HBM per device.

```python
import math
import jax
import jax.numpy as jnp
import numpy as np
from jax import lax

ANC = 12288
SUPER = 256
R_ONE = 10752
R_TWO = 9216
TILES_DEV = 6
CAP = 2
N_ROW = 8
N_COL = 4
DEVICES = 32


def draw_ancestor_inverse(key, part):
    first, second = jax.random.split(jax.random.fold_in(key, 11), 2)
    entries = jax.random.truncated_normal(first, -6.0, 6.0, (ANC, ANC), jnp.float32)
    upper_part = jnp.triu(entries, 1)
    diagonal_values = jax.random.uniform(second, (ANC,), jnp.float32, 2.5, 5.0)
    matrix = 16.0 * (jnp.diag(diagonal_values) + 0.8 / (2.0 * ANC) ** 0.5 * (upper_part + upper_part.T))
    return matrix


def structure_lists(key):
    first, second, third = jax.random.split(jax.random.fold_in(key, 23), 3)
    positions = jnp.arange(ANC, dtype=jnp.int32)
    region = positions // (ANC // 16)
    base_score = jax.random.randint(first, (ANC,), 0, 2 ** 14, dtype=jnp.int32)
    region_lift = jax.random.randint(second, (16,), 0, 2 ** 15, dtype=jnp.int32)
    scores = (base_score + region_lift[region]) * ANC + positions
    chosen = lax.top_k(scores, R_ONE)[1].astype(jnp.int32)
    shuffle = jax.random.permutation(third, R_ONE)
    return (chosen, chosen[shuffle[:R_TWO]].astype(jnp.int32))


def draw_struct_one(key, part):
    return structure_lists(key)[0]


def draw_struct_two(key, part):
    return structure_lists(key)[1]


def lower_factor(key):
    first, second = jax.random.split(key, 2)
    lower_part = jnp.tril(jax.random.truncated_normal(first, -4.0, 4.0, (SUPER, SUPER), jnp.float32) * (0.5 / SUPER ** 0.5), -1)
    diagonal_values = jnp.exp(jax.random.uniform(second, (SUPER,), jnp.float32, math.log(0.5), math.log(2.0)))
    return lower_part + jnp.diag(diagonal_values)


def draw_lower_one(key, part):
    return lower_factor(jax.random.fold_in(key, 31))


def draw_lower_two(key, part):
    return lower_factor(jax.random.fold_in(key, 37))


def level_of(own_key, dims, shards, low, high):
    def one(axis_at, shards_of):
        heights = jax.random.uniform(jax.random.fold_in(jax.random.fold_in(own_key, 6), axis_at), (shards_of,), jnp.float32, low / len(shards), high / len(shards))
        return jnp.repeat(jnp.exp(heights), dims[axis_at] // shards_of).reshape((-1,) + (1,) * (len(dims) - axis_at - 1))

    loudness = one(*shards[0])
    for cut in shards[1:]:
        loudness = loudness * one(*cut)
    return loudness


def assign_block(key, own, number, rows, amount, top, most, skew):
    ranking = jax.random.permutation(key, amount)
    heavy_load, common = shares(amount, rows * top, most, skew, True), shares(amount, rows * top, most, skew, False)
    places = jnp.arange(amount)

    def named(tallies, turn):
        used = int((tallies > 0).sum())
        fixed = max(1, used // 4)
        shifted = fixed + (places - fixed + turn * (used - fixed)) % max(1, amount - fixed)
        return jnp.zeros((amount,), jnp.int32).at[ranking[jnp.where(places < fixed, places, shifted)]].set(jnp.asarray(tallies, jnp.int32))

    tallies = jnp.where(number % 4 == 0, named(heavy_load, number // 4), named(common, number - number // 4 - 1))
    mixed = jax.random.permutation(jax.random.fold_in(own, 3), amount)
    giver, receiver = mixed[0:amount // 2 * 2:2], mixed[1:amount // 2 * 2:2]
    slack = jnp.minimum(tallies[giver] - 1, most - tallies[receiver]) // 2
    slack = jnp.where((giver == ranking[0]) | (receiver == ranking[0]) | (tallies[receiver] == 0), 0, jnp.maximum(slack, 0))
    shifted = jax.random.randint(jax.random.fold_in(own, 4), (amount // 2,), 0, 1 << 20) % (slack + 1)
    tallies = tallies.at[giver].add(-shifted).at[receiver].add(shifted)
    members = jnp.searchsorted(jnp.cumsum(tallies), jnp.arange(rows * top), side="right").astype(jnp.int32)
    grid = members.reshape(top, rows).T
    grid = grid[jax.random.permutation(jax.random.fold_in(own, 1), rows)]
    turn = jax.random.randint(jax.random.fold_in(own, 2), (rows, 1), 0, top)
    return jnp.take_along_axis(grid, (jnp.arange(top)[None, :] + turn) % top, axis=1)


def shares(count, total, bound, skew, full):
    weights = [(1 << 20) // math.isqrt(grade ** skew) + 1 for grade in range(1, count + 1)]
    largest = bound if full else min(bound, max(-(-total // count), total * weights[0] // sum(weights)))
    least = 1 if total - largest >= count - 1 else 0
    counts, rest = [largest] + [least] * (count - 1), total - largest - least * (count - 1)
    while rest > 0:
        free = [i for i in range(1, count) if counts[i] < largest] or [i for i in range(1, count) if counts[i] < bound]
        whole, left = sum([weights[i] for i in free]), rest
        for i in free:
            extra = min(bound - counts[i], max(1, left * weights[i] // whole), rest)
            counts[i] = counts[i] + extra
            rest = rest - extra
    return np.array(counts)


def normal_values(own_key, extent, deviation, limit, cuts=(), held_as=jnp.bfloat16):
    level = level_of(own_key, extent, cuts, -0.22, 0.18) if cuts else 1.0
    drawn = jax.random.normal(own_key, extent, jnp.float32) * deviation * level
    return jnp.minimum(jnp.maximum(drawn, -limit), limit).astype(held_as)


def setup_inputs(seed: int = 0) -> dict:
    splits = jax.random.split(jax.random.key(seed), 10)
    ancestor_inverse = draw_ancestor_inverse(jax.random.fold_in(splits[9], 71), 0)
    panel_one = normal_values(splits[1], (ANC, SUPER), (15 * R_ONE) ** -0.5, 0.015625, ((0, 32),), jnp.float32)
    struct_one = draw_struct_one(jax.random.fold_in(splits[9], 71), 0)
    lower_one = draw_lower_one(jax.random.fold_in(splits[9], 71), 0)
    panel_two = normal_values(splits[4], (ANC, SUPER), (15 * R_TWO) ** -0.5, 0.015625, ((0, 32),), jnp.float32)
    struct_two = draw_struct_two(jax.random.fold_in(splits[9], 71), 0)
    panel_above = normal_values(splits[6], (SUPER, SUPER), SUPER ** -0.5, 0.375, (), jnp.float32)
    lower_two = draw_lower_two(jax.random.fold_in(splits[9], 71), 0)
    tile_owner_keys = jax.random.split(jax.random.fold_in(splits[8], 1), (DEVICES * TILES_DEV) // TILES_DEV)
    tile_owner_turns = jax.random.permutation(jax.random.fold_in(splits[8], 3), (DEVICES * TILES_DEV) // TILES_DEV)
    tile_owner = jax.vmap(lambda own, number: assign_block(jax.random.fold_in(splits[8], 2), own, number, TILES_DEV, N_COL, 1, CAP, 2))(tile_owner_keys, tile_owner_turns).reshape((DEVICES * TILES_DEV, 1))
    return dict(ancestor_inverse=ancestor_inverse, panel_one=panel_one, struct_one=struct_one, lower_one=lower_one, panel_two=panel_two, struct_two=struct_two, panel_above=panel_above, lower_two=lower_two, tile_owner=tile_owner)


def matmul(left, right):
    return jnp.dot(left, right, precision=lax.Precision.HIGHEST, preferred_element_type=jnp.float32)


def deliver(values, tile_owner):
    tile_rows = ANC // (N_ROW * N_COL * TILES_DEV)
    tile_count = ANC // tile_rows
    all_tiles = values.reshape(tile_count, tile_rows, SUPER)
    owner_col = tile_owner[:, 0].astype(jnp.int32)
    onehot = (owner_col[:, None] == jnp.arange(N_COL, dtype=jnp.int32)[None, :]).astype(jnp.int32)
    grouped = onehot.reshape(tile_count // TILES_DEV, TILES_DEV, N_COL)
    earlier = jnp.cumsum(grouped, axis=1) - grouped
    tile_rank = jnp.sum(earlier * grouped, axis=2).reshape(tile_count)
    tile_group = jnp.arange(tile_count, dtype=jnp.int32) // TILES_DEV
    source_row = tile_group % N_ROW
    source_col = tile_group // N_ROW
    target = ((source_row * N_COL + owner_col) * N_COL + source_col) * CAP + tile_rank
    empty_slots = jnp.zeros((N_ROW * N_COL * N_COL * CAP, tile_rows, SUPER), jnp.float32)
    return empty_slots.at[target.astype(jnp.int32)].set(all_tiles)


def reference(ancestor_inverse, panel_one, struct_one, lower_one, panel_two, struct_two, panel_above, lower_two, tile_owner):
    mask_one = jnp.zeros((ANC,), jnp.float32).at[struct_one].set(1.0)
    mask_two = jnp.zeros((ANC,), jnp.float32).at[struct_two].set(1.0)
    masked_one = panel_one * mask_one[:, None]
    masked_two = panel_two * mask_two[:, None]
    inverse_one = -matmul(ancestor_inverse, masked_one) * mask_one[:, None]
    diag_one = matmul(lower_one.T, lower_one) - matmul(masked_one.T, inverse_one)
    inverse_two = -(matmul(ancestor_inverse, masked_two) + matmul(inverse_one, panel_above)) * mask_two[:, None]
    cross_two = -(matmul(inverse_one.T, masked_two) + matmul(diag_one, panel_above))
    diag_two = matmul(lower_two.T, lower_two) - matmul(masked_two.T, inverse_two) - matmul(panel_above.T, cross_two)
    delivered = deliver(inverse_two, tile_owner)
    return inverse_one, diag_one, cross_two, diag_two, delivered
```

```python
import functools

import jax
import jax.numpy as jnp
from jax import lax
from jax.experimental import pallas as pl
from jax.experimental.pallas import tpu as pltpu
from jax.sharding import PartitionSpec as P

CAP = 2


def matmul(left, right):
    return jnp.dot(left, right, precision=lax.Precision.HIGHEST, preferred_element_type=jnp.float32)


def contract_rows(left, right, precision=lax.Precision.HIGHEST):
    return lax.dot_general(
        left,
        right,
        (((0,), (0,)), ((), ())),
        precision=precision,
        preferred_element_type=jnp.float32,
    )


def row_mask(struct, count):
    lanes = 128
    high = struct // lanes
    low = struct % lanes
    high_hot = (jnp.arange(count // lanes, dtype=jnp.int32)[:, None] == high[None, :]).astype(jnp.bfloat16)
    low_hot = (jnp.arange(lanes, dtype=jnp.int32)[:, None] == low[None, :]).astype(jnp.bfloat16)
    counts = lax.dot_general(high_hot, low_hot, (((1,), (1,)), ((), ())), preferred_element_type=jnp.float32)
    return (counts > 0.5).astype(jnp.float32).reshape(count)


MESH = pl.DeviceIdType.MESH


def greet(peers):
    barrier = pltpu.get_barrier_semaphore()
    for peer in peers:
        pl.semaphore_signal(barrier, inc=1, device_id=peer, device_id_type=MESH)
    pl.semaphore_wait(barrier, len(peers))


def scatter_kernel(rows, value_ref, out_ref, pair_in, total, major_in, pair_send, pair_recv, major_send, major_recv):
    majors = rows // 2
    row = lax.axis_index("row")
    col = lax.axis_index("col")
    major, minor = row // 2, row % 2
    partner = (major * 2 + 1 - minor, col)

    def peer(offset):
        return (lax.rem(major + offset, majors) * 2 + minor, col)

    greet([partner] + [peer(offset) for offset in range(1, majors)])
    order = sorted(range(1, majors), key=lambda offset: -min(offset, majors - offset)) + [0]
    started = []
    pair_copies = {}
    for offset in order:
        target = lax.rem(major + offset, majors)
        copy = pltpu.make_async_remote_copy(
            src_ref=value_ref.at[target * 2 + 1 - minor],
            dst_ref=pair_in.at[offset],
            send_sem=pair_send.at[offset],
            recv_sem=pair_recv.at[offset],
            device_id=partner,
            device_id_type=MESH,
        )
        copy.start()
        pair_copies[offset] = copy
    for offset in order:
        target = lax.rem(major + offset, majors)
        pair_copies[offset].wait_recv()
        total[offset] = pair_in[offset] + value_ref[target * 2 + minor]
        if offset:
            copy = pltpu.make_async_remote_copy(
                src_ref=total.at[offset],
                dst_ref=major_in.at[offset - 1],
                send_sem=major_send.at[offset - 1],
                recv_sem=major_recv.at[offset - 1],
                device_id=peer(offset),
                device_id_type=MESH,
            )
            copy.start()
            started.append(copy)
    for copy in started:
        copy.wait_recv()
    result = total[0]
    for slot in range(majors - 1):
        result = result + major_in[slot]
    out_ref[...] = result
    for copy in started:
        copy.wait_send()
    for offset in order:
        pair_copies[offset].wait_send()


def scatter_rows(value, rows):
    chunk, width = value.shape[0] // rows, value.shape[1]
    majors = rows // 2
    dma = pltpu.SemaphoreType.DMA
    return pl.pallas_call(
        functools.partial(scatter_kernel, rows),
        out_shape=jax.ShapeDtypeStruct((chunk, width), jnp.float32),
        in_specs=[pl.BlockSpec(memory_space=pltpu.VMEM)],
        out_specs=pl.BlockSpec(memory_space=pltpu.VMEM),
        scratch_shapes=[
            pltpu.VMEM((majors, chunk, width), jnp.float32),
            pltpu.VMEM((majors, chunk, width), jnp.float32),
            pltpu.VMEM((majors - 1, chunk, width), jnp.float32),
            dma((majors,)),
            dma((majors,)),
            dma((majors - 1,)),
            dma((majors - 1,)),
        ],
        compiler_params=pltpu.CompilerParams(
            collective_id=0, has_side_effects=True, vmem_limit_bytes=40 * 2**20
        ),
    )(value.reshape(rows, chunk, width))


def sum_kernel(rows, cols, value_ref, out_ref, full, sum_a, sum_b, in_a, in_b, in_c, *sems):
    row = lax.axis_index("row")
    col = lax.axis_index("col")
    outer = cols // 2
    far, core = col // 2, col % 2
    half = outer * rows
    base_a = core * half
    base_b = base_a + far * rows
    base_c = base_b + row

    def pair_peer(offset):
        return (row, far * 2 + 1 - core)

    def far_peer(offset):
        return (row, lax.rem(far + offset, outer) * 2 + core)

    def row_peer(offset):
        return (lax.rem(row + offset, rows), col)

    greet(
        [pair_peer(1)]
        + [far_peer(offset) for offset in range(1, outer)]
        + [row_peer(offset) for offset in range(1, rows)]
    )

    def exchange(count, peer, source, landing, stage):
        copies = []
        for offset in range(1, count):
            copy = pltpu.make_async_remote_copy(
                src_ref=source(offset),
                dst_ref=landing(offset),
                send_sem=sems[2 * stage].at[offset - 1],
                recv_sem=sems[2 * stage + 1].at[offset - 1],
                device_id=peer(offset),
                device_id_type=MESH,
            )
            copy.start()
            copies.append(copy)
        for copy in copies:
            copy.wait_recv()
        return copies

    pending = []
    pending += exchange(
        2, pair_peer, lambda k: value_ref.at[pl.ds((1 - core) * half, half)], lambda k: in_a.at[k - 1], 0
    )
    sum_a[...] = value_ref[pl.ds(base_a, half)] + in_a[0]
    pending += exchange(
        outer, far_peer, lambda k: sum_a.at[pl.ds(lax.rem(far + k, outer) * rows, rows)], lambda k: in_b.at[k - 1], 1
    )
    total = sum_a[pl.ds(far * rows, rows)]
    for slot in range(outer - 1):
        total = total + in_b[slot]
    sum_b[...] = total
    pending += exchange(
        rows, row_peer, lambda k: sum_b.at[lax.rem(row + k, rows)], lambda k: in_c.at[k - 1], 2
    )
    total = sum_b[row]
    for slot in range(rows - 1):
        total = total + in_c[slot]
    full[base_c] = total
    pending += exchange(rows, row_peer, lambda k: full.at[base_c], lambda k: full.at[base_c], 3)
    pending += exchange(
        outer, far_peer, lambda k: full.at[pl.ds(base_b, rows)], lambda k: full.at[pl.ds(base_b, rows)], 4
    )
    pending += exchange(
        2, pair_peer, lambda k: full.at[pl.ds(base_a, half)], lambda k: full.at[pl.ds(base_a, half)], 5
    )
    out_ref[...] = full[...]
    for copy in pending:
        copy.wait_send()


def sum_everywhere(value, rows, cols):
    devices = rows * cols
    lanes = value.shape[1]
    depth = value.shape[0] // devices
    outer = cols // 2
    dma = pltpu.SemaphoreType.DMA
    vmem = lambda *lead: pltpu.VMEM(lead + (depth, lanes), jnp.float32)
    total = pl.pallas_call(
        functools.partial(sum_kernel, rows, cols),
        out_shape=jax.ShapeDtypeStruct((devices, depth, lanes), jnp.float32),
        in_specs=[pl.BlockSpec(memory_space=pltpu.VMEM)],
        out_specs=pl.BlockSpec(memory_space=pltpu.VMEM),
        scratch_shapes=[
            vmem(devices),
            vmem(devices // 2),
            vmem(rows),
            vmem(1, devices // 2),
            vmem(outer - 1, rows),
            vmem(rows - 1),
        ]
        + [dma((count - 1,)) for count in (2, outer, rows, rows, outer, 2) for _ in range(2)],
        compiler_params=pltpu.CompilerParams(
            collective_id=1, has_side_effects=True, vmem_limit_bytes=24 * 2**20
        ),
        cost_estimate=pl.CostEstimate(flops=0, bytes_accessed=100 * value.size * 4, transcendentals=0),
    )(value.reshape(devices, depth, lanes))
    return total.reshape(value.shape)


def deliver(values, tile_owner, col_count):
    tile_count = tile_owner.shape[0]
    tile_rows = values.shape[0] // tile_count
    all_tiles = values.reshape(tile_count, tile_rows, values.shape[1])
    owner_col = tile_owner[:, 0]
    col_ids = jnp.arange(col_count, dtype=jnp.int32)
    onehot = (owner_col[:, None] == col_ids[None, :]).astype(jnp.int32)
    tile_rank = jnp.sum((jnp.cumsum(onehot, axis=0) - onehot) * onehot, axis=1)
    slot_index = jnp.arange(CAP, dtype=jnp.int32)
    select = (
        (owner_col[None, None, :] == col_ids[:, None, None])
        & (tile_rank[None, None, :] == slot_index[None, :, None])
    ).astype(jnp.float32)
    outgoing = jnp.einsum("cks,srb->ckrb", select, all_tiles, precision=lax.Precision.HIGHEST)
    incoming = lax.all_to_all(outgoing, "col", split_axis=0, concat_axis=0, tiled=True)
    return incoming.reshape(col_count * CAP, tile_rows, values.shape[1])


ROWS, COLS, CHIPS = 8, 4, 16
CHUNKS = 4
LANES = 128


def fits_fused(matrix, panel, struct_one, struct_two, tile_owner, rows, cols):
    span, width = panel.shape
    return (
        (rows, cols) == (ROWS, COLS)
        and span % LANES == 0
        and width == 2 * LANES
        and matrix.shape == (cols * span, rows * span)
        and struct_one.shape[0] % LANES == 0
        and struct_two.shape[0] % LANES == 0
        and span % (8 * tile_owner.shape[0]) == 0
    )


def exact(left, right, contract):
    return lax.dot_general(
        left, right, (contract, ((), ())), precision=lax.Precision.HIGHEST, preferred_element_type=jnp.float32
    )


def fused_kernel(
    matrix, panel_one, panel_two, struct_one, struct_two, lower_one, above, lower_two, owner,
    inverse_one, diag_one, cross_two, diag_two, delivered,
    window, high, low, own, land, left, other, mine, pair_in, major_in, masks, resident, product,
    packed, fold_in, fold, part_in, full, outgoing,
    fetch_sem, own_sem, move_sem, near_gather, far_gather, relay_gather, pair_sem, major_sem, sum_sem, chip_sem,
    spread_sem, tile_sem,
):
    row = lax.axis_index("row")
    col = lax.axis_index("col")
    z, y = row // 2, row % 2
    x, core = col // 2, col % 2
    upper, lower = z // 2, z % 2
    chip = (z * 2 + y) * 2 + x
    depth, total_columns = matrix.shape
    span, width = own.shape[1:]
    chunk = left.shape[1] // 2
    per_panel = width // chunk

    def device(z_at, y_at, x_at, core_at):
        return (z_at * 2 + y_at, x_at * 2 + core_at)

    partner = device(z, y, x, 1 - core)
    across = device(z, y, 1 - x, core)
    beside = device(z, 1 - y, x, core)
    near = device(upper * 2 + 1 - lower, y, x, core)
    away = device((1 - upper) * 2 + lower, y, x, core)

    def remote(source, target, sems, at, peer):
        return pltpu.make_async_remote_copy(
            src_ref=source,
            dst_ref=target,
            send_sem=sems.at[(0,) + at],
            recv_sem=sems.at[(1,) + at],
            device_id=peer,
            device_id_type=MESH,
        )

    own_copies = [
        pltpu.make_async_copy(panel, own.at[at], own_sem.at[at]) for at, panel in enumerate((panel_one, panel_two))
    ]
    for copy in own_copies:
        copy.start()

    def fetch(step, which):
        target_upper = lax.rem(upper + 1 + step // 2, 2)
        target_lower = lax.rem(lower + 1 + step, 2)
        target = (target_upper * 2 + target_lower) * 2 + lax.rem(1 - y + which, 2)
        return pltpu.make_async_copy(
            matrix.at[:, pl.ds(pl.multiple_of(target * span, LANES), span)], window.at[which], fetch_sem.at[which]
        )

    barrier = pltpu.get_barrier_semaphore()
    devices = ROWS * COLS
    for offset in range(1, devices):
        flat = lax.rem(row * COLS + col + offset, devices)
        pl.semaphore_signal(barrier, inc=1, device_id=(flat // COLS, lax.rem(flat, COLS)), device_id_type=MESH)
    for which in range(2):
        fetch(0, which).start()
    pl.semaphore_wait(barrier, devices - 1)
    for copy in own_copies:
        copy.wait()

    def piece(at):
        return own.at[at // per_panel, :, pl.ds(at % per_panel * chunk, chunk)]

    def far_copy(at, source=None):
        return remote(land.at[0, at] if source is None else source, land.at[col, at], far_gather, (at,), across)

    def near_copy(at, source=None):
        return remote(land.at[0, at] if source is None else source, land.at[col, at], near_gather, (at,), partner)

    def relay_copy(at):
        slot = (1 - x) * 2 + core
        return remote(land.at[slot, at], land.at[slot, at], relay_gather, (at,), partner)

    place = row * COLS + col
    move_row, move_col = lax.rem(place, ROWS), place // ROWS
    stays = (move_row == row) & (move_col == col)
    moved = remote(own, resident, move_sem, (), (move_row, move_col))
    kept = pltpu.make_async_copy(own, resident, move_sem.at[1])
    for at in range(CHUNKS):
        far_copy(at, piece(at)).start()
        near_copy(at, piece(at)).start()
        if at == 0:
            pl.when(stays)(lambda: kept.start())
            pl.when(jnp.logical_not(stays))(lambda: moved.start())
    for at in range(CHUNKS):
        land[col, at] = piece(at)[...]

    blocks = span // LANES
    slots_of = COLS * blocks
    mask_rows = masks.shape[1]
    place_rows = lax.broadcasted_iota(jnp.int32, (mask_rows, LANES), 0)
    block_base = row * slots_of
    result_base = (col * ROWS + row) * blocks
    wanted = jnp.where(place_rows < slots_of, block_base + place_rows, result_base + place_rows - slots_of)
    lane_ids = lax.broadcasted_iota(jnp.int32, (LANES, LANES), 0)
    for at, struct in enumerate((struct_one, struct_two)):
        count = struct.shape[0]
        group = max(size for size in range(1, 17) if count % size == 0)
        counts = jnp.zeros((mask_rows, LANES), jnp.float32)
        for begin in range(0, count, group):
            highs, lows = [], []
            for entry in range(begin, begin + group):
                value = struct[pl.ds(entry, 1), :]
                highs.append(jnp.where(wanted == value // LANES, 1.0, 0.0))
                lows.append(jnp.where(lane_ids == value % LANES, 1.0, 0.0))
            counts = counts + lax.dot_general(
                jnp.concatenate(highs, axis=1).astype(jnp.bfloat16),
                jnp.concatenate(lows, axis=1).astype(jnp.bfloat16),
                (((1,), (1,)), ((), ())),
                preferred_element_type=jnp.float32,
            )
        masks[at] = jnp.where(counts > 0.5, 1.0, 0.0)
    diag_one[...] = exact(lower_one[...].T, lower_one[...], ((1,), (0,)))
    diag_two[...] = exact(lower_two[...].T, lower_two[...], ((1,), (0,)))

    def mask_of(panel, begin):
        return jnp.concatenate([masks[panel, pl.ds(begin + at, 1), :] for at in range(blocks)], axis=1)

    def prepare(at):
        near_copy(at).wait_recv()
        far_copy(at).wait_recv()
        relay_copy(at).start()
        relay_copy(at).wait_recv()
        for slot in range(COLS):
            value = land[slot, at].T * mask_of(at // per_panel, slot * blocks)
            upper_part = value.astype(jnp.bfloat16)
            columns = pl.ds(slot * span, span)
            left[at, pl.ds(0, chunk), columns] = upper_part
            left[at, pl.ds(chunk, chunk), columns] = (value - upper_part.astype(jnp.float32)).astype(jnp.bfloat16)

    def pair_copy(at, step):
        return remote(other.at[at, step], pair_in.at[at, step], pair_sem, (at, step), beside)

    def multiply(at, step, which):
        target = step * 2 + which
        both = jnp.dot(left[at], high[target], preferred_element_type=jnp.float32)
        rest = jnp.dot(left[at, pl.ds(0, chunk), :], low[target], preferred_element_type=jnp.float32)
        value = both[:chunk] + (both[chunk:] + rest)
        if which == 0:
            other[at, step] = value
            pair_copy(at, step).start()
        else:
            mine[at, step] = value

    def first_step(step, carry):
        for which in range(2):
            fetch(step, which).wait()
            target = step * 2 + which
            for begin in range(0, depth, 256):
                size = min(256, depth - begin)
                value = window[which, pl.ds(begin, size), :]
                upper_part = value.astype(jnp.bfloat16)
                high[target, pl.ds(begin, size), :] = upper_part
                low[target, pl.ds(begin, size), :] = (value - upper_part.astype(jnp.float32)).astype(jnp.bfloat16)

            @pl.when(step + 1 < 4)
            def _():
                fetch(step + 1, which).start()

            multiply(0, step, which)
        return carry

    def later_steps(at):
        def body(step, carry):
            for which in range(2):
                multiply(at, step, which)
            return carry

        lax.fori_loop(0, 4, body, 0)

    def major_copy(at, slot, peer):
        return remote(mine.at[at, slot], major_in.at[at, slot], major_sem, (at, slot), peer)

    def collect(at):
        pair_copy(at, 0).wait_recv()
        mine[at, 0] = mine[at, 0] + pair_in[at, 0]
        major_copy(at, 0, near).start()
        pair_copy(at, 1).wait_recv()
        mine[at, 1] = mine[at, 1] + pair_in[at, 1]
        major_copy(at, 0, near).wait_recv()
        mine[at, 1] = mine[at, 1] + major_in[at, 0]
        major_copy(at, 1, away).start()
        pair_copy(at, 2).wait_recv()
        mine[at, 2] = mine[at, 2] + pair_in[at, 2]
        major_copy(at, 2, near).start()
        pair_copy(at, 3).wait_recv()
        value = mine[at, 3] + pair_in[at, 3]
        major_copy(at, 1, away).wait_recv()
        major_copy(at, 2, near).wait_recv()
        product[at] = value + (major_in[at, 1] + major_in[at, 2])

    prepare(0)
    lax.fori_loop(0, 4, first_step, 0)

    def rest_of(at, carry):
        prepare(at)
        later_steps(at)
        collect(at - 1)
        return carry

    lax.fori_loop(1, CHUNKS, rest_of, 0)
    collect(CHUNKS - 1)

    one_row = mask_of(0, slots_of)
    two_row = mask_of(1, slots_of)
    inv_one_t = -(jnp.concatenate([product[at] for at in range(per_panel)], axis=0) * one_row)
    part_two_t = -(jnp.concatenate([product[at] for at in range(per_panel, CHUNKS)], axis=0) * two_row)
    moved.wait_recv()
    last = ((1,), (1,))
    panel_one_t = resident[0].T
    panel_two_t = resident[1].T
    gram_one = exact(panel_one_t, inv_one_t, last)
    cross_sum = exact(inv_one_t * two_row, panel_two_t, last)
    gram_two = exact(panel_two_t, part_two_t, last)
    half = width // 2

    def quarters(value, places):
        return [value[i * half : (i + 1) * half, j * half : (j + 1) * half] for i, j in places]

    upper_places = ((0, 0), (0, 1), (1, 1))
    every_place = ((0, 0), (0, 1), (1, 0), (1, 1))
    tiles = quarters(gram_one, upper_places) + quarters(cross_sum, every_place) + quarters(gram_two, upper_places)
    for at, tile in enumerate(tiles):
        packed[pl.ds(at * half, half), :] = tile

    share = fold.shape[0]
    slice_rows = share // CHIPS
    base = core * share

    def sum_copy(stage, source, target):
        return remote(source, target, sum_sem, (stage,), partner)

    fold_copy = sum_copy(0, packed.at[pl.ds((1 - core) * share, share)], fold_in)
    fold_copy.start()

    tile_count = owner.shape[0]
    tile_rows = span // tile_count
    inv_two_t = part_two_t - exact(above[...].T, inv_one_t, ((1,), (0,))) * two_row
    inverse_one[...] = inv_one_t.T
    inv_two = inv_two_t.T

    def chip_at(offset):
        flat = lax.rem(chip + offset, CHIPS)
        return flat, device(flat // 4, lax.rem(flat // 2, 2), lax.rem(flat, 2), core)

    fold_copy.wait_recv()
    fold[...] = packed[pl.ds(base, share), :] + fold_in[...]
    order = sorted(range(1, CHIPS), key=lambda offset: -min(offset, CHIPS - offset))
    chip_copies = []
    for offset in order:
        flat, peer = chip_at(offset)
        copy = remote(
            fold.at[pl.ds(flat * slice_rows, slice_rows)], part_in.at[offset - 1], chip_sem, (offset - 1,), peer
        )
        copy.start()
        chip_copies.append(copy)

    names = [owner[at] for at in range(tile_count)]
    ranks = [sum([jnp.where(names[before] == names[at], 1, 0) for before in range(at)], jnp.int32(0)) for at in range(tile_count)]

    def slot_value(name, rank):
        value = jnp.zeros((tile_rows, width), jnp.float32)
        for at in range(tile_count):
            chosen = (names[at] == name) & (ranks[at] == rank)
            value = jnp.where(chosen, inv_two[at * tile_rows : (at + 1) * tile_rows], value)
        return value

    tile_copies = []
    for offset in range(1, COLS):
        name = lax.rem(col + offset, COLS)
        for rank in range(CAP):
            outgoing[offset - 1, rank] = slot_value(name, rank)
        copy = remote(
            outgoing.at[offset - 1], delivered.at[pl.ds(col * CAP, CAP)], tile_sem, (offset - 1,), (row, name)
        )
        copy.start()
        tile_copies.append(copy)
    for rank in range(CAP):
        delivered[col * CAP + rank] = slot_value(col, rank)

    for copy in chip_copies:
        copy.wait_recv()
    value = fold[pl.ds(chip * slice_rows, slice_rows), :]
    for slot in range(CHIPS - 1):
        value = value + part_in[slot]
    mine_rows = pl.ds(base + chip * slice_rows, slice_rows)
    full[mine_rows, :] = value
    spread_copies = []
    for offset in order:
        _, peer = chip_at(offset)
        copy = remote(full.at[mine_rows], full.at[mine_rows], spread_sem, (offset - 1,), peer)
        copy.start()
        spread_copies.append(copy)
    for copy in spread_copies:
        copy.wait_recv()
    half_rows = pl.ds(base, share)
    last_copy = sum_copy(1, full.at[half_rows], full.at[half_rows])
    last_copy.start()
    last_copy.wait_recv()

    def tile_at(at):
        return full[pl.ds(at * half, half), :]

    def square(first, second, third, fourth):
        return jnp.concatenate(
            [jnp.concatenate([first, second], axis=1), jnp.concatenate([third, fourth], axis=1)], axis=0
        )

    pa = above[...]
    pa_t = pa.T
    plain = ((1,), (0,))
    diag_one_value = diag_one[...] - square(tile_at(0), tile_at(1), tile_at(1).T, tile_at(2))
    cross_total = square(tile_at(3), tile_at(4), tile_at(5), tile_at(6))
    diag_one[...] = diag_one_value
    cross_value = -(cross_total + exact(diag_one_value, pa, plain))
    cross_two[...] = cross_value
    gram_total = square(tile_at(7), tile_at(8), tile_at(8).T, tile_at(9)) - exact(cross_total.T, pa, plain)
    diag_two[...] = (diag_two[...] - gram_total) - exact(pa_t, cross_value, plain)

    for copy in tile_copies:
        copy.wait_recv()
    pl.when(jnp.logical_not(stays))(lambda: moved.wait_send())
    for copy in chip_copies + spread_copies + tile_copies + [fold_copy, last_copy]:
        copy.wait_send()
    for at in range(CHUNKS):
        for copy in (near_copy(at), far_copy(at), relay_copy(at)):
            copy.wait_send()
        for step in range(4):
            pair_copy(at, step).wait_send()
        for slot, peer in enumerate((near, away, near)):
            major_copy(at, slot, peer).wait_send()


def fused(matrix, panel_one, panel_two, struct_one, struct_two, lower_one, above, lower_two, tile_owner):
    depth, _ = matrix.shape
    span, width = panel_one.shape
    chunk = 2 * width // CHUNKS
    tile_count = tile_owner.shape[0]
    share = 5 * (width // 2)
    mask_rows = -(-(COLS + 1) * (span // LANES) // 8) * 8
    dma = pltpu.SemaphoreType.DMA
    vmem = lambda *shape: pltpu.VMEM(shape, jnp.float32)
    half_vmem = lambda *shape: pltpu.VMEM(shape, jnp.bfloat16)
    anywhere = pl.BlockSpec(memory_space=pl.ANY)
    whole = pl.BlockSpec(memory_space=pltpu.VMEM)
    scalars = pl.BlockSpec(memory_space=pltpu.SMEM)
    shape = lambda *dims: jax.ShapeDtypeStruct(dims, jnp.float32)
    return tuple(pl.pallas_call(
        fused_kernel,
        out_shape=[
            shape(span, width),
            shape(width, width),
            shape(width, width),
            shape(width, width),
            shape(COLS * CAP, span // tile_count, width),
        ],
        in_specs=[anywhere] * 3 + [whole] * 5 + [scalars],
        out_specs=[whole] * 5,
        scratch_shapes=[
            vmem(2, depth, span),
            half_vmem(8, depth, span),
            half_vmem(8, depth, span),
            vmem(2, span, width),
            vmem(COLS, CHUNKS, span, chunk),
            half_vmem(CHUNKS, 2 * chunk, depth),
            vmem(CHUNKS, 4, chunk, span),
            vmem(CHUNKS, 4, chunk, span),
            vmem(CHUNKS, 4, chunk, span),
            vmem(CHUNKS, 3, chunk, span),
            vmem(2, mask_rows, LANES),
            vmem(2, span, width),
            vmem(CHUNKS, chunk, span),
            vmem(2 * share, LANES),
            vmem(share, LANES),
            vmem(share, LANES),
            vmem(CHIPS - 1, share // CHIPS, LANES),
            vmem(2 * share, LANES),
            vmem(COLS - 1, CAP, span // tile_count, width),
            dma((2,)),
            dma((2,)),
            dma((2,)),
            dma((2, CHUNKS)),
            dma((2, CHUNKS)),
            dma((2, CHUNKS)),
            dma((2, CHUNKS, 4)),
            dma((2, CHUNKS, 3)),
            dma((2, 2)),
            dma((2, CHIPS - 1)),
            dma((2, CHIPS - 1)),
            dma((2, COLS - 1)),
        ],
        compiler_params=pltpu.CompilerParams(
            collective_id=3, has_side_effects=True, vmem_limit_bytes=62 * 2**20
        ),
        cost_estimate=pl.CostEstimate(
            flops=12 * matrix.size * width, bytes_accessed=4 * matrix.size, transcendentals=0
        ),
    )(
        matrix,
        panel_one,
        panel_two,
        struct_one.reshape(-1, LANES),
        struct_two.reshape(-1, LANES),
        lower_one,
        above,
        lower_two,
        tile_owner.reshape(-1),
    ))


def local(
    ancestor_inverse,
    panel_one,
    struct_one,
    lower_one,
    panel_two,
    struct_two,
    panel_above,
    lower_two,
    tile_owner,
):
    row_count = lax.axis_size("row")
    col_count = lax.axis_size("col")
    row_index = lax.axis_index("row")
    col_index = lax.axis_index("col")
    local_rows = panel_one.shape[0]
    if fits_fused(ancestor_inverse, panel_one, struct_one, struct_two, tile_owner, row_count, col_count):
        return fused(
            ancestor_inverse,
            panel_one,
            panel_two,
            struct_one,
            struct_two,
            lower_one,
            panel_above,
            lower_two,
            tile_owner,
        )
    order = local_rows * row_count * col_count
    width = panel_one.shape[1]
    mask_one = row_mask(struct_one, order)
    mask_two = row_mask(struct_two, order)
    panel_start = (row_index * col_count + col_index) * local_rows
    result_start = (col_index * row_count + row_index) * local_rows
    local_one = panel_one * lax.dynamic_slice_in_dim(mask_one, panel_start, local_rows)[:, None]
    local_two = panel_two * lax.dynamic_slice_in_dim(mask_two, panel_start, local_rows)[:, None]
    result_mask_one = lax.dynamic_slice_in_dim(mask_one, result_start, local_rows)[:, None]
    result_mask_two = lax.dynamic_slice_in_dim(mask_two, result_start, local_rows)[:, None]

    both = jnp.concatenate([local_one, local_two], axis=1)
    gathered = lax.all_gather(both, "col", axis=0, tiled=True)
    product = scatter_rows(contract_rows(ancestor_inverse, gathered, lax.Precision.HIGH), row_count)
    moves = [(f, (f % row_count) * col_count + f // row_count) for f in range(row_count * col_count)]
    resident = lax.ppermute(both, ("row", "col"), moves)
    resident_one = resident[:, :width]
    resident_two = resident[:, width:]
    inverse_one = -product[:, :width] * result_mask_one
    inverse_two = -(product[:, width:] + matmul(inverse_one, panel_above)) * result_mask_two
    grams = (
        contract_rows(resident_one, inverse_one),
        contract_rows(inverse_one, resident_two),
        contract_rows(resident_two, inverse_two),
    )
    lanes = 128
    packed = jnp.concatenate(
        [gram[:, at : at + lanes] for gram in grams for at in range(0, width, lanes)], axis=0
    )
    sums = sum_everywhere(packed, row_count, col_count).reshape(len(grams), width // lanes, width, lanes)
    gram_one, cross_sum, gram_two = (
        jnp.concatenate([sums[at, block] for block in range(width // lanes)], axis=1) for at in range(len(grams))
    )
    diag_one = matmul(lower_one.T, lower_one) - gram_one
    cross_two = -(cross_sum + matmul(diag_one, panel_above))
    diag_two = matmul(lower_two.T, lower_two) - gram_two - matmul(panel_above.T, cross_two)
    delivered = deliver(inverse_two, tile_owner, col_count)
    return (inverse_one, diag_one, cross_two, diag_two, delivered)


def solution(mesh):
    return jax.shard_map(
        local,
        mesh=mesh,
        in_specs=(
            P("row", "col"),
            P(("row", "col"), None),
            P(),
            P(),
            P(("row", "col"), None),
            P(),
            P(),
            P(),
            P(("col", "row"), None),
        ),
        out_specs=(P(("col", "row"), None), P(), P(), P(), P(("row", "col"), None, None)),
        check_vma=False,
    )
```

```python
import functools

import jax
import jax.numpy as jnp
from jax import lax
from jax.experimental import pallas as pl
from jax.experimental.pallas import tpu as pltpu
from jax.sharding import PartitionSpec as P

CAP = 2


def matmul(left, right):
    return jnp.dot(left, right, precision=lax.Precision.HIGHEST, preferred_element_type=jnp.float32)


def contract_rows(left, right, precision=lax.Precision.HIGHEST):
    return lax.dot_general(
        left,
        right,
        (((0,), (0,)), ((), ())),
        precision=precision,
        preferred_element_type=jnp.float32,
    )


def row_mask(struct, count):
    lanes = 128
    high = struct // lanes
    low = struct % lanes
    high_hot = (jnp.arange(count // lanes, dtype=jnp.int32)[:, None] == high[None, :]).astype(jnp.bfloat16)
    low_hot = (jnp.arange(lanes, dtype=jnp.int32)[:, None] == low[None, :]).astype(jnp.bfloat16)
    counts = lax.dot_general(high_hot, low_hot, (((1,), (1,)), ((), ())), preferred_element_type=jnp.float32)
    return (counts > 0.5).astype(jnp.float32).reshape(count)


MESH = pl.DeviceIdType.MESH


def greet(peers):
    barrier = pltpu.get_barrier_semaphore()
    for peer in peers:
        pl.semaphore_signal(barrier, inc=1, device_id=peer, device_id_type=MESH)
    pl.semaphore_wait(barrier, len(peers))


def scatter_kernel(rows, value_ref, out_ref, pair_in, total, major_in, pair_send, pair_recv, major_send, major_recv):
    majors = rows // 2
    row = lax.axis_index("row")
    col = lax.axis_index("col")
    major, minor = row // 2, row % 2
    partner = (major * 2 + 1 - minor, col)

    def peer(offset):
        return (lax.rem(major + offset, majors) * 2 + minor, col)

    greet([partner] + [peer(offset) for offset in range(1, majors)])
    order = sorted(range(1, majors), key=lambda offset: -min(offset, majors - offset)) + [0]
    started = []
    pair_copies = {}
    for offset in order:
        target = lax.rem(major + offset, majors)
        copy = pltpu.make_async_remote_copy(
            src_ref=value_ref.at[target * 2 + 1 - minor],
            dst_ref=pair_in.at[offset],
            send_sem=pair_send.at[offset],
            recv_sem=pair_recv.at[offset],
            device_id=partner,
            device_id_type=MESH,
        )
        copy.start()
        pair_copies[offset] = copy
    for offset in order:
        target = lax.rem(major + offset, majors)
        pair_copies[offset].wait_recv()
        total[offset] = pair_in[offset] + value_ref[target * 2 + minor]
        if offset:
            copy = pltpu.make_async_remote_copy(
                src_ref=total.at[offset],
                dst_ref=major_in.at[offset - 1],
                send_sem=major_send.at[offset - 1],
                recv_sem=major_recv.at[offset - 1],
                device_id=peer(offset),
                device_id_type=MESH,
            )
            copy.start()
            started.append(copy)
    for copy in started:
        copy.wait_recv()
    result = total[0]
    for slot in range(majors - 1):
        result = result + major_in[slot]
    out_ref[...] = result
    for copy in started:
        copy.wait_send()
    for offset in order:
        pair_copies[offset].wait_send()


def scatter_rows(value, rows):
    chunk, width = value.shape[0] // rows, value.shape[1]
    majors = rows // 2
    dma = pltpu.SemaphoreType.DMA
    return pl.pallas_call(
        functools.partial(scatter_kernel, rows),
        out_shape=jax.ShapeDtypeStruct((chunk, width), jnp.float32),
        in_specs=[pl.BlockSpec(memory_space=pltpu.VMEM)],
        out_specs=pl.BlockSpec(memory_space=pltpu.VMEM),
        scratch_shapes=[
            pltpu.VMEM((majors, chunk, width), jnp.float32),
            pltpu.VMEM((majors, chunk, width), jnp.float32),
            pltpu.VMEM((majors - 1, chunk, width), jnp.float32),
            dma((majors,)),
            dma((majors,)),
            dma((majors - 1,)),
            dma((majors - 1,)),
        ],
        compiler_params=pltpu.CompilerParams(
            collective_id=0, has_side_effects=True, vmem_limit_bytes=40 * 2**20
        ),
    )(value.reshape(rows, chunk, width))


def sum_kernel(rows, cols, value_ref, out_ref, full, sum_a, sum_b, in_a, in_b, in_c, *sems):
    row = lax.axis_index("row")
    col = lax.axis_index("col")
    outer = cols // 2
    far, core = col // 2, col % 2
    half = outer * rows
    base_a = core * half
    base_b = base_a + far * rows
    base_c = base_b + row

    def pair_peer(offset):
        return (row, far * 2 + 1 - core)

    def far_peer(offset):
        return (row, lax.rem(far + offset, outer) * 2 + core)

    def row_peer(offset):
        return (lax.rem(row + offset, rows), col)

    greet(
        [pair_peer(1)]
        + [far_peer(offset) for offset in range(1, outer)]
        + [row_peer(offset) for offset in range(1, rows)]
    )

    def exchange(count, peer, source, landing, stage):
        copies = []
        for offset in range(1, count):
            copy = pltpu.make_async_remote_copy(
                src_ref=source(offset),
                dst_ref=landing(offset),
                send_sem=sems[2 * stage].at[offset - 1],
                recv_sem=sems[2 * stage + 1].at[offset - 1],
                device_id=peer(offset),
                device_id_type=MESH,
            )
            copy.start()
            copies.append(copy)
        for copy in copies:
            copy.wait_recv()
        return copies

    pending = []
    pending += exchange(
        2, pair_peer, lambda k: value_ref.at[pl.ds((1 - core) * half, half)], lambda k: in_a.at[k - 1], 0
    )
    sum_a[...] = value_ref[pl.ds(base_a, half)] + in_a[0]
    pending += exchange(
        outer, far_peer, lambda k: sum_a.at[pl.ds(lax.rem(far + k, outer) * rows, rows)], lambda k: in_b.at[k - 1], 1
    )
    total = sum_a[pl.ds(far * rows, rows)]
    for slot in range(outer - 1):
        total = total + in_b[slot]
    sum_b[...] = total
    pending += exchange(
        rows, row_peer, lambda k: sum_b.at[lax.rem(row + k, rows)], lambda k: in_c.at[k - 1], 2
    )
    total = sum_b[row]
    for slot in range(rows - 1):
        total = total + in_c[slot]
    full[base_c] = total
    pending += exchange(rows, row_peer, lambda k: full.at[base_c], lambda k: full.at[base_c], 3)
    pending += exchange(
        outer, far_peer, lambda k: full.at[pl.ds(base_b, rows)], lambda k: full.at[pl.ds(base_b, rows)], 4
    )
    pending += exchange(
        2, pair_peer, lambda k: full.at[pl.ds(base_a, half)], lambda k: full.at[pl.ds(base_a, half)], 5
    )
    out_ref[...] = full[...]
    for copy in pending:
        copy.wait_send()


def sum_everywhere(value, rows, cols):
    devices = rows * cols
    lanes = value.shape[1]
    depth = value.shape[0] // devices
    outer = cols // 2
    dma = pltpu.SemaphoreType.DMA
    vmem = lambda *lead: pltpu.VMEM(lead + (depth, lanes), jnp.float32)
    total = pl.pallas_call(
        functools.partial(sum_kernel, rows, cols),
        out_shape=jax.ShapeDtypeStruct((devices, depth, lanes), jnp.float32),
        in_specs=[pl.BlockSpec(memory_space=pltpu.VMEM)],
        out_specs=pl.BlockSpec(memory_space=pltpu.VMEM),
        scratch_shapes=[
            vmem(devices),
            vmem(devices // 2),
            vmem(rows),
            vmem(1, devices // 2),
            vmem(outer - 1, rows),
            vmem(rows - 1),
        ]
        + [dma((count - 1,)) for count in (2, outer, rows, rows, outer, 2) for _ in range(2)],
        compiler_params=pltpu.CompilerParams(
            collective_id=1, has_side_effects=True, vmem_limit_bytes=24 * 2**20
        ),
        cost_estimate=pl.CostEstimate(flops=0, bytes_accessed=100 * value.size * 4, transcendentals=0),
    )(value.reshape(devices, depth, lanes))
    return total.reshape(value.shape)


def deliver(values, tile_owner, col_count):
    tile_count = tile_owner.shape[0]
    tile_rows = values.shape[0] // tile_count
    all_tiles = values.reshape(tile_count, tile_rows, values.shape[1])
    owner_col = tile_owner[:, 0]
    col_ids = jnp.arange(col_count, dtype=jnp.int32)
    onehot = (owner_col[:, None] == col_ids[None, :]).astype(jnp.int32)
    tile_rank = jnp.sum((jnp.cumsum(onehot, axis=0) - onehot) * onehot, axis=1)
    slot_index = jnp.arange(CAP, dtype=jnp.int32)
    select = (
        (owner_col[None, None, :] == col_ids[:, None, None])
        & (tile_rank[None, None, :] == slot_index[None, :, None])
    ).astype(jnp.float32)
    outgoing = jnp.einsum("cks,srb->ckrb", select, all_tiles, precision=lax.Precision.HIGHEST)
    incoming = lax.all_to_all(outgoing, "col", split_axis=0, concat_axis=0, tiled=True)
    return incoming.reshape(col_count * CAP, tile_rows, values.shape[1])


ROWS, COLS, CHIPS = 8, 4, 16
CHUNKS = 4
LANES = 128


def fits_fused(matrix, panel, struct_one, struct_two, tile_owner, rows, cols):
    span, width = panel.shape
    return (
        (rows, cols) == (ROWS, COLS)
        and span % LANES == 0
        and width == 2 * LANES
        and matrix.shape == (cols * span, rows * span)
        and struct_one.shape[0] % LANES == 0
        and struct_two.shape[0] % LANES == 0
        and span % (8 * tile_owner.shape[0]) == 0
    )


def exact(left, right, contract):
    return lax.dot_general(
        left, right, (contract, ((), ())), precision=lax.Precision.HIGHEST, preferred_element_type=jnp.float32
    )


def fused_kernel(
    matrix, panel_one, panel_two, struct_one_in, struct_two_in, lower_one_in, above_in, lower_two_in, owner,
    inverse_one_out, diag_one_out, cross_two_out, diag_two_out, delivered,
    inverse_one, diag_one, cross_two, diag_two, tiles_here,
    struct_one, struct_two, lower_one, above, lower_two, window, high, low, own, land, left, other, mine, pair_in, major_in, masks, turned, resident, product,
    inv_one_t, part_two_t, panel_two_t, correction, packed, fold_in, fold, part_in, full, outgoing,
    out_sem, small_sem, fetch_sem, own_sem, turn_sem, move_sem, near_gather, far_gather, relay_gather, pair_sem, major_sem, sum_sem, chip_sem,
    spread_sem, tile_sem,
):
    row = lax.axis_index("row")
    col = lax.axis_index("col")
    z, y = row // 2, row % 2
    x, core = col // 2, col % 2
    upper, lower = z // 2, z % 2
    chip = (z * 2 + y) * 2 + x
    depth, total_columns = matrix.shape
    span, width = own.shape[1:]
    chunk = left.shape[1] // 2
    per_panel = width // chunk

    def device(z_at, y_at, x_at, core_at):
        return (z_at * 2 + y_at, x_at * 2 + core_at)

    partner = device(z, y, x, 1 - core)
    across = device(z, y, 1 - x, core)
    beside = device(z, 1 - y, x, core)
    near = device(upper * 2 + 1 - lower, y, x, core)
    away = device((1 - upper) * 2 + lower, y, x, core)

    def remote(source, target, sems, at, peer):
        return pltpu.make_async_remote_copy(
            src_ref=source,
            dst_ref=target,
            send_sem=sems.at[(0,) + at],
            recv_sem=sems.at[(1,) + at],
            device_id=peer,
            device_id_type=MESH,
        )

    own_copies = [
        pltpu.make_async_copy(panel, own.at[at], own_sem.at[at]) for at, panel in enumerate((panel_one, panel_two))
    ]
    for copy in own_copies:
        copy.start()

    def fetch(step, which):
        target_upper = lax.rem(upper + 1 + step // 2, 2)
        target_lower = lax.rem(lower + 1 + step, 2)
        target = (target_upper * 2 + target_lower) * 2 + lax.rem(1 - y + which, 2)
        return pltpu.make_async_copy(
            matrix.at[:, pl.ds(pl.multiple_of(target * span, LANES), span)], window.at[which], fetch_sem.at[which]
        )

    small_pairs = (
        (struct_one_in, struct_one),
        (struct_two_in, struct_two),
        (lower_one_in, lower_one),
        (above_in, above),
        (lower_two_in, lower_two),
    )
    small_copies = [
        pltpu.make_async_copy(source, target, small_sem.at[at]) for at, (source, target) in enumerate(small_pairs)
    ]
    for copy in small_copies:
        copy.start()
    barrier = pltpu.get_barrier_semaphore()
    devices = ROWS * COLS
    for offset in range(1, devices):
        flat = lax.rem(row * COLS + col + offset, devices)
        pl.semaphore_signal(barrier, inc=1, device_id=(flat // COLS, lax.rem(flat, COLS)), device_id_type=MESH)
    for which in range(2):
        fetch(0, which).start()
    pl.semaphore_wait(barrier, devices - 1)
    for copy in own_copies:
        copy.wait()

    def piece(at):
        return own.at[at // per_panel, :, pl.ds(at % per_panel * chunk, chunk)]

    def far_copy(at, source=None):
        return remote(land.at[0, at] if source is None else source, land.at[col, at], far_gather, (at,), across)

    def near_copy(at, source=None):
        return remote(land.at[0, at] if source is None else source, land.at[col, at], near_gather, (at,), partner)

    def relay_copy(at):
        slot = (1 - x) * 2 + core
        return remote(land.at[slot, at], land.at[slot, at], relay_gather, (at,), partner)

    turns = core != y
    direct = jnp.where(x == upper, 0, 1)
    relays_move = lower == x

    def move_copy(source, slot, panel, at, peer):
        return pltpu.make_async_remote_copy(
            src_ref=source.at[panel],
            dst_ref=resident.at[slot, panel],
            send_sem=move_sem.at[0, panel, at],
            recv_sem=move_sem.at[1, panel, slot],
            device_id=peer,
            device_id_type=MESH,
        )

    def climb(source, panel, at, from_y):
        peer = device(2 * from_y + x, y, x, lower)
        return move_copy(source, direct, panel, at, peer), (peer[0] == row) & (peer[1] == col)

    def start_climb(source, panel, at, from_y):
        copy, stays = climb(source, panel, at, from_y)
        kept = pltpu.make_async_copy(source.at[panel], resident.at[direct, panel], move_sem.at[1, panel, direct])
        pl.when(stays)(lambda: kept.start())
        pl.when(jnp.logical_not(stays))(lambda: copy.start())

    def end_climb(source, panel, at, from_y):
        copy, stays = climb(source, panel, at, from_y)
        pl.when(jnp.logical_not(stays))(lambda: copy.wait_send())

    turn = [remote(own.at[panel], turned.at[panel], turn_sem, (panel,), beside) for panel in range(2)]
    passed = [move_copy(resident.at[1], 0, panel, 2, across) for panel in range(2)]

    def climb_turned(panel):
        @pl.when(jnp.logical_not(turns))
        def _():
            turn[panel].wait_recv()
            start_climb(turned, panel, 1, 1 - y)

    def pass_on(panel):
        @pl.when(relays_move)
        def _():
            move_copy(own, 1, panel, 0, beside).wait_recv()
            passed[panel].start()

    for at in range(CHUNKS):
        far_copy(at, piece(at)).start()
        near_copy(at, piece(at)).start()
        if at == 0:
            @pl.when(turns)
            def _():
                for copy in turn:
                    copy.start()

            @pl.when(jnp.logical_not(turns))
            def _():
                for panel in range(2):
                    start_climb(own, panel, 0, y)

    for at in range(CHUNKS):
        land[col, at] = piece(at)[...]

    for copy in small_copies:
        copy.wait()
    blocks = span // LANES
    slots_of = COLS * blocks
    mask_rows = masks.shape[1]
    place_rows = lax.broadcasted_iota(jnp.int32, (mask_rows, LANES), 0)
    block_base = row * slots_of
    result_base = (col * ROWS + row) * blocks
    wanted = jnp.where(place_rows < slots_of, block_base + place_rows, result_base + place_rows - slots_of)
    lane_ids = lax.broadcasted_iota(jnp.int32, (LANES, LANES), 0)
    for at, struct in enumerate((struct_one, struct_two)):
        count = struct.shape[0]
        group = max(size for size in range(1, 17) if count % size == 0)
        counts = jnp.zeros((mask_rows, LANES), jnp.float32)
        for begin in range(0, count, group):
            highs, lows = [], []
            for entry in range(begin, begin + group):
                value = struct[pl.ds(entry, 1), :]
                highs.append(jnp.where(wanted == value // LANES, 1.0, 0.0))
                lows.append(jnp.where(lane_ids == value % LANES, 1.0, 0.0))
            counts = counts + lax.dot_general(
                jnp.concatenate(highs, axis=1).astype(jnp.bfloat16),
                jnp.concatenate(lows, axis=1).astype(jnp.bfloat16),
                (((1,), (1,)), ((), ())),
                preferred_element_type=jnp.float32,
            )
        masks[at] = jnp.where(counts > 0.5, 1.0, 0.0)
    diag_one[...] = exact(lower_one[...].T, lower_one[...], ((1,), (0,)))
    diag_two[...] = exact(lower_two[...].T, lower_two[...], ((1,), (0,)))

    def mask_of(panel, begin):
        return jnp.concatenate([masks[panel, pl.ds(begin + at, 1), :] for at in range(blocks)], axis=1)

    def prepare(at):
        near_copy(at).wait_recv()
        far_copy(at).wait_recv()
        relay_copy(at).start()
        relay_copy(at).wait_recv()
        for slot in range(COLS):
            value = land[slot, at].T * mask_of(at // per_panel, slot * blocks)
            upper_part = value.astype(jnp.bfloat16)
            columns = pl.ds(slot * span, span)
            left[at, pl.ds(0, chunk), columns] = upper_part
            left[at, pl.ds(chunk, chunk), columns] = (value - upper_part.astype(jnp.float32)).astype(jnp.bfloat16)

    def pair_copy(at, step):
        return remote(other.at[at, step], pair_in.at[at, step], pair_sem, (at, step), beside)

    def multiply(at, step, which):
        target = step * 2 + which
        both = jnp.dot(left[at], high[target], preferred_element_type=jnp.float32)
        rest = jnp.dot(left[at, pl.ds(0, chunk), :], low[target], preferred_element_type=jnp.float32)
        value = both[:chunk] + (both[chunk:] + rest)
        if which == 0:
            other[at, step] = value
            pair_copy(at, step).start()
        else:
            mine[at, step] = value

    def first_step(step, carry):
        for which in range(2):
            fetch(step, which).wait()
            target = step * 2 + which
            for begin in range(0, depth, 256):
                size = min(256, depth - begin)
                value = window[which, pl.ds(begin, size), :]
                upper_part = value.astype(jnp.bfloat16)
                high[target, pl.ds(begin, size), :] = upper_part
                low[target, pl.ds(begin, size), :] = (value - upper_part.astype(jnp.float32)).astype(jnp.bfloat16)

            @pl.when(step + 1 < 4)
            def _():
                fetch(step + 1, which).start()

            multiply(0, step, which)
        pl.when(step == 1)(lambda: climb_turned(1))
        return carry

    def later_steps(at):
        def body(step, carry):
            for which in range(2):
                multiply(at, step, which)
            return carry

        lax.fori_loop(0, 4, body, 0)

    def major_copy(at, slot, peer):
        return remote(mine.at[at, slot], major_in.at[at, slot], major_sem, (at, slot), peer)

    def open_near(at):
        pair_copy(at, 0).wait_recv()
        mine[at, 0] = mine[at, 0] + pair_in[at, 0]
        major_copy(at, 0, near).start()

    def open_away(at):
        pair_copy(at, 1).wait_recv()
        mine[at, 1] = mine[at, 1] + pair_in[at, 1]
        major_copy(at, 0, near).wait_recv()
        mine[at, 1] = mine[at, 1] + major_in[at, 0]
        major_copy(at, 1, away).start()

    def close_near(at):
        pair_copy(at, 2).wait_recv()
        mine[at, 2] = mine[at, 2] + pair_in[at, 2]
        major_copy(at, 2, near).start()

    def collect(at):
        pair_copy(at, 3).wait_recv()
        value = mine[at, 3] + pair_in[at, 3]
        major_copy(at, 1, away).wait_recv()
        major_copy(at, 2, near).wait_recv()
        product[at] = value + (major_in[at, 1] + major_in[at, 2])

    half = width // 2
    share_of = (4 * half, 2 * half)
    starts = (0, 4 * half)
    order = sorted(range(1, CHIPS), key=lambda offset: -min(offset, CHIPS - offset))
    plain, last = ((1,), (0,)), ((1,), (1,))

    def chip_at(offset):
        flat = lax.rem(chip + offset, CHIPS)
        return flat, device(flat // 4, lax.rem(flat // 2, 2), lax.rem(flat, 2), core)

    class Total:
        def __init__(self, at):
            self.at, self.share, self.start = at, share_of[at], starts[at]
            self.rows = self.share // CHIPS
            self.base = 2 * self.start + core * self.share
            self.half_rows = pl.ds(self.base, self.share)
            self.sent = []

        def partner_copy(self, stage, source, target):
            copy = remote(source, target, sum_sem, (self.at, stage), partner)
            self.sent.append(copy)
            copy.start()
            return copy

        def begin(self, tiles):
            for at in range(2 * self.share // half):
                tile = tiles[at] if at < len(tiles) else jnp.zeros((half, half), jnp.float32)
                packed[pl.ds(2 * self.start + at * half, half), :] = tile
            theirs = pl.ds(2 * self.start + (1 - core) * self.share, self.share)
            self.first = self.partner_copy(0, packed.at[theirs], fold_in.at[pl.ds(self.start, self.share)])

        def scatter(self):
            self.first.wait_recv()
            rows = pl.ds(self.start, self.share)
            fold[rows, :] = packed[self.half_rows, :] + fold_in[rows, :]
            self.copies = []
            for offset in order:
                flat, peer = chip_at(offset)
                copy = remote(
                    fold.at[pl.ds(self.start + flat * self.rows, self.rows)],
                    part_in.at[offset - 1, pl.ds(self.start // CHIPS, self.rows)],
                    chip_sem,
                    (self.at, offset - 1),
                    peer,
                )
                copy.start()
                self.copies.append(copy)

        def gather(self):
            for copy in self.copies:
                copy.wait_recv()
            value = fold[pl.ds(self.start + chip * self.rows, self.rows), :]
            for slot in range(CHIPS - 1):
                value = value + part_in[slot, pl.ds(self.start // CHIPS, self.rows), :]
            mine_rows = pl.ds(self.base + chip * self.rows, self.rows)
            full[mine_rows, :] = value
            self.sent += self.copies
            self.copies = []
            for offset in order:
                copy = remote(
                    full.at[mine_rows], full.at[mine_rows], spread_sem, (self.at, offset - 1), chip_at(offset)[1]
                )
                copy.start()
                self.copies.append(copy)

        def finish(self):
            for copy in self.copies:
                copy.wait_recv()
            self.final = self.partner_copy(1, full.at[self.half_rows], full.at[self.half_rows])
            self.sent += self.copies

        def tile(self, at):
            return full[pl.ds(2 * self.start + at * half, half), :]

    def quarters(value, places):
        return [value[i * half : (i + 1) * half, j * half : (j + 1) * half] for i, j in places]

    upper_places = ((0, 0), (0, 1), (1, 1))
    every_place = ((0, 0), (0, 1), (1, 0), (1, 1))
    tile_count = owner.shape[0]
    tile_rows = span // tile_count
    names = [owner[at] for at in range(tile_count)]
    ranks = [
        sum([jnp.where(names[before] == names[at], 1, 0) for before in range(at)], jnp.int32(0))
        for at in range(tile_count)
    ]
    tile_copies = []

    def send_tiles(part, values):
        columns = pl.ds(part * half, half)

        def slot_value(name, rank):
            value = jnp.zeros((tile_rows, half), jnp.float32)
            for at in range(tile_count):
                chosen = (names[at] == name) & (ranks[at] == rank)
                value = jnp.where(chosen, values[at * tile_rows : (at + 1) * tile_rows], value)
            return value

        for offset in range(1, COLS):
            name = lax.rem(col + offset, COLS)
            for rank in range(CAP):
                outgoing[offset - 1, rank, :, columns] = slot_value(name, rank)
            copy = remote(
                outgoing.at[offset - 1, :, :, columns],
                delivered.at[pl.ds(col * CAP, CAP), :, columns],
                tile_sem,
                (part, offset - 1),
                (row, name),
            )
            copy.start()
            tile_copies.append(copy)
        for rank in range(CAP):
            tiles_here[rank, :, columns] = slot_value(col, rank)

    first_total, second_total = Total(0), Total(1)

    prepare(0)
    climb_turned(0)
    lax.fori_loop(0, 4, first_step, 0)
    prepare(1)
    open_near(0)
    later_steps(1)
    close_near(0)
    pass_on(0)
    prepare(2)
    later_steps(2)
    open_near(1)
    open_away(0)
    pass_on(1)
    close_near(1)
    open_away(1)
    collect(0)
    prepare(3)
    open_near(2)
    later_steps(3)
    collect(1)
    one_row = mask_of(0, slots_of)
    two_row = mask_of(1, slots_of)
    inv_one_t[...] = -(jnp.concatenate([product[at] for at in range(per_panel)], axis=0) * one_row)
    for copy in passed:
        copy.wait_recv()
    panel_two_t[...] = resident[0, 1].T
    gram_one = exact(resident[0, 0].T, inv_one_t[...], last)
    cross_sum = exact(inv_one_t[...] * two_row, panel_two_t[...], last)
    first_total.begin(quarters(gram_one, upper_places) + quarters(cross_sum, every_place))
    above_t = above[...].T
    correction[...] = exact(above_t, inv_one_t[...], plain) * two_row
    inverse_one[...] = inv_one_t[...].T
    outs = [pltpu.make_async_copy(inverse_one, inverse_one_out, out_sem.at[0])]
    outs[0].start()
    first_total.scatter()
    open_away(2)
    close_near(2)
    open_near(3)
    collect(2)
    part_two_t[pl.ds(0, half), :] = -(product[2] * two_row)
    send_tiles(0, (part_two_t[pl.ds(0, half), :] - correction[pl.ds(0, half), :]).T)
    open_away(3)
    close_near(3)
    first_total.gather()
    collect(3)
    part_two_t[pl.ds(half, half), :] = -(product[3] * two_row)
    gram_two = exact(panel_two_t[...], part_two_t[...], last)
    second_total.begin(quarters(gram_two, upper_places))
    first_total.finish()
    second_total.scatter()
    send_tiles(1, (part_two_t[pl.ds(half, half), :] - correction[pl.ds(half, half), :]).T)

    here = pltpu.make_async_copy(tiles_here, delivered.at[pl.ds(col * CAP, CAP)], out_sem.at[4])
    here.start()
    outs.append(here)

    def put(at, source, target):
        copy = pltpu.make_async_copy(source, target, out_sem.at[at])
        copy.start()
        outs.append(copy)

    def square(first, second, third, fourth):
        return jnp.concatenate(
            [jnp.concatenate([first, second], axis=1), jnp.concatenate([third, fourth], axis=1)], axis=0
        )

    first_total.final.wait_recv()
    tile = first_total.tile
    diag_one_value = diag_one[...] - square(tile(0), tile(1), tile(1).T, tile(2))
    cross_total = square(tile(3), tile(4), tile(5), tile(6))
    diag_one[...] = diag_one_value
    put(1, diag_one, diag_one_out)
    cross_value = -(cross_total + exact(diag_one_value, above[...], plain))
    cross_two[...] = cross_value
    put(2, cross_two, cross_two_out)
    diag_two[...] = diag_two[...] + (exact(cross_total.T, above[...], plain) - exact(above_t, cross_value, plain))
    second_total.gather()
    second_total.finish()
    second_total.final.wait_recv()
    tile = second_total.tile
    diag_two[...] = diag_two[...] - square(tile(0), tile(1), tile(1).T, tile(2))
    put(3, diag_two, diag_two_out)

    for copy in tile_copies:
        copy.wait_recv()

    for panel in range(2):

        @pl.when(turns)
        def _():
            turn[panel].wait_send()

        @pl.when(jnp.logical_not(turns))
        def _():
            end_climb(own, panel, 0, y)
            end_climb(turned, panel, 1, 1 - y)

        pl.when(relays_move)(lambda: passed[panel].wait_send())

    for copy in outs:
        copy.wait()
    for copy in first_total.sent + second_total.sent + tile_copies:
        copy.wait_send()
    for at in range(CHUNKS):
        for copy in (near_copy(at), far_copy(at), relay_copy(at)):
            copy.wait_send()
        for step in range(4):
            pair_copy(at, step).wait_send()
        for slot, peer in enumerate((near, away, near)):
            major_copy(at, slot, peer).wait_send()


def place_kernel(count, *refs):
    sources, targets, buffers, sems = refs[:count], refs[count : 2 * count], refs[2 * count : -1], refs[-1]
    loads = [pltpu.make_async_copy(sources[at], buffers[at], sems.at[0, at]) for at in range(count)]
    stores = [pltpu.make_async_copy(buffers[at], targets[at], sems.at[1, at]) for at in range(count)]
    for copy in loads:
        copy.start()
    for load, store in zip(loads, stores):
        load.wait()
        store.start()
    for copy in stores:
        copy.wait()


def fused(matrix, panel_one, panel_two, struct_one, struct_two, lower_one, above, lower_two, tile_owner):
    depth, _ = matrix.shape
    span, width = panel_one.shape
    chunk = 2 * width // CHUNKS
    tile_count = tile_owner.shape[0]
    share = 6 * (width // 2)
    mask_rows = -(-(COLS + 1) * (span // LANES) // 8) * 8
    dma = pltpu.SemaphoreType.DMA
    vmem = lambda *shape: pltpu.VMEM(shape, jnp.float32)
    half_vmem = lambda *shape: pltpu.VMEM(shape, jnp.bfloat16)
    anywhere = pl.BlockSpec(memory_space=pl.ANY)
    scalars = pl.BlockSpec(memory_space=pltpu.SMEM)
    shape = lambda *dims: jax.ShapeDtypeStruct(dims, jnp.float32)
    results = pl.pallas_call(
        fused_kernel,
        out_shape=[
            shape(span, width),
            shape(width, width),
            shape(width, width),
            shape(width, width),
            shape(COLS * CAP, span // tile_count, width),
        ],
        in_specs=[anywhere] * 8 + [scalars],
        out_specs=[anywhere] * 5,
        scratch_shapes=[
            vmem(span, width),
            vmem(width, width),
            vmem(width, width),
            vmem(width, width),
            vmem(CAP, span // tile_count, width),
            pltpu.VMEM((struct_one.shape[0] // LANES, LANES), jnp.int32),
            pltpu.VMEM((struct_two.shape[0] // LANES, LANES), jnp.int32),
            vmem(width, width),
            vmem(width, width),
            vmem(width, width),
            vmem(2, depth, span),
            half_vmem(8, depth, span),
            half_vmem(8, depth, span),
            vmem(2, span, width),
            vmem(COLS, CHUNKS, span, chunk),
            half_vmem(CHUNKS, 2 * chunk, depth),
            vmem(CHUNKS, 4, chunk, span),
            vmem(CHUNKS, 4, chunk, span),
            vmem(CHUNKS, 4, chunk, span),
            vmem(CHUNKS, 3, chunk, span),
            vmem(2, mask_rows, LANES),
            vmem(2, span, width),
            vmem(2, 2, span, width),
            vmem(CHUNKS, chunk, span),
            vmem(width, span),
            vmem(width, span),
            vmem(width, span),
            vmem(width, span),
            vmem(2 * share, LANES),
            vmem(share, LANES),
            vmem(share, LANES),
            vmem(CHIPS - 1, share // CHIPS, LANES),
            vmem(2 * share, LANES),
            vmem(COLS - 1, CAP, span // tile_count, width),
            dma((5,)),
            dma((5,)),
            dma((2,)),
            dma((2,)),
            dma((2, 2)),
            dma((2, 2, 3)),
            dma((2, CHUNKS)),
            dma((2, CHUNKS)),
            dma((2, CHUNKS)),
            dma((2, CHUNKS, 4)),
            dma((2, CHUNKS, 3)),
            dma((2, 2, 2)),
            dma((2, 2, CHIPS - 1)),
            dma((2, 2, CHIPS - 1)),
            dma((2, 2, COLS - 1)),
        ],
        compiler_params=pltpu.CompilerParams(
            collective_id=3, has_side_effects=True, vmem_limit_bytes=54 * 2**20
        ),
        cost_estimate=pl.CostEstimate(
            flops=12 * matrix.size * width, bytes_accessed=4 * matrix.size, transcendentals=0
        ),
    )(
        matrix,
        panel_one,
        panel_two,
        struct_one.reshape(-1, LANES),
        struct_two.reshape(-1, LANES),
        lower_one,
        above,
        lower_two,
        tile_owner.reshape(-1),
    )
    return tuple(pl.pallas_call(
        functools.partial(place_kernel, len(results)),
        out_shape=[shape(*result.shape) for result in results],
        in_specs=[anywhere] * len(results),
        out_specs=[anywhere] * len(results),
        scratch_shapes=[vmem(*result.shape) for result in results] + [dma((2, len(results)))],
        compiler_params=pltpu.CompilerParams(vmem_limit_bytes=60 * 2**20),
    )(*results))


def local(
    ancestor_inverse,
    panel_one,
    struct_one,
    lower_one,
    panel_two,
    struct_two,
    panel_above,
    lower_two,
    tile_owner,
):
    row_count = lax.axis_size("row")
    col_count = lax.axis_size("col")
    row_index = lax.axis_index("row")
    col_index = lax.axis_index("col")
    local_rows = panel_one.shape[0]
    if fits_fused(ancestor_inverse, panel_one, struct_one, struct_two, tile_owner, row_count, col_count):
        return fused(
            ancestor_inverse,
            panel_one,
            panel_two,
            struct_one,
            struct_two,
            lower_one,
            panel_above,
            lower_two,
            tile_owner,
        )
    order = local_rows * row_count * col_count
    width = panel_one.shape[1]
    mask_one = row_mask(struct_one, order)
    mask_two = row_mask(struct_two, order)
    panel_start = (row_index * col_count + col_index) * local_rows
    result_start = (col_index * row_count + row_index) * local_rows
    local_one = panel_one * lax.dynamic_slice_in_dim(mask_one, panel_start, local_rows)[:, None]
    local_two = panel_two * lax.dynamic_slice_in_dim(mask_two, panel_start, local_rows)[:, None]
    result_mask_one = lax.dynamic_slice_in_dim(mask_one, result_start, local_rows)[:, None]
    result_mask_two = lax.dynamic_slice_in_dim(mask_two, result_start, local_rows)[:, None]

    both = jnp.concatenate([local_one, local_two], axis=1)
    gathered = lax.all_gather(both, "col", axis=0, tiled=True)
    product = scatter_rows(contract_rows(ancestor_inverse, gathered, lax.Precision.HIGH), row_count)
    moves = [(f, (f % row_count) * col_count + f // row_count) for f in range(row_count * col_count)]
    resident = lax.ppermute(both, ("row", "col"), moves)
    resident_one = resident[:, :width]
    resident_two = resident[:, width:]
    inverse_one = -product[:, :width] * result_mask_one
    inverse_two = -(product[:, width:] + matmul(inverse_one, panel_above)) * result_mask_two
    grams = (
        contract_rows(resident_one, inverse_one),
        contract_rows(inverse_one, resident_two),
        contract_rows(resident_two, inverse_two),
    )
    lanes = 128
    packed = jnp.concatenate(
        [gram[:, at : at + lanes] for gram in grams for at in range(0, width, lanes)], axis=0
    )
    sums = sum_everywhere(packed, row_count, col_count).reshape(len(grams), width // lanes, width, lanes)
    gram_one, cross_sum, gram_two = (
        jnp.concatenate([sums[at, block] for block in range(width // lanes)], axis=1) for at in range(len(grams))
    )
    diag_one = matmul(lower_one.T, lower_one) - gram_one
    cross_two = -(cross_sum + matmul(diag_one, panel_above))
    diag_two = matmul(lower_two.T, lower_two) - gram_two - matmul(panel_above.T, cross_two)
    delivered = deliver(inverse_two, tile_owner, col_count)
    return (inverse_one, diag_one, cross_two, diag_two, delivered)


def solution(mesh):
    return jax.shard_map(
        local,
        mesh=mesh,
        in_specs=(
            P("row", "col"),
            P(("row", "col"), None),
            P(),
            P(),
            P(("row", "col"), None),
            P(),
            P(),
            P(),
            P(("col", "row"), None),
        ),
        out_specs=(P(("col", "row"), None), P(), P(), P(), P(("row", "col"), None, None)),
        check_vma=False,
    )
```

```python
import functools

import jax
import jax.numpy as jnp
from jax import lax
from jax.experimental import pallas as pl
from jax.experimental.pallas import tpu as pltpu
from jax.sharding import PartitionSpec as P

CAP = 2


def matmul(left, right):
    return jnp.dot(left, right, precision=lax.Precision.HIGHEST, preferred_element_type=jnp.float32)


def contract_rows(left, right, precision=lax.Precision.HIGHEST):
    return lax.dot_general(
        left,
        right,
        (((0,), (0,)), ((), ())),
        precision=precision,
        preferred_element_type=jnp.float32,
    )


def row_mask(struct, count):
    lanes = 128
    high = struct // lanes
    low = struct % lanes
    high_hot = (jnp.arange(count // lanes, dtype=jnp.int32)[:, None] == high[None, :]).astype(jnp.bfloat16)
    low_hot = (jnp.arange(lanes, dtype=jnp.int32)[:, None] == low[None, :]).astype(jnp.bfloat16)
    counts = lax.dot_general(high_hot, low_hot, (((1,), (1,)), ((), ())), preferred_element_type=jnp.float32)
    return (counts > 0.5).astype(jnp.float32).reshape(count)


MESH = pl.DeviceIdType.MESH


def greet(peers):
    barrier = pltpu.get_barrier_semaphore()
    for peer in peers:
        pl.semaphore_signal(barrier, inc=1, device_id=peer, device_id_type=MESH)
    pl.semaphore_wait(barrier, len(peers))


def scatter_kernel(rows, value_ref, out_ref, pair_in, total, major_in, pair_send, pair_recv, major_send, major_recv):
    majors = rows // 2
    row = lax.axis_index("row")
    col = lax.axis_index("col")
    major, minor = row // 2, row % 2
    partner = (major * 2 + 1 - minor, col)

    def peer(offset):
        return (lax.rem(major + offset, majors) * 2 + minor, col)

    greet([partner] + [peer(offset) for offset in range(1, majors)])
    order = sorted(range(1, majors), key=lambda offset: -min(offset, majors - offset)) + [0]
    started = []
    pair_copies = {}
    for offset in order:
        target = lax.rem(major + offset, majors)
        copy = pltpu.make_async_remote_copy(
            src_ref=value_ref.at[target * 2 + 1 - minor],
            dst_ref=pair_in.at[offset],
            send_sem=pair_send.at[offset],
            recv_sem=pair_recv.at[offset],
            device_id=partner,
            device_id_type=MESH,
        )
        copy.start()
        pair_copies[offset] = copy
    for offset in order:
        target = lax.rem(major + offset, majors)
        pair_copies[offset].wait_recv()
        total[offset] = pair_in[offset] + value_ref[target * 2 + minor]
        if offset:
            copy = pltpu.make_async_remote_copy(
                src_ref=total.at[offset],
                dst_ref=major_in.at[offset - 1],
                send_sem=major_send.at[offset - 1],
                recv_sem=major_recv.at[offset - 1],
                device_id=peer(offset),
                device_id_type=MESH,
            )
            copy.start()
            started.append(copy)
    for copy in started:
        copy.wait_recv()
    result = total[0]
    for slot in range(majors - 1):
        result = result + major_in[slot]
    out_ref[...] = result
    for copy in started:
        copy.wait_send()
    for offset in order:
        pair_copies[offset].wait_send()


def scatter_rows(value, rows):
    chunk, width = value.shape[0] // rows, value.shape[1]
    majors = rows // 2
    dma = pltpu.SemaphoreType.DMA
    return pl.pallas_call(
        functools.partial(scatter_kernel, rows),
        out_shape=jax.ShapeDtypeStruct((chunk, width), jnp.float32),
        in_specs=[pl.BlockSpec(memory_space=pltpu.VMEM)],
        out_specs=pl.BlockSpec(memory_space=pltpu.VMEM),
        scratch_shapes=[
            pltpu.VMEM((majors, chunk, width), jnp.float32),
            pltpu.VMEM((majors, chunk, width), jnp.float32),
            pltpu.VMEM((majors - 1, chunk, width), jnp.float32),
            dma((majors,)),
            dma((majors,)),
            dma((majors - 1,)),
            dma((majors - 1,)),
        ],
        compiler_params=pltpu.CompilerParams(
            collective_id=0, has_side_effects=True, vmem_limit_bytes=40 * 2**20
        ),
    )(value.reshape(rows, chunk, width))


def sum_kernel(rows, cols, value_ref, out_ref, full, sum_a, sum_b, in_a, in_b, in_c, *sems):
    row = lax.axis_index("row")
    col = lax.axis_index("col")
    outer = cols // 2
    far, core = col // 2, col % 2
    half = outer * rows
    base_a = core * half
    base_b = base_a + far * rows
    base_c = base_b + row

    def pair_peer(offset):
        return (row, far * 2 + 1 - core)

    def far_peer(offset):
        return (row, lax.rem(far + offset, outer) * 2 + core)

    def row_peer(offset):
        return (lax.rem(row + offset, rows), col)

    greet(
        [pair_peer(1)]
        + [far_peer(offset) for offset in range(1, outer)]
        + [row_peer(offset) for offset in range(1, rows)]
    )

    def exchange(count, peer, source, landing, stage):
        copies = []
        for offset in range(1, count):
            copy = pltpu.make_async_remote_copy(
                src_ref=source(offset),
                dst_ref=landing(offset),
                send_sem=sems[2 * stage].at[offset - 1],
                recv_sem=sems[2 * stage + 1].at[offset - 1],
                device_id=peer(offset),
                device_id_type=MESH,
            )
            copy.start()
            copies.append(copy)
        for copy in copies:
            copy.wait_recv()
        return copies

    pending = []
    pending += exchange(
        2, pair_peer, lambda k: value_ref.at[pl.ds((1 - core) * half, half)], lambda k: in_a.at[k - 1], 0
    )
    sum_a[...] = value_ref[pl.ds(base_a, half)] + in_a[0]
    pending += exchange(
        outer, far_peer, lambda k: sum_a.at[pl.ds(lax.rem(far + k, outer) * rows, rows)], lambda k: in_b.at[k - 1], 1
    )
    total = sum_a[pl.ds(far * rows, rows)]
    for slot in range(outer - 1):
        total = total + in_b[slot]
    sum_b[...] = total
    pending += exchange(
        rows, row_peer, lambda k: sum_b.at[lax.rem(row + k, rows)], lambda k: in_c.at[k - 1], 2
    )
    total = sum_b[row]
    for slot in range(rows - 1):
        total = total + in_c[slot]
    full[base_c] = total
    pending += exchange(rows, row_peer, lambda k: full.at[base_c], lambda k: full.at[base_c], 3)
    pending += exchange(
        outer, far_peer, lambda k: full.at[pl.ds(base_b, rows)], lambda k: full.at[pl.ds(base_b, rows)], 4
    )
    pending += exchange(
        2, pair_peer, lambda k: full.at[pl.ds(base_a, half)], lambda k: full.at[pl.ds(base_a, half)], 5
    )
    out_ref[...] = full[...]
    for copy in pending:
        copy.wait_send()


def sum_everywhere(value, rows, cols):
    devices = rows * cols
    lanes = value.shape[1]
    depth = value.shape[0] // devices
    outer = cols // 2
    dma = pltpu.SemaphoreType.DMA
    vmem = lambda *lead: pltpu.VMEM(lead + (depth, lanes), jnp.float32)
    total = pl.pallas_call(
        functools.partial(sum_kernel, rows, cols),
        out_shape=jax.ShapeDtypeStruct((devices, depth, lanes), jnp.float32),
        in_specs=[pl.BlockSpec(memory_space=pltpu.VMEM)],
        out_specs=pl.BlockSpec(memory_space=pltpu.VMEM),
        scratch_shapes=[
            vmem(devices),
            vmem(devices // 2),
            vmem(rows),
            vmem(1, devices // 2),
            vmem(outer - 1, rows),
            vmem(rows - 1),
        ]
        + [dma((count - 1,)) for count in (2, outer, rows, rows, outer, 2) for _ in range(2)],
        compiler_params=pltpu.CompilerParams(
            collective_id=1, has_side_effects=True, vmem_limit_bytes=24 * 2**20
        ),
        cost_estimate=pl.CostEstimate(flops=0, bytes_accessed=100 * value.size * 4, transcendentals=0),
    )(value.reshape(devices, depth, lanes))
    return total.reshape(value.shape)


def deliver(values, tile_owner, col_count):
    tile_count = tile_owner.shape[0]
    tile_rows = values.shape[0] // tile_count
    all_tiles = values.reshape(tile_count, tile_rows, values.shape[1])
    owner_col = tile_owner[:, 0]
    col_ids = jnp.arange(col_count, dtype=jnp.int32)
    onehot = (owner_col[:, None] == col_ids[None, :]).astype(jnp.int32)
    tile_rank = jnp.sum((jnp.cumsum(onehot, axis=0) - onehot) * onehot, axis=1)
    slot_index = jnp.arange(CAP, dtype=jnp.int32)
    select = (
        (owner_col[None, None, :] == col_ids[:, None, None])
        & (tile_rank[None, None, :] == slot_index[None, :, None])
    ).astype(jnp.float32)
    outgoing = jnp.einsum("cks,srb->ckrb", select, all_tiles, precision=lax.Precision.HIGHEST)
    incoming = lax.all_to_all(outgoing, "col", split_axis=0, concat_axis=0, tiled=True)
    return incoming.reshape(col_count * CAP, tile_rows, values.shape[1])


ROWS, COLS, CHIPS = 8, 4, 16
CHUNKS = 4
LANES = 128


def fits_fused(matrix, panel, struct_one, struct_two, tile_owner, rows, cols):
    span, width = panel.shape
    return (
        (rows, cols) == (ROWS, COLS)
        and span % LANES == 0
        and width == 2 * LANES
        and matrix.shape == (cols * span, rows * span)
        and struct_one.shape[0] % LANES == 0
        and struct_two.shape[0] % LANES == 0
        and span % (8 * tile_owner.shape[0]) == 0
    )


def exact(left, right, contract):
    return lax.dot_general(
        left, right, (contract, ((), ())), precision=lax.Precision.HIGHEST, preferred_element_type=jnp.float32
    )


def fused_kernel(
    matrix, panel_one, panel_two, struct_one_in, struct_two_in, lower_one_in, above_in, lower_two_in, owner,
    inverse_one_out, diag_one_out, cross_two_out, diag_two_out, delivered,
    inverse_one, diag_one, cross_two, diag_two, tiles_here,
    struct_one, struct_two, lower_one, above, lower_two, window, high, low, own, land, left, other, mine, pair_in, major_in, masks, turned, resident, product,
    inv_one_t, part_two_t, panel_two_t, correction, packed, fold_in, fold, part_in, full, outgoing,
    out_sem, small_sem, fetch_sem, own_sem, turn_sem, move_sem, near_gather, far_gather, relay_gather, pair_sem, major_sem, sum_sem, chip_sem,
    spread_sem, tile_sem,
):
    row = lax.axis_index("row")
    col = lax.axis_index("col")
    z, y = row // 2, row % 2
    x, core = col // 2, col % 2
    upper, lower = z // 2, z % 2
    chip = (z * 2 + y) * 2 + x
    depth, total_columns = matrix.shape
    span, width = own.shape[1:]
    chunk = left.shape[1] // 2
    per_panel = width // chunk

    def device(z_at, y_at, x_at, core_at):
        return (z_at * 2 + y_at, x_at * 2 + core_at)

    partner = device(z, y, x, 1 - core)
    across = device(z, y, 1 - x, core)
    beside = device(z, 1 - y, x, core)
    near = device(upper * 2 + 1 - lower, y, x, core)
    inner = device(3 - z, y, x, core)
    ends = upper == lower
    middle = upper != lower

    def remote(source, target, sems, at, peer):
        return pltpu.make_async_remote_copy(
            src_ref=source,
            dst_ref=target,
            send_sem=sems.at[(0,) + at],
            recv_sem=sems.at[(1,) + at],
            device_id=peer,
            device_id_type=MESH,
        )

    own_copies = [
        pltpu.make_async_copy(panel, own.at[at], own_sem.at[at]) for at, panel in enumerate((panel_one, panel_two))
    ]
    for copy in own_copies:
        copy.start()

    def fetch(step, which):
        rank = jnp.where(ends, step, jnp.where(step == 0, 0, jnp.where(step == 3, 2, 5 - 2 * step)))
        target = jnp.where(upper == 0, 3 - rank, rank) * 2 + lax.rem(1 - y + which, 2)
        return pltpu.make_async_copy(
            matrix.at[:, pl.ds(pl.multiple_of(target * span, LANES), span)], window.at[which], fetch_sem.at[which]
        )

    small_pairs = (
        (struct_one_in, struct_one),
        (struct_two_in, struct_two),
        (lower_one_in, lower_one),
        (above_in, above),
        (lower_two_in, lower_two),
    )
    small_copies = [
        pltpu.make_async_copy(source, target, small_sem.at[at]) for at, (source, target) in enumerate(small_pairs)
    ]
    for copy in small_copies:
        copy.start()
    barrier = pltpu.get_barrier_semaphore()
    devices = ROWS * COLS
    for offset in range(1, devices):
        flat = lax.rem(row * COLS + col + offset, devices)
        pl.semaphore_signal(barrier, inc=1, device_id=(flat // COLS, lax.rem(flat, COLS)), device_id_type=MESH)
    for which in range(2):
        fetch(0, which).start()
    pl.semaphore_wait(barrier, devices - 1)
    for copy in own_copies:
        copy.wait()

    def piece(at):
        return own.at[at // per_panel, :, pl.ds(at % per_panel * chunk, chunk)]

    def far_copy(at, source=None):
        return remote(land.at[0, at] if source is None else source, land.at[col, at], far_gather, (at,), across)

    def near_copy(at, source=None):
        return remote(land.at[0, at] if source is None else source, land.at[col, at], near_gather, (at,), partner)

    def relay_copy(at):
        slot = (1 - x) * 2 + core
        return remote(land.at[slot, at], land.at[slot, at], relay_gather, (at,), partner)

    turns = core != y
    direct = jnp.where(x == upper, 0, 1)
    relays_move = lower == x

    def move_copy(source, slot, panel, at, peer):
        return pltpu.make_async_remote_copy(
            src_ref=source.at[panel],
            dst_ref=resident.at[slot, panel],
            send_sem=move_sem.at[0, panel, at],
            recv_sem=move_sem.at[1, panel, slot],
            device_id=peer,
            device_id_type=MESH,
        )

    def climb(source, panel, at, from_y):
        peer = device(2 * from_y + x, y, x, lower)
        return move_copy(source, direct, panel, at, peer), (peer[0] == row) & (peer[1] == col)

    def start_climb(source, panel, at, from_y):
        copy, stays = climb(source, panel, at, from_y)
        kept = pltpu.make_async_copy(source.at[panel], resident.at[direct, panel], move_sem.at[1, panel, direct])
        pl.when(stays)(lambda: kept.start())
        pl.when(jnp.logical_not(stays))(lambda: copy.start())

    def end_climb(source, panel, at, from_y):
        copy, stays = climb(source, panel, at, from_y)
        pl.when(jnp.logical_not(stays))(lambda: copy.wait_send())

    turn = [remote(own.at[panel], turned.at[panel], turn_sem, (panel,), beside) for panel in range(2)]
    passed = [move_copy(resident.at[1], 0, panel, 2, across) for panel in range(2)]

    def climb_turned(panel):
        @pl.when(jnp.logical_not(turns))
        def _():
            turn[panel].wait_recv()
            start_climb(turned, panel, 1, 1 - y)

    def pass_on(panel):
        @pl.when(relays_move)
        def _():
            move_copy(own, 1, panel, 0, beside).wait_recv()
            passed[panel].start()

    for at in range(CHUNKS):
        far_copy(at, piece(at)).start()
        near_copy(at, piece(at)).start()
        if at == 0:
            @pl.when(turns)
            def _():
                for copy in turn:
                    copy.start()

            @pl.when(jnp.logical_not(turns))
            def _():
                for panel in range(2):
                    start_climb(own, panel, 0, y)

    for at in range(CHUNKS):
        land[col, at] = piece(at)[...]

    for copy in small_copies:
        copy.wait()
    blocks = span // LANES
    slots_of = COLS * blocks
    mask_rows = masks.shape[1]
    place_rows = lax.broadcasted_iota(jnp.int32, (mask_rows, LANES), 0)
    block_base = row * slots_of
    result_base = (col * ROWS + row) * blocks
    wanted = jnp.where(place_rows < slots_of, block_base + place_rows, result_base + place_rows - slots_of)
    lane_ids = lax.broadcasted_iota(jnp.int32, (LANES, LANES), 0)
    for at, struct in enumerate((struct_one, struct_two)):
        count = struct.shape[0]
        group = max(size for size in range(1, 17) if count % size == 0)
        counts = jnp.zeros((mask_rows, LANES), jnp.float32)
        for begin in range(0, count, group):
            highs, lows = [], []
            for entry in range(begin, begin + group):
                value = struct[pl.ds(entry, 1), :]
                highs.append(jnp.where(wanted == value // LANES, 1.0, 0.0))
                lows.append(jnp.where(lane_ids == value % LANES, 1.0, 0.0))
            counts = counts + lax.dot_general(
                jnp.concatenate(highs, axis=1).astype(jnp.bfloat16),
                jnp.concatenate(lows, axis=1).astype(jnp.bfloat16),
                (((1,), (1,)), ((), ())),
                preferred_element_type=jnp.float32,
            )
        masks[at] = jnp.where(counts > 0.5, 1.0, 0.0)
    diag_one[...] = exact(lower_one[...].T, lower_one[...], ((1,), (0,)))
    diag_two[...] = exact(lower_two[...].T, lower_two[...], ((1,), (0,)))

    def mask_of(panel, begin):
        return jnp.concatenate([masks[panel, pl.ds(begin + at, 1), :] for at in range(blocks)], axis=1)

    def prepare(at):
        near_copy(at).wait_recv()
        far_copy(at).wait_recv()
        relay_copy(at).start()
        relay_copy(at).wait_recv()
        for slot in range(COLS):
            value = land[slot, at].T * mask_of(at // per_panel, slot * blocks)
            upper_part = value.astype(jnp.bfloat16)
            columns = pl.ds(slot * span, span)
            left[at, pl.ds(0, chunk), columns] = upper_part
            left[at, pl.ds(chunk, chunk), columns] = (value - upper_part.astype(jnp.float32)).astype(jnp.bfloat16)

    def pair_copy(at, step):
        return remote(other.at[at, step], pair_in.at[at, step], pair_sem, (at, step), beside)

    def multiply(at, step, which):
        target = step * 2 + which
        both = jnp.dot(left[at], high[target], preferred_element_type=jnp.float32)
        rest = jnp.dot(left[at, pl.ds(0, chunk), :], low[target], preferred_element_type=jnp.float32)
        value = both[:chunk] + (both[chunk:] + rest)
        if which == 0:
            other[at, step] = value
            pair_copy(at, step).start()
        else:
            mine[at, step] = value

    def first_step(step, carry):
        for which in range(2):
            fetch(step, which).wait()
            target = step * 2 + which
            for begin in range(0, depth, 256):
                size = min(256, depth - begin)
                value = window[which, pl.ds(begin, size), :]
                upper_part = value.astype(jnp.bfloat16)
                high[target, pl.ds(begin, size), :] = upper_part
                low[target, pl.ds(begin, size), :] = (value - upper_part.astype(jnp.float32)).astype(jnp.bfloat16)

            @pl.when(step + 1 < 4)
            def _():
                fetch(step + 1, which).start()

            multiply(0, step, which)
        pl.when(step == 1)(lambda: climb_turned(1))
        return carry

    def later_steps(chunks, begin, end):
        def body(step, carry):
            for at in chunks:
                for which in range(2):
                    multiply(at, step, which)
            return carry

        lax.fori_loop(begin, end, body, 0)

    def major_copy(at, step):
        slot = jnp.where(ends, (0, 2, 3)[step], (1, 3, 4)[step])
        return pltpu.make_async_remote_copy(
            src_ref=mine.at[at, step],
            dst_ref=major_in.at[at, slot],
            send_sem=major_sem.at[0, at, step],
            recv_sem=major_sem.at[1, at, slot],
            device_id=near if step == 1 else (jnp.where(ends, near[0], inner[0]), col),
            device_id_type=MESH,
        )

    def arrived(at, slot):
        pltpu.make_async_copy(mine.at[at, 0], major_in.at[at, slot], major_sem.at[1, at, slot]).wait()
        return major_in[at, slot]

    def forward(at, step):
        pair_copy(at, step).wait_recv()
        mine[at, step] = mine[at, step] + pair_in[at, step]

        @pl.when(middle)
        def _():
            mine[at, step] = mine[at, step] + arrived(at, step)

        major_copy(at, step).start()

    def collect(at):
        pair_copy(at, 3).wait_recv()
        product[at] = (mine[at, 3] + pair_in[at, 3]) + arrived(at, 3)

        @pl.when(middle)
        def _():
            product[at] = product[at] + arrived(at, 4)

    half = width // 2
    share_of = (4 * half, half, half)
    starts = (0, 4 * half, 5 * half)
    order = sorted(range(1, CHIPS), key=lambda offset: -min(offset, CHIPS - offset))
    plain, last = ((1,), (0,)), ((1,), (1,))

    def chip_at(offset):
        flat = lax.rem(chip + offset, CHIPS)
        return flat, device(flat // 4, lax.rem(flat // 2, 2), lax.rem(flat, 2), core)

    class Total:
        def __init__(self, at):
            self.at, self.share, self.start = at, share_of[at], starts[at]
            self.rows = self.share // CHIPS
            self.base = 2 * self.start + core * self.share
            self.half_rows = pl.ds(self.base, self.share)
            self.sent = []

        def partner_copy(self, stage, source, target):
            copy = remote(source, target, sum_sem, (self.at, stage), partner)
            self.sent.append(copy)
            copy.start()
            return copy

        def begin(self, tiles):
            for at in range(2 * self.share // half):
                tile = tiles[at] if at < len(tiles) else jnp.zeros((half, half), jnp.float32)
                packed[pl.ds(2 * self.start + at * half, half), :] = tile
            theirs = pl.ds(2 * self.start + (1 - core) * self.share, self.share)
            self.first = self.partner_copy(0, packed.at[theirs], fold_in.at[pl.ds(self.start, self.share)])

        def scatter(self):
            self.first.wait_recv()
            rows = pl.ds(self.start, self.share)
            fold[rows, :] = packed[self.half_rows, :] + fold_in[rows, :]
            self.copies = []
            for offset in order:
                flat, peer = chip_at(offset)
                copy = remote(
                    fold.at[pl.ds(self.start + flat * self.rows, self.rows)],
                    part_in.at[offset - 1, pl.ds(self.start // CHIPS, self.rows)],
                    chip_sem,
                    (self.at, offset - 1),
                    peer,
                )
                copy.start()
                self.copies.append(copy)

        def gather(self):
            for copy in self.copies:
                copy.wait_recv()
            value = fold[pl.ds(self.start + chip * self.rows, self.rows), :]
            for slot in range(CHIPS - 1):
                value = value + part_in[slot, pl.ds(self.start // CHIPS, self.rows), :]
            mine_rows = pl.ds(self.base + chip * self.rows, self.rows)
            full[mine_rows, :] = value
            self.sent += self.copies
            self.copies = []
            for offset in order:
                copy = remote(
                    full.at[mine_rows], full.at[mine_rows], spread_sem, (self.at, offset - 1), chip_at(offset)[1]
                )
                copy.start()
                self.copies.append(copy)

        def finish(self):
            for copy in self.copies:
                copy.wait_recv()
            self.final = self.partner_copy(1, full.at[self.half_rows], full.at[self.half_rows])
            self.sent += self.copies

        def tile(self, at):
            return full[pl.ds(2 * self.start + at * half, half), :]

    def quarters(value, places):
        return [value[i * half : (i + 1) * half, j * half : (j + 1) * half] for i, j in places]

    upper_places = ((0, 0), (0, 1), (1, 1))
    every_place = ((0, 0), (0, 1), (1, 0), (1, 1))
    tile_count = owner.shape[0]
    tile_rows = span // tile_count
    names = [owner[at] for at in range(tile_count)]
    ranks = [
        sum([jnp.where(names[before] == names[at], 1, 0) for before in range(at)], jnp.int32(0))
        for at in range(tile_count)
    ]
    tile_copies = []

    def send_tiles(part, values):
        columns = pl.ds(part * half, half)

        def slot_value(name, rank):
            value = jnp.zeros((tile_rows, half), jnp.float32)
            for at in range(tile_count):
                chosen = (names[at] == name) & (ranks[at] == rank)
                value = jnp.where(chosen, values[at * tile_rows : (at + 1) * tile_rows], value)
            return value

        for offset in range(1, COLS):
            name = lax.rem(col + offset, COLS)
            for rank in range(CAP):
                outgoing[offset - 1, rank, :, columns] = slot_value(name, rank)
            copy = remote(
                outgoing.at[offset - 1, :, :, columns],
                delivered.at[pl.ds(col * CAP, CAP), :, columns],
                tile_sem,
                (part, offset - 1),
                (row, name),
            )
            copy.start()
            tile_copies.append(copy)
        for rank in range(CAP):
            tiles_here[rank, :, columns] = slot_value(col, rank)

    first_total, middle_total, second_total = Total(0), Total(1), Total(2)

    prepare(0)
    climb_turned(0)
    lax.fori_loop(0, 4, first_step, 0)
    prepare(1)
    def only(where, *steps):
        @pl.when(where)
        def _():
            for at, step in steps:
                forward(at, step)

    only(ends, (0, 0))
    later_steps((1,), 0, 4)
    only(middle, (0, 0))
    only(ends, (0, 1))
    prepare(2)
    prepare(3)
    only(ends, (0, 2))
    later_steps((2, 3), 0, 2)
    only(middle, (0, 1), (0, 2))
    only(ends, (1, 0))
    pass_on(0)
    pass_on(1)
    only(ends, (1, 1))
    collect(0)
    only(middle, (1, 0), (1, 1))
    forward(1, 2)
    only(ends, (2, 0))
    collect(1)
    only(ends, (3, 0))
    only(middle, (2, 0))
    one_row = mask_of(0, slots_of)
    two_row = mask_of(1, slots_of)
    inv_one_t[...] = -(jnp.concatenate([product[at] for at in range(per_panel)], axis=0) * one_row)
    for copy in passed:
        copy.wait_recv()
    panel_two_t[...] = resident[0, 1].T
    gram_one = exact(resident[0, 0].T, inv_one_t[...], last)
    cross_sum = exact(inv_one_t[...] * two_row, panel_two_t[...], last)
    first_total.begin(quarters(gram_one, upper_places) + quarters(cross_sum, every_place))
    above_t = above[...].T
    correction[...] = exact(above_t, inv_one_t[...], plain) * two_row
    inverse_one[...] = inv_one_t[...].T
    outs = [pltpu.make_async_copy(inverse_one, inverse_one_out, out_sem.at[0])]
    outs[0].start()
    first_total.scatter()
    later_steps((2, 3), 2, 4)
    only(middle, (3, 0))
    forward(2, 1)
    forward(3, 1)
    first_total.gather()
    forward(2, 2)
    forward(3, 2)
    collect(2)
    low_half, high_half = pl.ds(0, half), pl.ds(half, half)
    part_two_t[low_half, :] = -(product[2] * two_row)
    gram_left = exact(panel_two_t[...], part_two_t[low_half, :], last)
    middle_total.begin([gram_left[:half], gram_left[half:]])
    early = (part_two_t[low_half, :] - correction[low_half, :]).T
    middle_total.scatter()
    send_tiles(0, early)
    collect(3)
    part_two_t[high_half, :] = -(product[3] * two_row)
    second_total.begin([exact(panel_two_t[high_half, :], part_two_t[high_half, :], last)])
    late = (part_two_t[high_half, :] - correction[high_half, :]).T
    second_total.scatter()
    send_tiles(1, late)
    middle_total.gather()
    first_total.finish()

    here = pltpu.make_async_copy(tiles_here, delivered.at[pl.ds(col * CAP, CAP)], out_sem.at[4])
    here.start()
    outs.append(here)

    def put(at, source, target):
        copy = pltpu.make_async_copy(source, target, out_sem.at[at])
        copy.start()
        outs.append(copy)

    def square(first, second, third, fourth):
        return jnp.concatenate(
            [jnp.concatenate([first, second], axis=1), jnp.concatenate([third, fourth], axis=1)], axis=0
        )

    first_total.final.wait_recv()
    tile = first_total.tile
    diag_one_value = diag_one[...] - square(tile(0), tile(1), tile(1).T, tile(2))
    cross_total = square(tile(3), tile(4), tile(5), tile(6))
    diag_one[...] = diag_one_value
    put(1, diag_one, diag_one_out)
    cross_value = -(cross_total + exact(diag_one_value, above[...], plain))
    cross_two[...] = cross_value
    put(2, cross_two, cross_two_out)
    diag_two[...] = diag_two[...] + (exact(cross_total.T, above[...], plain) - exact(above_t, cross_value, plain))
    second_total.gather()
    middle_total.finish()
    middle_total.final.wait_recv()
    tile = middle_total.tile
    second_total.finish()
    second_total.final.wait_recv()
    diag_two[...] = diag_two[...] - square(tile(0), tile(1).T, tile(1), second_total.tile(0))
    put(3, diag_two, diag_two_out)

    for copy in tile_copies:
        copy.wait_recv()

    for panel in range(2):

        @pl.when(turns)
        def _():
            turn[panel].wait_send()

        @pl.when(jnp.logical_not(turns))
        def _():
            end_climb(own, panel, 0, y)
            end_climb(turned, panel, 1, 1 - y)

        pl.when(relays_move)(lambda: passed[panel].wait_send())

    for copy in outs:
        copy.wait()
    for copy in first_total.sent + middle_total.sent + second_total.sent + tile_copies:
        copy.wait_send()
    for at in range(CHUNKS):
        for copy in (near_copy(at), far_copy(at), relay_copy(at)):
            copy.wait_send()
        for step in range(4):
            pair_copy(at, step).wait_send()
        for step in range(3):
            major_copy(at, step).wait_send()


def place_kernel(count, *refs):
    sources, targets, buffers, sems = refs[:count], refs[count : 2 * count], refs[2 * count : -1], refs[-1]
    loads = [pltpu.make_async_copy(sources[at], buffers[at], sems.at[0, at]) for at in range(count)]
    stores = [pltpu.make_async_copy(buffers[at], targets[at], sems.at[1, at]) for at in range(count)]
    for copy in loads:
        copy.start()
    for load, store in zip(loads, stores):
        load.wait()
        store.start()
    for copy in stores:
        copy.wait()


def fused(matrix, panel_one, panel_two, struct_one, struct_two, lower_one, above, lower_two, tile_owner):
    depth, _ = matrix.shape
    span, width = panel_one.shape
    chunk = 2 * width // CHUNKS
    tile_count = tile_owner.shape[0]
    share = 6 * (width // 2)
    mask_rows = -(-(COLS + 1) * (span // LANES) // 8) * 8
    dma = pltpu.SemaphoreType.DMA
    vmem = lambda *shape: pltpu.VMEM(shape, jnp.float32)
    half_vmem = lambda *shape: pltpu.VMEM(shape, jnp.bfloat16)
    anywhere = pl.BlockSpec(memory_space=pl.ANY)
    scalars = pl.BlockSpec(memory_space=pltpu.SMEM)
    shape = lambda *dims: jax.ShapeDtypeStruct(dims, jnp.float32)
    results = pl.pallas_call(
        fused_kernel,
        out_shape=[
            shape(span, width),
            shape(width, width),
            shape(width, width),
            shape(width, width),
            shape(COLS * CAP, span // tile_count, width),
        ],
        in_specs=[anywhere] * 8 + [scalars],
        out_specs=[anywhere] * 5,
        scratch_shapes=[
            vmem(span, width),
            vmem(width, width),
            vmem(width, width),
            vmem(width, width),
            vmem(CAP, span // tile_count, width),
            pltpu.VMEM((struct_one.shape[0] // LANES, LANES), jnp.int32),
            pltpu.VMEM((struct_two.shape[0] // LANES, LANES), jnp.int32),
            vmem(width, width),
            vmem(width, width),
            vmem(width, width),
            vmem(2, depth, span),
            half_vmem(8, depth, span),
            half_vmem(8, depth, span),
            vmem(2, span, width),
            vmem(COLS, CHUNKS, span, chunk),
            half_vmem(CHUNKS, 2 * chunk, depth),
            vmem(CHUNKS, 4, chunk, span),
            vmem(CHUNKS, 4, chunk, span),
            vmem(CHUNKS, 4, chunk, span),
            vmem(CHUNKS, 5, chunk, span),
            vmem(2, mask_rows, LANES),
            vmem(2, span, width),
            vmem(2, 2, span, width),
            vmem(CHUNKS, chunk, span),
            vmem(width, span),
            vmem(width, span),
            vmem(width, span),
            vmem(width, span),
            vmem(2 * share, LANES),
            vmem(share, LANES),
            vmem(share, LANES),
            vmem(CHIPS - 1, share // CHIPS, LANES),
            vmem(2 * share, LANES),
            vmem(COLS - 1, CAP, span // tile_count, width),
            dma((5,)),
            dma((5,)),
            dma((2,)),
            dma((2,)),
            dma((2, 2)),
            dma((2, 2, 3)),
            dma((2, CHUNKS)),
            dma((2, CHUNKS)),
            dma((2, CHUNKS)),
            dma((2, CHUNKS, 4)),
            dma((2, CHUNKS, 5)),
            dma((2, 3, 2)),
            dma((2, 3, CHIPS - 1)),
            dma((2, 3, CHIPS - 1)),
            dma((2, 2, COLS - 1)),
        ],
        compiler_params=pltpu.CompilerParams(
            collective_id=3, has_side_effects=True, vmem_limit_bytes=58 * 2**20
        ),
        cost_estimate=pl.CostEstimate(
            flops=12 * matrix.size * width, bytes_accessed=4 * matrix.size, transcendentals=0
        ),
    )(
        matrix,
        panel_one,
        panel_two,
        struct_one.reshape(-1, LANES),
        struct_two.reshape(-1, LANES),
        lower_one,
        above,
        lower_two,
        tile_owner.reshape(-1),
    )
    return tuple(pl.pallas_call(
        functools.partial(place_kernel, len(results)),
        out_shape=[shape(*result.shape) for result in results],
        in_specs=[anywhere] * len(results),
        out_specs=[anywhere] * len(results),
        scratch_shapes=[vmem(*result.shape) for result in results] + [dma((2, len(results)))],
        compiler_params=pltpu.CompilerParams(vmem_limit_bytes=60 * 2**20),
    )(*results))


def local(
    ancestor_inverse,
    panel_one,
    struct_one,
    lower_one,
    panel_two,
    struct_two,
    panel_above,
    lower_two,
    tile_owner,
):
    row_count = lax.axis_size("row")
    col_count = lax.axis_size("col")
    row_index = lax.axis_index("row")
    col_index = lax.axis_index("col")
    local_rows = panel_one.shape[0]
    if fits_fused(ancestor_inverse, panel_one, struct_one, struct_two, tile_owner, row_count, col_count):
        return fused(
            ancestor_inverse,
            panel_one,
            panel_two,
            struct_one,
            struct_two,
            lower_one,
            panel_above,
            lower_two,
            tile_owner,
        )
    order = local_rows * row_count * col_count
    width = panel_one.shape[1]
    mask_one = row_mask(struct_one, order)
    mask_two = row_mask(struct_two, order)
    panel_start = (row_index * col_count + col_index) * local_rows
    result_start = (col_index * row_count + row_index) * local_rows
    local_one = panel_one * lax.dynamic_slice_in_dim(mask_one, panel_start, local_rows)[:, None]
    local_two = panel_two * lax.dynamic_slice_in_dim(mask_two, panel_start, local_rows)[:, None]
    result_mask_one = lax.dynamic_slice_in_dim(mask_one, result_start, local_rows)[:, None]
    result_mask_two = lax.dynamic_slice_in_dim(mask_two, result_start, local_rows)[:, None]

    both = jnp.concatenate([local_one, local_two], axis=1)
    gathered = lax.all_gather(both, "col", axis=0, tiled=True)
    product = scatter_rows(contract_rows(ancestor_inverse, gathered, lax.Precision.HIGH), row_count)
    moves = [(f, (f % row_count) * col_count + f // row_count) for f in range(row_count * col_count)]
    resident = lax.ppermute(both, ("row", "col"), moves)
    resident_one = resident[:, :width]
    resident_two = resident[:, width:]
    inverse_one = -product[:, :width] * result_mask_one
    inverse_two = -(product[:, width:] + matmul(inverse_one, panel_above)) * result_mask_two
    grams = (
        contract_rows(resident_one, inverse_one),
        contract_rows(inverse_one, resident_two),
        contract_rows(resident_two, inverse_two),
    )
    lanes = 128
    packed = jnp.concatenate(
        [gram[:, at : at + lanes] for gram in grams for at in range(0, width, lanes)], axis=0
    )
    sums = sum_everywhere(packed, row_count, col_count).reshape(len(grams), width // lanes, width, lanes)
    gram_one, cross_sum, gram_two = (
        jnp.concatenate([sums[at, block] for block in range(width // lanes)], axis=1) for at in range(len(grams))
    )
    diag_one = matmul(lower_one.T, lower_one) - gram_one
    cross_two = -(cross_sum + matmul(diag_one, panel_above))
    diag_two = matmul(lower_two.T, lower_two) - gram_two - matmul(panel_above.T, cross_two)
    delivered = deliver(inverse_two, tile_owner, col_count)
    return (inverse_one, diag_one, cross_two, diag_two, delivered)


def solution(mesh):
    return jax.shard_map(
        local,
        mesh=mesh,
        in_specs=(
            P("row", "col"),
            P(("row", "col"), None),
            P(),
            P(),
            P(("row", "col"), None),
            P(),
            P(),
            P(),
            P(("col", "row"), None),
        ),
        out_specs=(P(("col", "row"), None), P(), P(), P(), P(("row", "col"), None, None)),
        check_vma=False,
    )
```

```python
import functools

import jax
import jax.numpy as jnp
from jax import lax
from jax.experimental import pallas as pl
from jax.experimental.pallas import tpu as pltpu
from jax.sharding import PartitionSpec as P

CAP = 2


def matmul(left, right):
    return jnp.dot(left, right, precision=lax.Precision.HIGHEST, preferred_element_type=jnp.float32)


def contract_rows(left, right, precision=lax.Precision.HIGHEST):
    return lax.dot_general(
        left,
        right,
        (((0,), (0,)), ((), ())),
        precision=precision,
        preferred_element_type=jnp.float32,
    )


def row_mask(struct, count):
    lanes = 128
    high = struct // lanes
    low = struct % lanes
    high_hot = (jnp.arange(count // lanes, dtype=jnp.int32)[:, None] == high[None, :]).astype(jnp.bfloat16)
    low_hot = (jnp.arange(lanes, dtype=jnp.int32)[:, None] == low[None, :]).astype(jnp.bfloat16)
    counts = lax.dot_general(high_hot, low_hot, (((1,), (1,)), ((), ())), preferred_element_type=jnp.float32)
    return (counts > 0.5).astype(jnp.float32).reshape(count)


MESH = pl.DeviceIdType.MESH


def greet(peers):
    barrier = pltpu.get_barrier_semaphore()
    for peer in peers:
        pl.semaphore_signal(barrier, inc=1, device_id=peer, device_id_type=MESH)
    pl.semaphore_wait(barrier, len(peers))


def scatter_kernel(rows, value_ref, out_ref, pair_in, total, major_in, pair_send, pair_recv, major_send, major_recv):
    majors = rows // 2
    row = lax.axis_index("row")
    col = lax.axis_index("col")
    major, minor = row // 2, row % 2
    partner = (major * 2 + 1 - minor, col)

    def peer(offset):
        return (lax.rem(major + offset, majors) * 2 + minor, col)

    greet([partner] + [peer(offset) for offset in range(1, majors)])
    order = sorted(range(1, majors), key=lambda offset: -min(offset, majors - offset)) + [0]
    started = []
    pair_copies = {}
    for offset in order:
        target = lax.rem(major + offset, majors)
        copy = pltpu.make_async_remote_copy(
            src_ref=value_ref.at[target * 2 + 1 - minor],
            dst_ref=pair_in.at[offset],
            send_sem=pair_send.at[offset],
            recv_sem=pair_recv.at[offset],
            device_id=partner,
            device_id_type=MESH,
        )
        copy.start()
        pair_copies[offset] = copy
    for offset in order:
        target = lax.rem(major + offset, majors)
        pair_copies[offset].wait_recv()
        total[offset] = pair_in[offset] + value_ref[target * 2 + minor]
        if offset:
            copy = pltpu.make_async_remote_copy(
                src_ref=total.at[offset],
                dst_ref=major_in.at[offset - 1],
                send_sem=major_send.at[offset - 1],
                recv_sem=major_recv.at[offset - 1],
                device_id=peer(offset),
                device_id_type=MESH,
            )
            copy.start()
            started.append(copy)
    for copy in started:
        copy.wait_recv()
    result = total[0]
    for slot in range(majors - 1):
        result = result + major_in[slot]
    out_ref[...] = result
    for copy in started:
        copy.wait_send()
    for offset in order:
        pair_copies[offset].wait_send()


def scatter_rows(value, rows):
    chunk, width = value.shape[0] // rows, value.shape[1]
    majors = rows // 2
    dma = pltpu.SemaphoreType.DMA
    return pl.pallas_call(
        functools.partial(scatter_kernel, rows),
        out_shape=jax.ShapeDtypeStruct((chunk, width), jnp.float32),
        in_specs=[pl.BlockSpec(memory_space=pltpu.VMEM)],
        out_specs=pl.BlockSpec(memory_space=pltpu.VMEM),
        scratch_shapes=[
            pltpu.VMEM((majors, chunk, width), jnp.float32),
            pltpu.VMEM((majors, chunk, width), jnp.float32),
            pltpu.VMEM((majors - 1, chunk, width), jnp.float32),
            dma((majors,)),
            dma((majors,)),
            dma((majors - 1,)),
            dma((majors - 1,)),
        ],
        compiler_params=pltpu.CompilerParams(
            collective_id=0, has_side_effects=True, vmem_limit_bytes=40 * 2**20
        ),
    )(value.reshape(rows, chunk, width))


def sum_kernel(rows, cols, value_ref, out_ref, full, sum_a, sum_b, in_a, in_b, in_c, *sems):
    row = lax.axis_index("row")
    col = lax.axis_index("col")
    outer = cols // 2
    far, core = col // 2, col % 2
    half = outer * rows
    base_a = core * half
    base_b = base_a + far * rows
    base_c = base_b + row

    def pair_peer(offset):
        return (row, far * 2 + 1 - core)

    def far_peer(offset):
        return (row, lax.rem(far + offset, outer) * 2 + core)

    def row_peer(offset):
        return (lax.rem(row + offset, rows), col)

    greet(
        [pair_peer(1)]
        + [far_peer(offset) for offset in range(1, outer)]
        + [row_peer(offset) for offset in range(1, rows)]
    )

    def exchange(count, peer, source, landing, stage):
        copies = []
        for offset in range(1, count):
            copy = pltpu.make_async_remote_copy(
                src_ref=source(offset),
                dst_ref=landing(offset),
                send_sem=sems[2 * stage].at[offset - 1],
                recv_sem=sems[2 * stage + 1].at[offset - 1],
                device_id=peer(offset),
                device_id_type=MESH,
            )
            copy.start()
            copies.append(copy)
        for copy in copies:
            copy.wait_recv()
        return copies

    pending = []
    pending += exchange(
        2, pair_peer, lambda k: value_ref.at[pl.ds((1 - core) * half, half)], lambda k: in_a.at[k - 1], 0
    )
    sum_a[...] = value_ref[pl.ds(base_a, half)] + in_a[0]
    pending += exchange(
        outer, far_peer, lambda k: sum_a.at[pl.ds(lax.rem(far + k, outer) * rows, rows)], lambda k: in_b.at[k - 1], 1
    )
    total = sum_a[pl.ds(far * rows, rows)]
    for slot in range(outer - 1):
        total = total + in_b[slot]
    sum_b[...] = total
    pending += exchange(
        rows, row_peer, lambda k: sum_b.at[lax.rem(row + k, rows)], lambda k: in_c.at[k - 1], 2
    )
    total = sum_b[row]
    for slot in range(rows - 1):
        total = total + in_c[slot]
    full[base_c] = total
    pending += exchange(rows, row_peer, lambda k: full.at[base_c], lambda k: full.at[base_c], 3)
    pending += exchange(
        outer, far_peer, lambda k: full.at[pl.ds(base_b, rows)], lambda k: full.at[pl.ds(base_b, rows)], 4
    )
    pending += exchange(
        2, pair_peer, lambda k: full.at[pl.ds(base_a, half)], lambda k: full.at[pl.ds(base_a, half)], 5
    )
    out_ref[...] = full[...]
    for copy in pending:
        copy.wait_send()


def sum_everywhere(value, rows, cols):
    devices = rows * cols
    lanes = value.shape[1]
    depth = value.shape[0] // devices
    outer = cols // 2
    dma = pltpu.SemaphoreType.DMA
    vmem = lambda *lead: pltpu.VMEM(lead + (depth, lanes), jnp.float32)
    total = pl.pallas_call(
        functools.partial(sum_kernel, rows, cols),
        out_shape=jax.ShapeDtypeStruct((devices, depth, lanes), jnp.float32),
        in_specs=[pl.BlockSpec(memory_space=pltpu.VMEM)],
        out_specs=pl.BlockSpec(memory_space=pltpu.VMEM),
        scratch_shapes=[
            vmem(devices),
            vmem(devices // 2),
            vmem(rows),
            vmem(1, devices // 2),
            vmem(outer - 1, rows),
            vmem(rows - 1),
        ]
        + [dma((count - 1,)) for count in (2, outer, rows, rows, outer, 2) for _ in range(2)],
        compiler_params=pltpu.CompilerParams(
            collective_id=1, has_side_effects=True, vmem_limit_bytes=24 * 2**20
        ),
        cost_estimate=pl.CostEstimate(flops=0, bytes_accessed=100 * value.size * 4, transcendentals=0),
    )(value.reshape(devices, depth, lanes))
    return total.reshape(value.shape)


def deliver(values, tile_owner, col_count):
    tile_count = tile_owner.shape[0]
    tile_rows = values.shape[0] // tile_count
    all_tiles = values.reshape(tile_count, tile_rows, values.shape[1])
    owner_col = tile_owner[:, 0]
    col_ids = jnp.arange(col_count, dtype=jnp.int32)
    onehot = (owner_col[:, None] == col_ids[None, :]).astype(jnp.int32)
    tile_rank = jnp.sum((jnp.cumsum(onehot, axis=0) - onehot) * onehot, axis=1)
    slot_index = jnp.arange(CAP, dtype=jnp.int32)
    select = (
        (owner_col[None, None, :] == col_ids[:, None, None])
        & (tile_rank[None, None, :] == slot_index[None, :, None])
    ).astype(jnp.float32)
    outgoing = jnp.einsum("cks,srb->ckrb", select, all_tiles, precision=lax.Precision.HIGHEST)
    incoming = lax.all_to_all(outgoing, "col", split_axis=0, concat_axis=0, tiled=True)
    return incoming.reshape(col_count * CAP, tile_rows, values.shape[1])


ROWS, COLS, CHIPS = 8, 4, 16
CHUNKS = 4
LANES = 128


def fits_fused(matrix, panel, struct_one, struct_two, tile_owner, rows, cols):
    span, width = panel.shape
    return (
        (rows, cols) == (ROWS, COLS)
        and span % LANES == 0
        and width == 2 * LANES
        and matrix.shape == (cols * span, rows * span)
        and struct_one.shape[0] % LANES == 0
        and struct_two.shape[0] % LANES == 0
        and span % (8 * tile_owner.shape[0]) == 0
    )


def exact(left, right, contract):
    return lax.dot_general(
        left, right, (contract, ((), ())), precision=lax.Precision.HIGHEST, preferred_element_type=jnp.float32
    )


def fused_kernel(
    matrix, panel_one, panel_two, struct_one_in, struct_two_in, lower_one_in, above_in, lower_two_in, owner,
    inverse_one_out, diag_one_out, cross_two_out, diag_two_out, delivered,
    inverse_one, diag_one, cross_two, diag_two, tiles_here,
    struct_one, struct_two, lower_one, above, lower_two, window, high, low, own, land, left, other, mine, pair_in, major_in, masks, turned, resident, product,
    inv_one_t, part_two_t, panel_two_t, correction, packed, fold_in, fold, part_in, side, wide_sum, straight, full, outgoing,
    out_sem, small_sem, fetch_sem, own_sem, turn_sem, move_sem, near_gather, far_gather, relay_gather, pair_sem, major_sem, sum_sem, line_sem,
    direct_send, direct_recv, hand_send, hand_recv, tile_sem,
):
    row = lax.axis_index("row")
    col = lax.axis_index("col")
    z, y = row // 2, row % 2
    x, core = col // 2, col % 2
    upper, lower = z // 2, z % 2
    chip = (z * 2 + y) * 2 + x
    depth, total_columns = matrix.shape
    span, width = own.shape[1:]
    chunk = left.shape[1] // 2
    per_panel = width // chunk

    def device(z_at, y_at, x_at, core_at):
        return (z_at * 2 + y_at, x_at * 2 + core_at)

    partner = device(z, y, x, 1 - core)
    across = device(z, y, 1 - x, core)
    beside = device(z, 1 - y, x, core)
    near = device(upper * 2 + 1 - lower, y, x, core)
    inner = device(3 - z, y, x, core)
    ends = upper == lower
    middle = upper != lower

    def remote(source, target, sems, at, peer):
        return pltpu.make_async_remote_copy(
            src_ref=source,
            dst_ref=target,
            send_sem=sems.at[(0,) + at],
            recv_sem=sems.at[(1,) + at],
            device_id=peer,
            device_id_type=MESH,
        )

    own_copies = [
        pltpu.make_async_copy(panel, own.at[at], own_sem.at[at]) for at, panel in enumerate((panel_one, panel_two))
    ]
    for copy in own_copies:
        copy.start()

    def fetch(step, which):
        rank = jnp.where(ends, step, jnp.where(step == 0, 0, jnp.where(step == 3, 2, 5 - 2 * step)))
        target = jnp.where(upper == 0, 3 - rank, rank) * 2 + lax.rem(1 - y + which, 2)
        return pltpu.make_async_copy(
            matrix.at[:, pl.ds(pl.multiple_of(target * span, LANES), span)], window.at[which], fetch_sem.at[which]
        )

    small_pairs = (
        (struct_one_in, struct_one),
        (struct_two_in, struct_two),
        (lower_one_in, lower_one),
        (above_in, above),
        (lower_two_in, lower_two),
    )
    small_copies = [
        pltpu.make_async_copy(source, target, small_sem.at[at]) for at, (source, target) in enumerate(small_pairs)
    ]
    for copy in small_copies:
        copy.start()
    barrier = pltpu.get_barrier_semaphore()

    def greet_at(semaphore, peer):
        pl.semaphore_signal(semaphore, inc=1, device_id=peer, device_id_type=MESH)

    devices = ROWS * COLS
    for offset in range(1, devices):
        flat = lax.rem(row * COLS + col + offset, devices)
        greet_at(barrier, (flat // COLS, lax.rem(flat, COLS)))
    for which in range(2):
        fetch(0, which).start()
    pl.semaphore_wait(barrier, devices - 1)
    for copy in own_copies:
        copy.wait()

    def piece(at):
        return own.at[at // per_panel, :, pl.ds(at % per_panel * chunk, chunk)]

    def far_copy(at, source=None):
        return remote(land.at[0, at] if source is None else source, land.at[col, at], far_gather, (at,), across)

    def near_copy(at, source=None):
        return remote(land.at[0, at] if source is None else source, land.at[col, at], near_gather, (at,), partner)

    def relay_copy(at):
        slot = (1 - x) * 2 + core
        return remote(land.at[slot, at], land.at[slot, at], relay_gather, (at,), partner)

    turns = core != y
    direct = jnp.where(x == upper, 0, 1)
    relays_move = lower == x

    def move_copy(source, slot, panel, at, peer):
        return pltpu.make_async_remote_copy(
            src_ref=source.at[panel],
            dst_ref=resident.at[slot, panel],
            send_sem=move_sem.at[0, panel, at],
            recv_sem=move_sem.at[1, panel, slot],
            device_id=peer,
            device_id_type=MESH,
        )

    def climb(source, panel, at, from_y):
        peer = device(2 * from_y + x, y, x, lower)
        return move_copy(source, direct, panel, at, peer), (peer[0] == row) & (peer[1] == col)

    def start_climb(source, panel, at, from_y):
        copy, stays = climb(source, panel, at, from_y)
        kept = pltpu.make_async_copy(source.at[panel], resident.at[direct, panel], move_sem.at[1, panel, direct])
        pl.when(stays)(lambda: kept.start())
        pl.when(jnp.logical_not(stays))(lambda: copy.start())

    def end_climb(source, panel, at, from_y):
        copy, stays = climb(source, panel, at, from_y)
        pl.when(jnp.logical_not(stays))(lambda: copy.wait_send())

    turn = [remote(own.at[panel], turned.at[panel], turn_sem, (panel,), beside) for panel in range(2)]
    passed = [move_copy(resident.at[1], 0, panel, 2, across) for panel in range(2)]

    def climb_turned(panel):
        @pl.when(jnp.logical_not(turns))
        def _():
            turn[panel].wait_recv()
            start_climb(turned, panel, 1, 1 - y)

    def pass_on(panel):
        @pl.when(relays_move)
        def _():
            move_copy(own, 1, panel, 0, beside).wait_recv()
            passed[panel].start()

    for at in range(CHUNKS):
        far_copy(at, piece(at)).start()
        near_copy(at, piece(at)).start()
        if at == 0:
            @pl.when(turns)
            def _():
                for copy in turn:
                    copy.start()

            @pl.when(jnp.logical_not(turns))
            def _():
                for panel in range(2):
                    start_climb(own, panel, 0, y)

    for at in range(CHUNKS):
        land[col, at] = piece(at)[...]

    for copy in small_copies:
        copy.wait()
    blocks = span // LANES
    slots_of = COLS * blocks
    mask_rows = masks.shape[1]
    place_rows = lax.broadcasted_iota(jnp.int32, (mask_rows, LANES), 0)
    block_base = row * slots_of
    result_base = (col * ROWS + row) * blocks
    wanted = jnp.where(place_rows < slots_of, block_base + place_rows, result_base + place_rows - slots_of)
    lane_ids = lax.broadcasted_iota(jnp.int32, (LANES, LANES), 0)
    for at, struct in enumerate((struct_one, struct_two)):
        count = struct.shape[0]
        group = max(size for size in range(1, 17) if count % size == 0)
        counts = jnp.zeros((mask_rows, LANES), jnp.float32)
        for begin in range(0, count, group):
            highs, lows = [], []
            for entry in range(begin, begin + group):
                value = struct[pl.ds(entry, 1), :]
                highs.append(jnp.where(wanted == value // LANES, 1.0, 0.0))
                lows.append(jnp.where(lane_ids == value % LANES, 1.0, 0.0))
            counts = counts + lax.dot_general(
                jnp.concatenate(highs, axis=1).astype(jnp.bfloat16),
                jnp.concatenate(lows, axis=1).astype(jnp.bfloat16),
                (((1,), (1,)), ((), ())),
                preferred_element_type=jnp.float32,
            )
        masks[at] = jnp.where(counts > 0.5, 1.0, 0.0)
    diag_one[...] = exact(lower_one[...].T, lower_one[...], ((1,), (0,)))
    diag_two[...] = exact(lower_two[...].T, lower_two[...], ((1,), (0,)))

    def mask_of(panel, begin):
        return jnp.concatenate([masks[panel, pl.ds(begin + at, 1), :] for at in range(blocks)], axis=1)

    def prepare(at):
        near_copy(at).wait_recv()
        far_copy(at).wait_recv()
        relay_copy(at).start()
        relay_copy(at).wait_recv()
        for slot in range(COLS):
            value = land[slot, at].T * mask_of(at // per_panel, slot * blocks)
            upper_part = value.astype(jnp.bfloat16)
            columns = pl.ds(slot * span, span)
            left[at, pl.ds(0, chunk), columns] = upper_part
            left[at, pl.ds(chunk, chunk), columns] = (value - upper_part.astype(jnp.float32)).astype(jnp.bfloat16)

    def pair_copy(at, step):
        return remote(other.at[at, step], pair_in.at[at, step], pair_sem, (at, step), beside)

    def multiply(at, step, which):
        target = step * 2 + which
        both = jnp.dot(left[at], high[target], preferred_element_type=jnp.float32)
        rest = jnp.dot(left[at, pl.ds(0, chunk), :], low[target], preferred_element_type=jnp.float32)
        value = both[:chunk] + (both[chunk:] + rest)
        if which == 0:
            other[at, step] = value
            pair_copy(at, step).start()
        else:
            mine[at, step] = value

    def first_step(step, carry):
        for which in range(2):
            fetch(step, which).wait()
            target = step * 2 + which
            for begin in range(0, depth, 256):
                size = min(256, depth - begin)
                value = window[which, pl.ds(begin, size), :]
                upper_part = value.astype(jnp.bfloat16)
                high[target, pl.ds(begin, size), :] = upper_part
                low[target, pl.ds(begin, size), :] = (value - upper_part.astype(jnp.float32)).astype(jnp.bfloat16)

            @pl.when(step + 1 < 4)
            def _():
                fetch(step + 1, which).start()

            multiply(0, step, which)
        pl.when(step == 1)(lambda: climb_turned(1))
        return carry

    def later_steps(chunks, begin, end):
        def body(step, carry):
            for at in chunks:
                for which in range(2):
                    multiply(at, step, which)
            return carry

        lax.fori_loop(begin, end, body, 0)

    def major_copy(at, step):
        slot = jnp.where(ends, (0, 2, 3)[step], (1, 3, 4)[step])
        return pltpu.make_async_remote_copy(
            src_ref=mine.at[at, step],
            dst_ref=major_in.at[at, slot],
            send_sem=major_sem.at[0, at, step],
            recv_sem=major_sem.at[1, at, slot],
            device_id=near if step == 1 else (jnp.where(ends, near[0], inner[0]), col),
            device_id_type=MESH,
        )

    def arrived(at, slot):
        pltpu.make_async_copy(mine.at[at, 0], major_in.at[at, slot], major_sem.at[1, at, slot]).wait()
        return major_in[at, slot]

    def forward(at, step):
        pair_copy(at, step).wait_recv()
        mine[at, step] = mine[at, step] + pair_in[at, step]

        @pl.when(middle)
        def _():
            mine[at, step] = mine[at, step] + arrived(at, step)

        major_copy(at, step).start()

    def collect(at):
        pair_copy(at, 3).wait_recv()
        product[at] = (mine[at, 3] + pair_in[at, 3]) + arrived(at, 3)

        @pl.when(middle)
        def _():
            product[at] = product[at] + arrived(at, 4)

    half = width // 2
    plain, last = ((1,), (0,)), ((1,), (1,))
    def flipped(upper_at, lower_at, y_at, x_at):
        z_at = jnp.where(upper_at, 1 - upper, upper) * 2 + jnp.where(lower_at, 1 - lower, lower)
        return z_at, jnp.where(y_at, 1 - y, y), jnp.where(x_at, 1 - x, x)

    def bits_of(offset):
        return offset // 8, offset // 4 % 2, offset // 2 % 2, offset % 2

    far_chips = sorted(range(1, CHIPS), key=lambda offset: -sum(w * b for w, b in zip((2.2, 1, 1, 1), bits_of(offset))))

    side_here = lax.rem(x + y, 2)
    opposite = device(z, 1 - y, 1 - x, core)

    class LineTotal:
        share = 7 * half // 2
        wide = share // 2
        rows = wide // 4

        def __init__(self):
            self.base = core * self.share
            self.half_rows = pl.ds(self.base, self.share)
            self.wide_rows = pl.ds(self.base + side_here * self.wide, self.wide)
            self.mine_rows = pl.ds(self.base + side_here * self.wide + z * self.rows, self.rows)
            self.sent = []

        def launch(self, *copy):
            copy = remote(*copy)
            copy.start()
            self.sent.append(copy)
            return copy

        def begin(self, tiles):
            for at, tile in enumerate(tiles):
                packed[pl.ds(at * half, half), :] = tile
            theirs = pl.ds((1 - core) * self.share, self.share)
            self.first = self.launch(packed.at[theirs], fold_in, sum_sem, (0,), partner)

        def scatter(self):
            self.first.wait_recv()
            fold[...] = packed[self.half_rows, :] + fold_in[...]
            theirs = pl.ds((1 - side_here) * self.wide, self.wide)
            self.second = self.launch(fold.at[theirs], wide_sum.at[1], sum_sem, (3,), across)

        def line(self):
            for at, (upper_at, lower_at) in enumerate(((1, 1), (1, 0), (0, 1))):
                z_at = flipped(upper_at, lower_at, 0, 0)[0]
                yield at, z_at, device(z_at, y, x, core)

        def climb(self):
            self.second.wait_recv()
            wide_sum[0] = fold[pl.ds(side_here * self.wide, self.wide), :] + wide_sum[1]
            self.copies = [
                self.launch(wide_sum.at[0, pl.ds(z_at * self.rows, self.rows)], part_in.at[at], line_sem, (0, at), peer)
                for at, z_at, peer in self.line()
            ]

        def cross(self):
            for copy in self.copies:
                copy.wait_recv()
            side[0] = (wide_sum[0, pl.ds(z * self.rows, self.rows), :] + part_in[0]) + (part_in[1] + part_in[2])
            self.crossing = self.launch(side.at[0], side.at[1], sum_sem, (2,), opposite)

        def spread(self):
            self.crossing.wait_recv()
            full[self.mine_rows, :] = side[0] + side[1]
            target = full.at[self.mine_rows]
            self.copies = [self.launch(target, target, line_sem, (1, at), peer) for at, _, peer in self.line()]

        def widen(self):
            for copy in self.copies:
                copy.wait_recv()
            target = full.at[self.wide_rows]
            self.second = self.launch(target, target, sum_sem, (4,), across)

        def finish(self):
            self.second.wait_recv()
            target = full.at[self.half_rows]
            self.final = self.launch(target, target, sum_sem, (1,), partner)

        def tile(self, at):
            return full[pl.ds(at * half, half), :]

    owner_here = core == x

    class DirectTotal:
        def __init__(self, at, start, blocks):
            self.at, self.start, self.rows = at, start, blocks * half // CHIPS
            self.mine_rows = pl.ds(start + chip * self.rows, self.rows)

        def place(self, offset, core_at=None):
            z_at, y_at, x_at = flipped(*bits_of(offset))
            return (z_at * 2 + y_at) * 2 + x_at, device(z_at, y_at, x_at, x_at if core_at is None else core_at)

        def sending(self, offset):
            flat, peer = self.place(offset)
            return pltpu.make_async_remote_copy(
                src_ref=packed.at[pl.ds(self.start + flat * self.rows, self.rows)],
                dst_ref=straight.at[self.at, offset * 2 + core, pl.ds(0, self.rows)],
                send_sem=direct_send.at[self.at, offset],
                recv_sem=direct_recv.at[self.at, offset * 2 + core],
                device_id=peer,
                device_id_type=MESH,
            )

        def handing(self, offset, core_at):
            peer = partner if core_at is None else self.place(offset, core_at)[1]
            return pltpu.make_async_remote_copy(
                src_ref=full.at[self.mine_rows],
                dst_ref=full.at[self.mine_rows],
                send_sem=hand_send.at[self.at, offset * 2 + (core_at or 0)],
                recv_sem=hand_recv.at[self.at, offset],
                device_id=peer,
                device_id_type=MESH,
            )

        def hands(self):
            return [self.handing(offset, core_at) for offset in far_chips for core_at in range(2)] + [
                self.handing(0, None)
            ]

        def begin(self, tiles):
            for at, tile in enumerate(tiles):
                packed[pl.ds(self.start + at * half, half), :] = tile
            for offset in far_chips:
                self.sending(offset).start()
            pl.when(jnp.logical_not(owner_here))(lambda: self.sending(0).start())

        def spread(self):
            @pl.when(owner_here)
            def _():
                rows = pl.ds(0, self.rows)

                def landed(slot):
                    target = straight.at[self.at, slot, rows]
                    pltpu.make_async_copy(target, target, direct_recv.at[self.at, slot]).wait()
                    return straight[self.at, slot, rows, :]

                value = packed[self.mine_rows, :] + landed(1 - core)
                for slot in range(2, 2 * CHIPS):
                    value = value + landed(slot)
                full[self.mine_rows, :] = value
                for copy in self.hands():
                    copy.start()

        def finish(self):
            for offset in range(1, CHIPS):
                self.handing(offset, 0).wait_recv()
            pl.when(jnp.logical_not(owner_here))(lambda: self.handing(0, None).wait_recv())

        def drain(self):
            for offset in range(1, CHIPS):
                self.sending(offset).wait_send()
            pl.when(jnp.logical_not(owner_here))(lambda: self.sending(0).wait_send())

            @pl.when(owner_here)
            def _():
                for copy in self.hands():
                    copy.wait_send()

        def tile(self, at):
            return full[pl.ds(self.start + at * half, half), :]

    def quarters(value, places):
        return [value[i * half : (i + 1) * half, j * half : (j + 1) * half] for i, j in places]

    upper_places = ((0, 0), (0, 1), (1, 1))
    every_place = ((0, 0), (0, 1), (1, 0), (1, 1))
    tile_count = owner.shape[0]
    tile_rows = span // tile_count
    names = [owner[at] for at in range(tile_count)]
    ranks = [
        sum([jnp.where(names[before] == names[at], 1, 0) for before in range(at)], jnp.int32(0))
        for at in range(tile_count)
    ]
    tile_copies = []

    def send_tiles(part, values):
        columns = pl.ds(part * half, half)

        def slot_value(name, rank):
            value = jnp.zeros((tile_rows, half), jnp.float32)
            for at in range(tile_count):
                chosen = (names[at] == name) & (ranks[at] == rank)
                value = jnp.where(chosen, values[at * tile_rows : (at + 1) * tile_rows], value)
            return value

        for offset in range(1, COLS):
            name = lax.rem(col + offset, COLS)
            for rank in range(CAP):
                outgoing[offset - 1, rank, :, columns] = slot_value(name, rank)
            copy = remote(
                outgoing.at[offset - 1, :, :, columns],
                delivered.at[pl.ds(col * CAP, CAP), :, columns],
                tile_sem,
                (part, offset - 1),
                (row, name),
            )
            copy.start()
            tile_copies.append(copy)
        for rank in range(CAP):
            tiles_here[rank, :, columns] = slot_value(col, rank)

    first_total = LineTotal()
    middle_total, second_total = DirectTotal(0, 7 * half, 2), DirectTotal(1, 9 * half, 1)

    prepare(0)
    climb_turned(0)
    lax.fori_loop(0, 4, first_step, 0)
    prepare(1)
    def only(where, *steps):
        @pl.when(where)
        def _():
            for at, step in steps:
                forward(at, step)

    only(ends, (0, 0))
    later_steps((1,), 0, 4)
    only(middle, (0, 0))
    only(ends, (0, 1))
    prepare(2)
    prepare(3)
    only(ends, (0, 2))
    later_steps((2, 3), 0, 2)
    only(middle, (0, 1), (0, 2))
    only(ends, (1, 0))
    pass_on(0)
    pass_on(1)
    only(ends, (1, 1))
    collect(0)
    only(middle, (1, 0), (1, 1))
    forward(1, 2)
    only(ends, (2, 0))
    collect(1)
    only(ends, (3, 0))
    only(middle, (2, 0))
    one_row = mask_of(0, slots_of)
    two_row = mask_of(1, slots_of)
    inv_one_t[...] = -(jnp.concatenate([product[at] for at in range(per_panel)], axis=0) * one_row)
    for copy in passed:
        copy.wait_recv()
    panel_two_t[...] = resident[0, 1].T
    gram_one = exact(resident[0, 0].T, inv_one_t[...], last)
    cross_sum = exact(inv_one_t[...] * two_row, panel_two_t[...], last)
    first_total.begin(quarters(gram_one, upper_places) + quarters(cross_sum, every_place))
    above_t = above[...].T
    correction[...] = exact(above_t, inv_one_t[...], plain) * two_row
    inverse_one[...] = inv_one_t[...].T
    outs = [pltpu.make_async_copy(inverse_one, inverse_one_out, out_sem.at[0])]
    outs[0].start()
    first_total.scatter()
    later_steps((2, 3), 2, 3)
    only(ends, (2, 1))
    only(middle, (3, 0), (2, 1))
    later_steps((2, 3), 3, 4)
    first_total.climb()
    forward(3, 1)
    forward(2, 2)
    first_total.cross()
    forward(3, 2)
    collect(2)
    first_total.spread()
    low_half, high_half = pl.ds(0, half), pl.ds(half, half)
    part_two_t[low_half, :] = -(product[2] * two_row)
    gram_left = exact(panel_two_t[...], part_two_t[low_half, :], last)
    middle_total.begin([gram_left[:half], gram_left[half:]])
    send_tiles(0, (part_two_t[low_half, :] - correction[low_half, :]).T)
    collect(3)
    part_two_t[high_half, :] = -(product[3] * two_row)
    second_total.begin([exact(panel_two_t[high_half, :], part_two_t[high_half, :], last)])
    late = (part_two_t[high_half, :] - correction[high_half, :]).T
    middle_total.spread()
    first_total.widen()
    send_tiles(1, late)
    second_total.spread()
    first_total.finish()

    here = pltpu.make_async_copy(tiles_here, delivered.at[pl.ds(col * CAP, CAP)], out_sem.at[4])
    here.start()
    outs.append(here)

    def put(at, source, target):
        copy = pltpu.make_async_copy(source, target, out_sem.at[at])
        copy.start()
        outs.append(copy)

    def square(first, second, third, fourth):
        return jnp.concatenate(
            [jnp.concatenate([first, second], axis=1), jnp.concatenate([third, fourth], axis=1)], axis=0
        )

    first_total.final.wait_recv()
    tile = first_total.tile
    diag_one_value = diag_one[...] - square(tile(0), tile(1), tile(1).T, tile(2))
    cross_total = square(tile(3), tile(4), tile(5), tile(6))
    diag_one[...] = diag_one_value
    put(1, diag_one, diag_one_out)
    cross_value = -(cross_total + exact(diag_one_value, above[...], plain))
    cross_two[...] = cross_value
    put(2, cross_two, cross_two_out)
    diag_two[...] = diag_two[...] + (exact(cross_total.T, above[...], plain) - exact(above_t, cross_value, plain))
    middle_total.finish()
    tile = middle_total.tile
    second_total.finish()
    diag_two[...] = diag_two[...] - square(tile(0), tile(1).T, tile(1), second_total.tile(0))
    put(3, diag_two, diag_two_out)

    for copy in tile_copies:
        copy.wait_recv()

    for panel in range(2):

        @pl.when(turns)
        def _():
            turn[panel].wait_send()

        @pl.when(jnp.logical_not(turns))
        def _():
            end_climb(own, panel, 0, y)
            end_climb(turned, panel, 1, 1 - y)

        pl.when(relays_move)(lambda: passed[panel].wait_send())

    for copy in outs:
        copy.wait()
    middle_total.drain()
    second_total.drain()
    for copy in first_total.sent + tile_copies:
        copy.wait_send()
    for at in range(CHUNKS):
        for copy in (near_copy(at), far_copy(at), relay_copy(at)):
            copy.wait_send()
        for step in range(4):
            pair_copy(at, step).wait_send()
        for step in range(3):
            major_copy(at, step).wait_send()


def place_kernel(count, *refs):
    sources, targets, buffers, sems = refs[:count], refs[count : 2 * count], refs[2 * count : -1], refs[-1]
    loads = [pltpu.make_async_copy(sources[at], buffers[at], sems.at[0, at]) for at in range(count)]
    stores = [pltpu.make_async_copy(buffers[at], targets[at], sems.at[1, at]) for at in range(count)]
    for copy in loads:
        copy.start()
    for load, store in zip(loads, stores):
        load.wait()
        store.start()
    for copy in stores:
        copy.wait()


def fused(matrix, panel_one, panel_two, struct_one, struct_two, lower_one, above, lower_two, tile_owner):
    depth, _ = matrix.shape
    span, width = panel_one.shape
    chunk = 2 * width // CHUNKS
    tile_count = tile_owner.shape[0]
    share = 7 * (width // 2) // 2
    mask_rows = -(-(COLS + 1) * (span // LANES) // 8) * 8
    dma = pltpu.SemaphoreType.DMA
    vmem = lambda *shape: pltpu.VMEM(shape, jnp.float32)
    half_vmem = lambda *shape: pltpu.VMEM(shape, jnp.bfloat16)
    anywhere = pl.BlockSpec(memory_space=pl.ANY)
    scalars = pl.BlockSpec(memory_space=pltpu.SMEM)
    shape = lambda *dims: jax.ShapeDtypeStruct(dims, jnp.float32)
    results = pl.pallas_call(
        fused_kernel,
        out_shape=[
            shape(span, width),
            shape(width, width),
            shape(width, width),
            shape(width, width),
            shape(COLS * CAP, span // tile_count, width),
        ],
        in_specs=[anywhere] * 8 + [scalars],
        out_specs=[anywhere] * 5,
        scratch_shapes=[
            vmem(span, width),
            vmem(width, width),
            vmem(width, width),
            vmem(width, width),
            vmem(CAP, span // tile_count, width),
            pltpu.VMEM((struct_one.shape[0] // LANES, LANES), jnp.int32),
            pltpu.VMEM((struct_two.shape[0] // LANES, LANES), jnp.int32),
            vmem(width, width),
            vmem(width, width),
            vmem(width, width),
            vmem(2, depth, span),
            half_vmem(8, depth, span),
            half_vmem(8, depth, span),
            vmem(2, span, width),
            vmem(COLS, CHUNKS, span, chunk),
            half_vmem(CHUNKS, 2 * chunk, depth),
            vmem(CHUNKS, 4, chunk, span),
            vmem(CHUNKS, 4, chunk, span),
            vmem(CHUNKS, 4, chunk, span),
            vmem(CHUNKS, 5, chunk, span),
            vmem(2, mask_rows, LANES),
            vmem(2, span, width),
            vmem(2, 2, span, width),
            vmem(CHUNKS, chunk, span),
            vmem(width, span),
            vmem(width, span),
            vmem(width, span),
            vmem(width, span),
            vmem(10 * (width // 2), LANES),
            vmem(share, LANES),
            vmem(share, LANES),
            vmem(3, share // 8, LANES),
            vmem(2, share // 8, LANES),
            vmem(2, share // 2, LANES),
            vmem(2, 2 * CHIPS, width // CHIPS, LANES),
            vmem(10 * (width // 2), LANES),
            vmem(COLS - 1, CAP, span // tile_count, width),
            dma((5,)),
            dma((5,)),
            dma((2,)),
            dma((2,)),
            dma((2, 2)),
            dma((2, 2, 3)),
            dma((2, CHUNKS)),
            dma((2, CHUNKS)),
            dma((2, CHUNKS)),
            dma((2, CHUNKS, 4)),
            dma((2, CHUNKS, 5)),
            dma((2, 5)),
            dma((2, 2, 3)),
            dma((2, CHIPS)),
            dma((2, 2 * CHIPS)),
            dma((2, 2 * CHIPS)),
            dma((2, CHIPS)),
            dma((2, 2, COLS - 1)),
        ],
        compiler_params=pltpu.CompilerParams(
            collective_id=3, has_side_effects=True, vmem_limit_bytes=58 * 2**20
        ),
        cost_estimate=pl.CostEstimate(
            flops=12 * matrix.size * width, bytes_accessed=4 * matrix.size, transcendentals=0
        ),
    )(
        matrix,
        panel_one,
        panel_two,
        struct_one.reshape(-1, LANES),
        struct_two.reshape(-1, LANES),
        lower_one,
        above,
        lower_two,
        tile_owner.reshape(-1),
    )
    return tuple(pl.pallas_call(
        functools.partial(place_kernel, len(results)),
        out_shape=[shape(*result.shape) for result in results],
        in_specs=[anywhere] * len(results),
        out_specs=[anywhere] * len(results),
        scratch_shapes=[vmem(*result.shape) for result in results] + [dma((2, len(results)))],
        compiler_params=pltpu.CompilerParams(vmem_limit_bytes=60 * 2**20),
    )(*results))


def local(
    ancestor_inverse,
    panel_one,
    struct_one,
    lower_one,
    panel_two,
    struct_two,
    panel_above,
    lower_two,
    tile_owner,
):
    row_count = lax.axis_size("row")
    col_count = lax.axis_size("col")
    row_index = lax.axis_index("row")
    col_index = lax.axis_index("col")
    local_rows = panel_one.shape[0]
    if fits_fused(ancestor_inverse, panel_one, struct_one, struct_two, tile_owner, row_count, col_count):
        return fused(
            ancestor_inverse,
            panel_one,
            panel_two,
            struct_one,
            struct_two,
            lower_one,
            panel_above,
            lower_two,
            tile_owner,
        )
    order = local_rows * row_count * col_count
    width = panel_one.shape[1]
    mask_one = row_mask(struct_one, order)
    mask_two = row_mask(struct_two, order)
    panel_start = (row_index * col_count + col_index) * local_rows
    result_start = (col_index * row_count + row_index) * local_rows
    local_one = panel_one * lax.dynamic_slice_in_dim(mask_one, panel_start, local_rows)[:, None]
    local_two = panel_two * lax.dynamic_slice_in_dim(mask_two, panel_start, local_rows)[:, None]
    result_mask_one = lax.dynamic_slice_in_dim(mask_one, result_start, local_rows)[:, None]
    result_mask_two = lax.dynamic_slice_in_dim(mask_two, result_start, local_rows)[:, None]

    both = jnp.concatenate([local_one, local_two], axis=1)
    gathered = lax.all_gather(both, "col", axis=0, tiled=True)
    product = scatter_rows(contract_rows(ancestor_inverse, gathered, lax.Precision.HIGH), row_count)
    moves = [(f, (f % row_count) * col_count + f // row_count) for f in range(row_count * col_count)]
    resident = lax.ppermute(both, ("row", "col"), moves)
    resident_one = resident[:, :width]
    resident_two = resident[:, width:]
    inverse_one = -product[:, :width] * result_mask_one
    inverse_two = -(product[:, width:] + matmul(inverse_one, panel_above)) * result_mask_two
    grams = (
        contract_rows(resident_one, inverse_one),
        contract_rows(inverse_one, resident_two),
        contract_rows(resident_two, inverse_two),
    )
    lanes = 128
    packed = jnp.concatenate(
        [gram[:, at : at + lanes] for gram in grams for at in range(0, width, lanes)], axis=0
    )
    sums = sum_everywhere(packed, row_count, col_count).reshape(len(grams), width // lanes, width, lanes)
    gram_one, cross_sum, gram_two = (
        jnp.concatenate([sums[at, block] for block in range(width // lanes)], axis=1) for at in range(len(grams))
    )
    diag_one = matmul(lower_one.T, lower_one) - gram_one
    cross_two = -(cross_sum + matmul(diag_one, panel_above))
    diag_two = matmul(lower_two.T, lower_two) - gram_two - matmul(panel_above.T, cross_two)
    delivered = deliver(inverse_two, tile_owner, col_count)
    return (inverse_one, diag_one, cross_two, diag_two, delivered)


def solution(mesh):
    return jax.shard_map(
        local,
        mesh=mesh,
        in_specs=(
            P("row", "col"),
            P(("row", "col"), None),
            P(),
            P(),
            P(("row", "col"), None),
            P(),
            P(),
            P(),
            P(("col", "row"), None),
        ),
        out_specs=(P(("col", "row"), None), P(), P(), P(), P(("row", "col"), None, None)),
        check_vma=False,
    )
```

```python
import functools

import jax
import jax.numpy as jnp
from jax import lax
from jax.experimental import pallas as pl
from jax.experimental.pallas import tpu as pltpu
from jax.sharding import PartitionSpec as P

CAP = 2


def matmul(left, right):
    return jnp.dot(left, right, precision=lax.Precision.HIGHEST, preferred_element_type=jnp.float32)


def contract_rows(left, right, precision=lax.Precision.HIGHEST):
    return lax.dot_general(
        left,
        right,
        (((0,), (0,)), ((), ())),
        precision=precision,
        preferred_element_type=jnp.float32,
    )


def row_mask(struct, count):
    lanes = 128
    high = struct // lanes
    low = struct % lanes
    high_hot = (jnp.arange(count // lanes, dtype=jnp.int32)[:, None] == high[None, :]).astype(jnp.bfloat16)
    low_hot = (jnp.arange(lanes, dtype=jnp.int32)[:, None] == low[None, :]).astype(jnp.bfloat16)
    counts = lax.dot_general(high_hot, low_hot, (((1,), (1,)), ((), ())), preferred_element_type=jnp.float32)
    return (counts > 0.5).astype(jnp.float32).reshape(count)


MESH = pl.DeviceIdType.MESH


def greet(peers):
    barrier = pltpu.get_barrier_semaphore()
    for peer in peers:
        pl.semaphore_signal(barrier, inc=1, device_id=peer, device_id_type=MESH)
    pl.semaphore_wait(barrier, len(peers))


def scatter_kernel(rows, value_ref, out_ref, pair_in, total, major_in, pair_send, pair_recv, major_send, major_recv):
    majors = rows // 2
    row = lax.axis_index("row")
    col = lax.axis_index("col")
    major, minor = row // 2, row % 2
    partner = (major * 2 + 1 - minor, col)

    def peer(offset):
        return (lax.rem(major + offset, majors) * 2 + minor, col)

    greet([partner] + [peer(offset) for offset in range(1, majors)])
    order = sorted(range(1, majors), key=lambda offset: -min(offset, majors - offset)) + [0]
    started = []
    pair_copies = {}
    for offset in order:
        target = lax.rem(major + offset, majors)
        copy = pltpu.make_async_remote_copy(
            src_ref=value_ref.at[target * 2 + 1 - minor],
            dst_ref=pair_in.at[offset],
            send_sem=pair_send.at[offset],
            recv_sem=pair_recv.at[offset],
            device_id=partner,
            device_id_type=MESH,
        )
        copy.start()
        pair_copies[offset] = copy
    for offset in order:
        target = lax.rem(major + offset, majors)
        pair_copies[offset].wait_recv()
        total[offset] = pair_in[offset] + value_ref[target * 2 + minor]
        if offset:
            copy = pltpu.make_async_remote_copy(
                src_ref=total.at[offset],
                dst_ref=major_in.at[offset - 1],
                send_sem=major_send.at[offset - 1],
                recv_sem=major_recv.at[offset - 1],
                device_id=peer(offset),
                device_id_type=MESH,
            )
            copy.start()
            started.append(copy)
    for copy in started:
        copy.wait_recv()
    result = total[0]
    for slot in range(majors - 1):
        result = result + major_in[slot]
    out_ref[...] = result
    for copy in started:
        copy.wait_send()
    for offset in order:
        pair_copies[offset].wait_send()


def scatter_rows(value, rows):
    chunk, width = value.shape[0] // rows, value.shape[1]
    majors = rows // 2
    dma = pltpu.SemaphoreType.DMA
    return pl.pallas_call(
        functools.partial(scatter_kernel, rows),
        out_shape=jax.ShapeDtypeStruct((chunk, width), jnp.float32),
        in_specs=[pl.BlockSpec(memory_space=pltpu.VMEM)],
        out_specs=pl.BlockSpec(memory_space=pltpu.VMEM),
        scratch_shapes=[
            pltpu.VMEM((majors, chunk, width), jnp.float32),
            pltpu.VMEM((majors, chunk, width), jnp.float32),
            pltpu.VMEM((majors - 1, chunk, width), jnp.float32),
            dma((majors,)),
            dma((majors,)),
            dma((majors - 1,)),
            dma((majors - 1,)),
        ],
        compiler_params=pltpu.CompilerParams(
            collective_id=0, has_side_effects=True, vmem_limit_bytes=40 * 2**20
        ),
    )(value.reshape(rows, chunk, width))


def sum_kernel(rows, cols, value_ref, out_ref, full, sum_a, sum_b, in_a, in_b, in_c, *sems):
    row = lax.axis_index("row")
    col = lax.axis_index("col")
    outer = cols // 2
    far, core = col // 2, col % 2
    half = outer * rows
    base_a = core * half
    base_b = base_a + far * rows
    base_c = base_b + row

    def pair_peer(offset):
        return (row, far * 2 + 1 - core)

    def far_peer(offset):
        return (row, lax.rem(far + offset, outer) * 2 + core)

    def row_peer(offset):
        return (lax.rem(row + offset, rows), col)

    greet(
        [pair_peer(1)]
        + [far_peer(offset) for offset in range(1, outer)]
        + [row_peer(offset) for offset in range(1, rows)]
    )

    def exchange(count, peer, source, landing, stage):
        copies = []
        for offset in range(1, count):
            copy = pltpu.make_async_remote_copy(
                src_ref=source(offset),
                dst_ref=landing(offset),
                send_sem=sems[2 * stage].at[offset - 1],
                recv_sem=sems[2 * stage + 1].at[offset - 1],
                device_id=peer(offset),
                device_id_type=MESH,
            )
            copy.start()
            copies.append(copy)
        for copy in copies:
            copy.wait_recv()
        return copies

    pending = []
    pending += exchange(
        2, pair_peer, lambda k: value_ref.at[pl.ds((1 - core) * half, half)], lambda k: in_a.at[k - 1], 0
    )
    sum_a[...] = value_ref[pl.ds(base_a, half)] + in_a[0]
    pending += exchange(
        outer, far_peer, lambda k: sum_a.at[pl.ds(lax.rem(far + k, outer) * rows, rows)], lambda k: in_b.at[k - 1], 1
    )
    total = sum_a[pl.ds(far * rows, rows)]
    for slot in range(outer - 1):
        total = total + in_b[slot]
    sum_b[...] = total
    pending += exchange(
        rows, row_peer, lambda k: sum_b.at[lax.rem(row + k, rows)], lambda k: in_c.at[k - 1], 2
    )
    total = sum_b[row]
    for slot in range(rows - 1):
        total = total + in_c[slot]
    full[base_c] = total
    pending += exchange(rows, row_peer, lambda k: full.at[base_c], lambda k: full.at[base_c], 3)
    pending += exchange(
        outer, far_peer, lambda k: full.at[pl.ds(base_b, rows)], lambda k: full.at[pl.ds(base_b, rows)], 4
    )
    pending += exchange(
        2, pair_peer, lambda k: full.at[pl.ds(base_a, half)], lambda k: full.at[pl.ds(base_a, half)], 5
    )
    out_ref[...] = full[...]
    for copy in pending:
        copy.wait_send()


def sum_everywhere(value, rows, cols):
    devices = rows * cols
    lanes = value.shape[1]
    depth = value.shape[0] // devices
    outer = cols // 2
    dma = pltpu.SemaphoreType.DMA
    vmem = lambda *lead: pltpu.VMEM(lead + (depth, lanes), jnp.float32)
    total = pl.pallas_call(
        functools.partial(sum_kernel, rows, cols),
        out_shape=jax.ShapeDtypeStruct((devices, depth, lanes), jnp.float32),
        in_specs=[pl.BlockSpec(memory_space=pltpu.VMEM)],
        out_specs=pl.BlockSpec(memory_space=pltpu.VMEM),
        scratch_shapes=[
            vmem(devices),
            vmem(devices // 2),
            vmem(rows),
            vmem(1, devices // 2),
            vmem(outer - 1, rows),
            vmem(rows - 1),
        ]
        + [dma((count - 1,)) for count in (2, outer, rows, rows, outer, 2) for _ in range(2)],
        compiler_params=pltpu.CompilerParams(
            collective_id=1, has_side_effects=True, vmem_limit_bytes=24 * 2**20
        ),
        cost_estimate=pl.CostEstimate(flops=0, bytes_accessed=100 * value.size * 4, transcendentals=0),
    )(value.reshape(devices, depth, lanes))
    return total.reshape(value.shape)


def deliver(values, tile_owner, col_count):
    tile_count = tile_owner.shape[0]
    tile_rows = values.shape[0] // tile_count
    all_tiles = values.reshape(tile_count, tile_rows, values.shape[1])
    owner_col = tile_owner[:, 0]
    col_ids = jnp.arange(col_count, dtype=jnp.int32)
    onehot = (owner_col[:, None] == col_ids[None, :]).astype(jnp.int32)
    tile_rank = jnp.sum((jnp.cumsum(onehot, axis=0) - onehot) * onehot, axis=1)
    slot_index = jnp.arange(CAP, dtype=jnp.int32)
    select = (
        (owner_col[None, None, :] == col_ids[:, None, None])
        & (tile_rank[None, None, :] == slot_index[None, :, None])
    ).astype(jnp.float32)
    outgoing = jnp.einsum("cks,srb->ckrb", select, all_tiles, precision=lax.Precision.HIGHEST)
    incoming = lax.all_to_all(outgoing, "col", split_axis=0, concat_axis=0, tiled=True)
    return incoming.reshape(col_count * CAP, tile_rows, values.shape[1])


ROWS, COLS, CHIPS = 8, 4, 16
CHUNKS = 4
LANES = 128


def fits_fused(matrix, panel, struct_one, struct_two, tile_owner, rows, cols):
    span, width = panel.shape
    return (
        (rows, cols) == (ROWS, COLS)
        and span % LANES == 0
        and width == 2 * LANES
        and matrix.shape == (cols * span, rows * span)
        and struct_one.shape[0] % LANES == 0
        and struct_two.shape[0] % LANES == 0
        and span % (8 * tile_owner.shape[0]) == 0
    )


def exact(left, right, contract):
    return lax.dot_general(
        left, right, (contract, ((), ())), precision=lax.Precision.HIGHEST, preferred_element_type=jnp.float32
    )


def fused_kernel(
    matrix, panel_one, panel_two, struct_one_in, struct_two_in, lower_one_in, above_in, lower_two_in, owner,
    inverse_one_out, diag_one_out, cross_two_out, diag_two_out, delivered,
    inverse_one, diag_one, cross_two, diag_two, tiles_here,
    struct_one, struct_two, lower_one, above, lower_two, window, high, low, own, land, left, other, mine, pair_in, major_in, masks, turned, resident, product,
    inv_one_t, part_two_t, panel_two_t, correction, packed, fold_in, fold, part_in, side, wide_sum, straight, full, outgoing,
    out_sem, small_sem, fetch_sem, own_sem, turn_sem, move_sem, flow_sem, gather_sem, pair_sem, major_sem, sum_sem, line_sem,
    direct_send, direct_recv, hand_send, hand_recv, tile_sem,
):
    row = lax.axis_index("row")
    col = lax.axis_index("col")
    z, y = row // 2, row % 2
    x, core = col // 2, col % 2
    upper, lower = z // 2, z % 2
    chip = (z * 2 + y) * 2 + x
    depth, total_columns = matrix.shape
    span, width = own.shape[1:]
    chunk = left.shape[1] // 2
    per_panel = width // chunk

    def device(z_at, y_at, x_at, core_at):
        return (z_at * 2 + y_at, x_at * 2 + core_at)

    partner = device(z, y, x, 1 - core)
    across = device(z, y, 1 - x, core)
    beside = device(z, 1 - y, x, core)
    near = device(upper * 2 + 1 - lower, y, x, core)
    inner = device(3 - z, y, x, core)
    ends = upper == lower
    middle = upper != lower

    def remote(source, target, sems, at, peer):
        return pltpu.make_async_remote_copy(
            src_ref=source,
            dst_ref=target,
            send_sem=sems.at[(0,) + at],
            recv_sem=sems.at[(1,) + at],
            device_id=peer,
            device_id_type=MESH,
        )

    own_copies = [
        pltpu.make_async_copy(panel, own.at[at], own_sem.at[at]) for at, panel in enumerate((panel_one, panel_two))
    ]
    for copy in own_copies:
        copy.start()

    def fetch(step, which):
        rank = jnp.where(ends, step, jnp.where(step == 0, 0, jnp.where(step == 3, 2, 5 - 2 * step)))
        target = jnp.where(upper == 0, 3 - rank, rank) * 2 + lax.rem(1 - y + which, 2)
        return pltpu.make_async_copy(
            matrix.at[:, pl.ds(pl.multiple_of(target * span, LANES), span)], window.at[which], fetch_sem.at[which]
        )

    small_pairs = (
        (struct_one_in, struct_one),
        (struct_two_in, struct_two),
        (lower_one_in, lower_one),
        (above_in, above),
        (lower_two_in, lower_two),
    )
    small_copies = [
        pltpu.make_async_copy(source, target, small_sem.at[at]) for at, (source, target) in enumerate(small_pairs)
    ]
    for copy in small_copies:
        copy.start()
    barrier = pltpu.get_barrier_semaphore()

    def greet_at(semaphore, peer):
        pl.semaphore_signal(semaphore, inc=1, device_id=peer, device_id_type=MESH)

    devices = ROWS * COLS
    for offset in range(1, devices):
        flat = lax.rem(row * COLS + col + offset, devices)
        greet_at(barrier, (flat // COLS, lax.rem(flat, COLS)))
    for which in range(2):
        fetch(0, which).start()
    pl.semaphore_wait(barrier, devices - 1)
    for copy in own_copies:
        copy.wait()

    def piece(at):
        return own.at[at // per_panel, :, pl.ds(at % per_panel * chunk, chunk)]

    def flow(kind, source, target, recv_sem, peer):
        return pltpu.make_async_remote_copy(
            src_ref=source,
            dst_ref=target,
            send_sem=flow_sem.at[kind],
            recv_sem=recv_sem,
            device_id=peer,
            device_id_type=MESH,
        )

    def take(like, semaphore):
        pltpu.make_async_copy(like, like, semaphore).wait()

    def far_copy(at, source=None):
        source = land.at[0, at] if source is None else source
        return flow(0, source, land.at[col, at], gather_sem.at[0, at], across)

    def near_copy(at, source=None):
        source = land.at[0, at] if source is None else source
        return flow(1, source, land.at[col, at], gather_sem.at[1, at], partner)

    def relay_copy(at):
        slot = (1 - x) * 2 + core
        return flow(2, land.at[slot, at], land.at[slot, at], gather_sem.at[2, at], partner)

    turns = core != y
    direct = jnp.where(x == upper, 0, 1)
    relays_move = lower == x

    def move_copy(source, slot, panel, at, peer):
        return pltpu.make_async_remote_copy(
            src_ref=source.at[panel],
            dst_ref=resident.at[slot, panel],
            send_sem=move_sem.at[0, panel, at],
            recv_sem=move_sem.at[1, panel, slot],
            device_id=peer,
            device_id_type=MESH,
        )

    def climb(source, panel, at, from_y):
        peer = device(2 * from_y + x, y, x, lower)
        return move_copy(source, direct, panel, at, peer), (peer[0] == row) & (peer[1] == col)

    def start_climb(source, panel, at, from_y):
        copy, stays = climb(source, panel, at, from_y)
        kept = pltpu.make_async_copy(source.at[panel], resident.at[direct, panel], move_sem.at[1, panel, direct])
        pl.when(stays)(lambda: kept.start())
        pl.when(jnp.logical_not(stays))(lambda: copy.start())

    def end_climb(source, panel, at, from_y):
        copy, stays = climb(source, panel, at, from_y)
        pl.when(jnp.logical_not(stays))(lambda: copy.wait_send())

    turn = [remote(own.at[panel], turned.at[panel], turn_sem, (panel,), beside) for panel in range(2)]
    passed = [move_copy(resident.at[1], 0, panel, 2, across) for panel in range(2)]

    def climb_turned(panel):
        @pl.when(jnp.logical_not(turns))
        def _():
            turn[panel].wait_recv()
            start_climb(turned, panel, 1, 1 - y)

    def pass_on(panel):
        @pl.when(relays_move)
        def _():
            move_copy(own, 1, panel, 0, beside).wait_recv()
            passed[panel].start()

    for at in range(CHUNKS):
        far_copy(at, piece(at)).start()
        near_copy(at, piece(at)).start()
        if at == 0:
            @pl.when(turns)
            def _():
                for copy in turn:
                    copy.start()

            @pl.when(jnp.logical_not(turns))
            def _():
                for panel in range(2):
                    start_climb(own, panel, 0, y)

    for at in range(CHUNKS):
        land[col, at] = piece(at)[...]

    for copy in small_copies:
        copy.wait()
    blocks = span // LANES
    slots_of = COLS * blocks
    mask_rows = masks.shape[1]
    place_rows = lax.broadcasted_iota(jnp.int32, (mask_rows, LANES), 0)
    block_base = row * slots_of
    result_base = (col * ROWS + row) * blocks
    wanted = jnp.where(place_rows < slots_of, block_base + place_rows, result_base + place_rows - slots_of)
    lane_ids = lax.broadcasted_iota(jnp.int32, (LANES, LANES), 0)
    for at, struct in enumerate((struct_one, struct_two)):
        count = struct.shape[0]
        group = max(size for size in range(1, 17) if count % size == 0)
        counts = jnp.zeros((mask_rows, LANES), jnp.float32)
        for begin in range(0, count, group):
            highs, lows = [], []
            for entry in range(begin, begin + group):
                value = struct[pl.ds(entry, 1), :]
                highs.append(jnp.where(wanted == value // LANES, 1.0, 0.0))
                lows.append(jnp.where(lane_ids == value % LANES, 1.0, 0.0))
            counts = counts + lax.dot_general(
                jnp.concatenate(highs, axis=1).astype(jnp.bfloat16),
                jnp.concatenate(lows, axis=1).astype(jnp.bfloat16),
                (((1,), (1,)), ((), ())),
                preferred_element_type=jnp.float32,
            )
        masks[at] = jnp.where(counts > 0.5, 1.0, 0.0)
    diag_one[...] = exact(lower_one[...].T, lower_one[...], ((1,), (0,)))
    diag_two[...] = exact(lower_two[...].T, lower_two[...], ((1,), (0,)))

    def mask_of(panel, begin):
        return jnp.concatenate([masks[panel, pl.ds(begin + at, 1), :] for at in range(blocks)], axis=1)

    def prepare(at):
        near_copy(at).wait_recv()
        far_copy(at).wait_recv()
        relay_copy(at).start()
        relay_copy(at).wait_recv()
        for slot in range(COLS):
            value = land[slot, at].T * mask_of(at // per_panel, slot * blocks)
            upper_part = value.astype(jnp.bfloat16)
            columns = pl.ds(slot * span, span)
            left[at, pl.ds(0, chunk), columns] = upper_part
            left[at, pl.ds(chunk, chunk), columns] = (value - upper_part.astype(jnp.float32)).astype(jnp.bfloat16)

    def pair_copy(at, step):
        return flow(3, other.at[at, step], pair_in.at[at, step], pair_sem.at[at, step], beside)

    def multiply(at, step, which):
        target = step * 2 + which
        both = jnp.dot(left[at], high[target], preferred_element_type=jnp.float32)
        rest = jnp.dot(left[at, pl.ds(0, chunk), :], low[target], preferred_element_type=jnp.float32)
        value = both[:chunk] + (both[chunk:] + rest)
        if which == 0:
            other[at, step] = value
            pair_copy(at, step).start()
        else:
            mine[at, step] = value

    def first_step(step, carry):
        for which in range(2):
            fetch(step, which).wait()
            target = step * 2 + which
            for begin in range(0, depth, 256):
                size = min(256, depth - begin)
                value = window[which, pl.ds(begin, size), :]
                upper_part = value.astype(jnp.bfloat16)
                high[target, pl.ds(begin, size), :] = upper_part
                low[target, pl.ds(begin, size), :] = (value - upper_part.astype(jnp.float32)).astype(jnp.bfloat16)

            @pl.when(step + 1 < 4)
            def _():
                fetch(step + 1, which).start()

            multiply(0, step, which)
        pl.when(step == 1)(lambda: climb_turned(1))
        return carry

    def later_steps(chunks, begin, end):
        def body(step, carry):
            for at in chunks:
                for which in range(2):
                    multiply(at, step, which)
            return carry

        lax.fori_loop(begin, end, body, 0)

    def major_copy(at, step):
        slot = jnp.where(ends, (0, 2, 3)[step], (1, 3, 4)[step])
        peer = near if step == 1 else (jnp.where(ends, near[0], inner[0]), col)
        return flow(4, mine.at[at, step], major_in.at[at, slot], major_sem.at[at, slot], peer)

    def arrived(at, slot):
        pltpu.make_async_copy(mine.at[at, 0], major_in.at[at, slot], major_sem.at[at, slot]).wait()
        return major_in[at, slot]

    def forward(at, step):
        pair_copy(at, step).wait_recv()
        mine[at, step] = mine[at, step] + pair_in[at, step]

        @pl.when(middle)
        def _():
            mine[at, step] = mine[at, step] + arrived(at, step)

        major_copy(at, step).start()

    def collect(at):
        pair_copy(at, 3).wait_recv()
        product[at] = (mine[at, 3] + pair_in[at, 3]) + arrived(at, 3)

        @pl.when(middle)
        def _():
            product[at] = product[at] + arrived(at, 4)

    half = width // 2
    plain, last = ((1,), (0,)), ((1,), (1,))
    def flipped(upper_at, lower_at, y_at, x_at):
        z_at = jnp.where(upper_at, 1 - upper, upper) * 2 + jnp.where(lower_at, 1 - lower, lower)
        return z_at, jnp.where(y_at, 1 - y, y), jnp.where(x_at, 1 - x, x)

    def bits_of(offset):
        return offset // 8, offset // 4 % 2, offset // 2 % 2, offset % 2

    far_chips = sorted(range(1, CHIPS), key=lambda offset: -sum(w * b for w, b in zip((2.2, 1, 1, 1), bits_of(offset))))

    side_here = lax.rem(x + y, 2)
    opposite = device(z, 1 - y, 1 - x, core)

    class LineTotal:
        share = 7 * half // 2
        wide = share // 2
        rows = wide // 4

        def __init__(self):
            self.base = core * self.share
            self.half_rows = pl.ds(self.base, self.share)
            self.wide_rows = pl.ds(self.base + side_here * self.wide, self.wide)
            self.mine_rows = pl.ds(self.base + side_here * self.wide + z * self.rows, self.rows)
            self.sent = []

        def launch(self, *copy):
            copy = remote(*copy)
            copy.start()
            self.sent.append(copy)
            return copy

        def begin(self, tiles):
            for at, tile in enumerate(tiles):
                packed[pl.ds(at * half, half), :] = tile
            theirs = pl.ds((1 - core) * self.share, self.share)
            self.first = self.launch(packed.at[theirs], fold_in, sum_sem, (0,), partner)

        def scatter(self):
            self.first.wait_recv()
            fold[...] = packed[self.half_rows, :] + fold_in[...]
            theirs = pl.ds((1 - side_here) * self.wide, self.wide)
            self.second = self.launch(fold.at[theirs], wide_sum.at[1], sum_sem, (3,), across)

        def line(self):
            for at, (upper_at, lower_at) in enumerate(((1, 1), (1, 0), (0, 1))):
                z_at = flipped(upper_at, lower_at, 0, 0)[0]
                yield at, z_at, device(z_at, y, x, core)

        def climb(self):
            self.second.wait_recv()
            wide_sum[0] = fold[pl.ds(side_here * self.wide, self.wide), :] + wide_sum[1]
            self.copies = [
                self.launch(wide_sum.at[0, pl.ds(z_at * self.rows, self.rows)], part_in.at[at], line_sem, (0, at), peer)
                for at, z_at, peer in self.line()
            ]

        def cross(self):
            for copy in self.copies:
                copy.wait_recv()
            side[0] = (wide_sum[0, pl.ds(z * self.rows, self.rows), :] + part_in[0]) + (part_in[1] + part_in[2])
            self.crossing = self.launch(side.at[0], side.at[1], sum_sem, (2,), opposite)

        def spread(self):
            self.crossing.wait_recv()
            full[self.mine_rows, :] = side[0] + side[1]
            target = full.at[self.mine_rows]
            self.copies = [self.launch(target, target, line_sem, (1, at), peer) for at, _, peer in self.line()]

        def widen(self):
            for copy in self.copies:
                copy.wait_recv()
            target = full.at[self.wide_rows]
            self.second = self.launch(target, target, sum_sem, (4,), across)

        def finish(self):
            self.second.wait_recv()
            target = full.at[self.half_rows]
            self.final = self.launch(target, target, sum_sem, (1,), partner)

        def tile(self, at):
            return full[pl.ds(at * half, half), :]

    owner_here = core == x

    class DirectTotal:
        def __init__(self, at, start, blocks):
            self.at, self.start, self.rows = at, start, blocks * half // CHIPS
            self.mine_rows = pl.ds(start + chip * self.rows, self.rows)

        def place(self, offset, core_at=None):
            z_at, y_at, x_at = flipped(*bits_of(offset))
            return (z_at * 2 + y_at) * 2 + x_at, device(z_at, y_at, x_at, x_at if core_at is None else core_at)

        def sending(self, offset):
            flat, peer = self.place(offset)
            return pltpu.make_async_remote_copy(
                src_ref=packed.at[pl.ds(self.start + flat * self.rows, self.rows)],
                dst_ref=straight.at[self.at, offset * 2 + core, pl.ds(0, self.rows)],
                send_sem=direct_send.at[self.at, 0 if offset else 1],
                recv_sem=direct_recv.at[self.at],
                device_id=peer,
                device_id_type=MESH,
            )

        def handing(self, offset, core_at):
            peer = partner if core_at is None else self.place(offset, core_at)[1]
            return pltpu.make_async_remote_copy(
                src_ref=full.at[self.mine_rows],
                dst_ref=full.at[self.mine_rows],
                send_sem=hand_send.at[self.at],
                recv_sem=hand_recv.at[self.at, 0 if offset else 1],
                device_id=peer,
                device_id_type=MESH,
            )

        def hands(self):
            return [self.handing(offset, core_at) for offset in far_chips for core_at in range(2)] + [
                self.handing(0, None)
            ]

        def begin(self, tiles):
            for at, tile in enumerate(tiles):
                packed[pl.ds(self.start + at * half, half), :] = tile
            for offset in far_chips:
                self.sending(offset).start()
            pl.when(jnp.logical_not(owner_here))(lambda: self.sending(0).start())

        def spread(self):
            @pl.when(owner_here)
            def _():
                rows = pl.ds(0, self.rows)
                take(straight.at[self.at, pl.ds(0, 2 * CHIPS - 1), rows], direct_recv.at[self.at])
                value = packed[self.mine_rows, :] + straight[self.at, 1 - core, rows, :]
                for slot in range(2, 2 * CHIPS):
                    value = value + straight[self.at, slot, rows, :]
                full[self.mine_rows, :] = value
                for copy in self.hands():
                    copy.start()

        def many(self, count):
            return packed.at[pl.ds(0, count * self.rows)]

        def finish(self):
            take(self.many(CHIPS - 1), hand_recv.at[self.at, 0])
            pl.when(jnp.logical_not(owner_here))(lambda: self.handing(0, None).wait_recv())

        def drain(self):
            take(self.many(CHIPS - 1), direct_send.at[self.at, 0])
            pl.when(jnp.logical_not(owner_here))(lambda: self.sending(0).wait_send())
            pl.when(owner_here)(lambda: take(self.many(2 * CHIPS - 1), hand_send.at[self.at]))

        def tile(self, at):
            return full[pl.ds(self.start + at * half, half), :]

    def quarters(value, places):
        return [value[i * half : (i + 1) * half, j * half : (j + 1) * half] for i, j in places]

    upper_places = ((0, 0), (0, 1), (1, 1))
    every_place = ((0, 0), (0, 1), (1, 0), (1, 1))
    tile_count = owner.shape[0]
    tile_rows = span // tile_count
    names = [owner[at] for at in range(tile_count)]
    ranks = [
        sum([jnp.where(names[before] == names[at], 1, 0) for before in range(at)], jnp.int32(0))
        for at in range(tile_count)
    ]
    tile_copies = []

    def send_tiles(part, values):
        columns = pl.ds(part * half, half)

        def slot_value(name, rank):
            value = jnp.zeros((tile_rows, half), jnp.float32)
            for at in range(tile_count):
                chosen = (names[at] == name) & (ranks[at] == rank)
                value = jnp.where(chosen, values[at * tile_rows : (at + 1) * tile_rows], value)
            return value

        for offset in range(1, COLS):
            name = lax.rem(col + offset, COLS)
            for rank in range(CAP):
                outgoing[offset - 1, rank, :, columns] = slot_value(name, rank)
            copy = remote(
                outgoing.at[offset - 1, :, :, columns],
                delivered.at[pl.ds(col * CAP, CAP), :, columns],
                tile_sem,
                (part, offset - 1),
                (row, name),
            )
            copy.start()
            tile_copies.append(copy)
        for rank in range(CAP):
            tiles_here[rank, :, columns] = slot_value(col, rank)

    first_total = LineTotal()
    middle_total, second_total = DirectTotal(0, 7 * half, 2), DirectTotal(1, 9 * half, 1)

    prepare(0)
    climb_turned(0)
    lax.fori_loop(0, 4, first_step, 0)
    prepare(1)
    def only(where, *steps):
        @pl.when(where)
        def _():
            for at, step in steps:
                forward(at, step)

    only(ends, (0, 0))
    later_steps((1,), 0, 4)
    only(middle, (0, 0))
    only(ends, (0, 1))
    prepare(2)
    prepare(3)
    only(ends, (0, 2))
    later_steps((2, 3), 0, 2)
    only(middle, (0, 1), (0, 2))
    only(ends, (1, 0))
    pass_on(0)
    pass_on(1)
    only(ends, (1, 1))
    collect(0)
    only(middle, (1, 0), (1, 1))
    forward(1, 2)
    only(ends, (2, 0))
    collect(1)
    only(ends, (3, 0))
    only(middle, (2, 0))
    one_row = mask_of(0, slots_of)
    two_row = mask_of(1, slots_of)
    inv_one_t[...] = -(jnp.concatenate([product[at] for at in range(per_panel)], axis=0) * one_row)
    for copy in passed:
        copy.wait_recv()
    panel_two_t[...] = resident[0, 1].T
    gram_one = exact(resident[0, 0].T, inv_one_t[...], last)
    cross_sum = exact(inv_one_t[...] * two_row, panel_two_t[...], last)
    first_total.begin(quarters(gram_one, upper_places) + quarters(cross_sum, every_place))
    above_t = above[...].T
    correction[...] = exact(above_t, inv_one_t[...], plain) * two_row
    inverse_one[...] = inv_one_t[...].T
    outs = [pltpu.make_async_copy(inverse_one, inverse_one_out, out_sem.at[0])]
    outs[0].start()
    first_total.scatter()
    later_steps((2, 3), 2, 3)
    only(ends, (2, 1))
    only(middle, (3, 0), (2, 1))
    later_steps((2, 3), 3, 4)
    first_total.climb()
    forward(3, 1)
    forward(2, 2)
    first_total.cross()
    forward(3, 2)
    collect(2)
    first_total.spread()
    low_half, high_half = pl.ds(0, half), pl.ds(half, half)
    part_two_t[low_half, :] = -(product[2] * two_row)
    gram_left = exact(panel_two_t[...], part_two_t[low_half, :], last)
    middle_total.begin([gram_left[:half], gram_left[half:]])
    send_tiles(0, (part_two_t[low_half, :] - correction[low_half, :]).T)
    collect(3)
    part_two_t[high_half, :] = -(product[3] * two_row)
    second_total.begin([exact(panel_two_t[high_half, :], part_two_t[high_half, :], last)])
    late = (part_two_t[high_half, :] - correction[high_half, :]).T
    first_total.widen()
    middle_total.spread()
    send_tiles(1, late)
    second_total.spread()
    first_total.finish()

    here = pltpu.make_async_copy(tiles_here, delivered.at[pl.ds(col * CAP, CAP)], out_sem.at[4])
    here.start()
    outs.append(here)

    def put(at, source, target):
        copy = pltpu.make_async_copy(source, target, out_sem.at[at])
        copy.start()
        outs.append(copy)

    def square(first, second, third, fourth):
        return jnp.concatenate(
            [jnp.concatenate([first, second], axis=1), jnp.concatenate([third, fourth], axis=1)], axis=0
        )

    for copy in tile_copies:
        copy.wait()

    for panel in range(2):

        @pl.when(turns)
        def _():
            turn[panel].wait_send()

        @pl.when(jnp.logical_not(turns))
        def _():
            end_climb(own, panel, 0, y)
            end_climb(turned, panel, 1, 1 - y)

        pl.when(relays_move)(lambda: passed[panel].wait_send())

    middle_total.drain()
    for copy in first_total.sent[:-1]:
        copy.wait_send()
    for kind, like in enumerate((own, own, land.at[0], other, mine.at[:, pl.ds(0, 3)])):
        take(like, flow_sem.at[kind])

    first_total.final.wait_recv()
    tile = first_total.tile
    diag_one_value = diag_one[...] - square(tile(0), tile(1), tile(1).T, tile(2))
    cross_total = square(tile(3), tile(4), tile(5), tile(6))
    diag_one[...] = diag_one_value
    put(1, diag_one, diag_one_out)
    cross_value = -(cross_total + exact(diag_one_value, above[...], plain))
    cross_two[...] = cross_value
    put(2, cross_two, cross_two_out)
    diag_two[...] = diag_two[...] + (exact(cross_total.T, above[...], plain) - exact(above_t, cross_value, plain))
    middle_total.finish()
    tile = middle_total.tile
    second_total.finish()
    diag_two[...] = diag_two[...] - square(tile(0), tile(1).T, tile(1), second_total.tile(0))
    put(3, diag_two, diag_two_out)

    for copy in outs:
        copy.wait()
    second_total.drain()
    first_total.final.wait_send()


def place_kernel(count, *refs):
    sources, targets, buffers, sems = refs[:count], refs[count : 2 * count], refs[2 * count : -1], refs[-1]
    loads = [pltpu.make_async_copy(sources[at], buffers[at], sems.at[0, at]) for at in range(count)]
    stores = [pltpu.make_async_copy(buffers[at], targets[at], sems.at[1, at]) for at in range(count)]
    for copy in loads:
        copy.start()
    for load, store in zip(loads, stores):
        load.wait()
        store.start()
    for copy in stores:
        copy.wait()


def fused(matrix, panel_one, panel_two, struct_one, struct_two, lower_one, above, lower_two, tile_owner):
    depth, _ = matrix.shape
    span, width = panel_one.shape
    chunk = 2 * width // CHUNKS
    tile_count = tile_owner.shape[0]
    share = 7 * (width // 2) // 2
    mask_rows = -(-(COLS + 1) * (span // LANES) // 8) * 8
    dma = pltpu.SemaphoreType.DMA
    vmem = lambda *shape: pltpu.VMEM(shape, jnp.float32)
    half_vmem = lambda *shape: pltpu.VMEM(shape, jnp.bfloat16)
    anywhere = pl.BlockSpec(memory_space=pl.ANY)
    scalars = pl.BlockSpec(memory_space=pltpu.SMEM)
    shape = lambda *dims: jax.ShapeDtypeStruct(dims, jnp.float32)
    results = pl.pallas_call(
        fused_kernel,
        out_shape=[
            shape(span, width),
            shape(width, width),
            shape(width, width),
            shape(width, width),
            shape(COLS * CAP, span // tile_count, width),
        ],
        in_specs=[anywhere] * 8 + [scalars],
        out_specs=[anywhere] * 5,
        scratch_shapes=[
            vmem(span, width),
            vmem(width, width),
            vmem(width, width),
            vmem(width, width),
            vmem(CAP, span // tile_count, width),
            pltpu.VMEM((struct_one.shape[0] // LANES, LANES), jnp.int32),
            pltpu.VMEM((struct_two.shape[0] // LANES, LANES), jnp.int32),
            vmem(width, width),
            vmem(width, width),
            vmem(width, width),
            vmem(2, depth, span),
            half_vmem(8, depth, span),
            half_vmem(8, depth, span),
            vmem(2, span, width),
            vmem(COLS, CHUNKS, span, chunk),
            half_vmem(CHUNKS, 2 * chunk, depth),
            vmem(CHUNKS, 4, chunk, span),
            vmem(CHUNKS, 4, chunk, span),
            vmem(CHUNKS, 4, chunk, span),
            vmem(CHUNKS, 5, chunk, span),
            vmem(2, mask_rows, LANES),
            vmem(2, span, width),
            vmem(2, 2, span, width),
            vmem(CHUNKS, chunk, span),
            vmem(width, span),
            vmem(width, span),
            vmem(width, span),
            vmem(width, span),
            vmem(10 * (width // 2), LANES),
            vmem(share, LANES),
            vmem(share, LANES),
            vmem(3, share // 8, LANES),
            vmem(2, share // 8, LANES),
            vmem(2, share // 2, LANES),
            vmem(2, 2 * CHIPS, width // CHIPS, LANES),
            vmem(10 * (width // 2), LANES),
            vmem(COLS - 1, CAP, span // tile_count, width),
            dma((5,)),
            dma((5,)),
            dma((2,)),
            dma((2,)),
            dma((2, 2)),
            dma((2, 2, 3)),
            dma((5,)),
            dma((3, CHUNKS)),
            dma((CHUNKS, 4)),
            dma((CHUNKS, 5)),
            dma((2, 5)),
            dma((2, 2, 3)),
            dma((2, 2)),
            dma((2,)),
            dma((2,)),
            dma((2, 2)),
            dma((2, 2, COLS - 1)),
        ],
        compiler_params=pltpu.CompilerParams(
            collective_id=3, has_side_effects=True, vmem_limit_bytes=58 * 2**20
        ),
        cost_estimate=pl.CostEstimate(
            flops=12 * matrix.size * width, bytes_accessed=4 * matrix.size, transcendentals=0
        ),
    )(
        matrix,
        panel_one,
        panel_two,
        struct_one.reshape(-1, LANES),
        struct_two.reshape(-1, LANES),
        lower_one,
        above,
        lower_two,
        tile_owner.reshape(-1),
    )
    return tuple(pl.pallas_call(
        functools.partial(place_kernel, len(results)),
        out_shape=[shape(*result.shape) for result in results],
        in_specs=[anywhere] * len(results),
        out_specs=[anywhere] * len(results),
        scratch_shapes=[vmem(*result.shape) for result in results] + [dma((2, len(results)))],
        compiler_params=pltpu.CompilerParams(vmem_limit_bytes=60 * 2**20),
    )(*results))


def local(
    ancestor_inverse,
    panel_one,
    struct_one,
    lower_one,
    panel_two,
    struct_two,
    panel_above,
    lower_two,
    tile_owner,
):
    row_count = lax.axis_size("row")
    col_count = lax.axis_size("col")
    row_index = lax.axis_index("row")
    col_index = lax.axis_index("col")
    local_rows = panel_one.shape[0]
    if fits_fused(ancestor_inverse, panel_one, struct_one, struct_two, tile_owner, row_count, col_count):
        return fused(
            ancestor_inverse,
            panel_one,
            panel_two,
            struct_one,
            struct_two,
            lower_one,
            panel_above,
            lower_two,
            tile_owner,
        )
    order = local_rows * row_count * col_count
    width = panel_one.shape[1]
    mask_one = row_mask(struct_one, order)
    mask_two = row_mask(struct_two, order)
    panel_start = (row_index * col_count + col_index) * local_rows
    result_start = (col_index * row_count + row_index) * local_rows
    local_one = panel_one * lax.dynamic_slice_in_dim(mask_one, panel_start, local_rows)[:, None]
    local_two = panel_two * lax.dynamic_slice_in_dim(mask_two, panel_start, local_rows)[:, None]
    result_mask_one = lax.dynamic_slice_in_dim(mask_one, result_start, local_rows)[:, None]
    result_mask_two = lax.dynamic_slice_in_dim(mask_two, result_start, local_rows)[:, None]

    both = jnp.concatenate([local_one, local_two], axis=1)
    gathered = lax.all_gather(both, "col", axis=0, tiled=True)
    product = scatter_rows(contract_rows(ancestor_inverse, gathered, lax.Precision.HIGH), row_count)
    moves = [(f, (f % row_count) * col_count + f // row_count) for f in range(row_count * col_count)]
    resident = lax.ppermute(both, ("row", "col"), moves)
    resident_one = resident[:, :width]
    resident_two = resident[:, width:]
    inverse_one = -product[:, :width] * result_mask_one
    inverse_two = -(product[:, width:] + matmul(inverse_one, panel_above)) * result_mask_two
    grams = (
        contract_rows(resident_one, inverse_one),
        contract_rows(inverse_one, resident_two),
        contract_rows(resident_two, inverse_two),
    )
    lanes = 128
    packed = jnp.concatenate(
        [gram[:, at : at + lanes] for gram in grams for at in range(0, width, lanes)], axis=0
    )
    sums = sum_everywhere(packed, row_count, col_count).reshape(len(grams), width // lanes, width, lanes)
    gram_one, cross_sum, gram_two = (
        jnp.concatenate([sums[at, block] for block in range(width // lanes)], axis=1) for at in range(len(grams))
    )
    diag_one = matmul(lower_one.T, lower_one) - gram_one
    cross_two = -(cross_sum + matmul(diag_one, panel_above))
    diag_two = matmul(lower_two.T, lower_two) - gram_two - matmul(panel_above.T, cross_two)
    delivered = deliver(inverse_two, tile_owner, col_count)
    return (inverse_one, diag_one, cross_two, diag_two, delivered)


def solution(mesh):
    return jax.shard_map(
        local,
        mesh=mesh,
        in_specs=(
            P("row", "col"),
            P(("row", "col"), None),
            P(),
            P(),
            P(("row", "col"), None),
            P(),
            P(),
            P(),
            P(("col", "row"), None),
        ),
        out_specs=(P(("col", "row"), None), P(), P(), P(), P(("row", "col"), None, None)),
        check_vma=False,
    )
```

```python
import functools

import jax
import jax.numpy as jnp
from jax import lax
from jax.experimental import pallas as pl
from jax.experimental.pallas import tpu as pltpu
from jax.sharding import PartitionSpec as P

CAP = 2


def matmul(left, right):
    return jnp.dot(left, right, precision=lax.Precision.HIGHEST, preferred_element_type=jnp.float32)


def contract_rows(left, right, precision=lax.Precision.HIGHEST):
    return lax.dot_general(
        left,
        right,
        (((0,), (0,)), ((), ())),
        precision=precision,
        preferred_element_type=jnp.float32,
    )


def row_mask(struct, count):
    lanes = 128
    high = struct // lanes
    low = struct % lanes
    high_hot = (jnp.arange(count // lanes, dtype=jnp.int32)[:, None] == high[None, :]).astype(jnp.bfloat16)
    low_hot = (jnp.arange(lanes, dtype=jnp.int32)[:, None] == low[None, :]).astype(jnp.bfloat16)
    counts = lax.dot_general(high_hot, low_hot, (((1,), (1,)), ((), ())), preferred_element_type=jnp.float32)
    return (counts > 0.5).astype(jnp.float32).reshape(count)


MESH = pl.DeviceIdType.MESH


def greet(peers):
    barrier = pltpu.get_barrier_semaphore()
    for peer in peers:
        pl.semaphore_signal(barrier, inc=1, device_id=peer, device_id_type=MESH)
    pl.semaphore_wait(barrier, len(peers))


def scatter_kernel(rows, value_ref, out_ref, pair_in, total, major_in, pair_send, pair_recv, major_send, major_recv):
    majors = rows // 2
    row = lax.axis_index("row")
    col = lax.axis_index("col")
    major, minor = row // 2, row % 2
    partner = (major * 2 + 1 - minor, col)

    def peer(offset):
        return (lax.rem(major + offset, majors) * 2 + minor, col)

    greet([partner] + [peer(offset) for offset in range(1, majors)])
    order = sorted(range(1, majors), key=lambda offset: -min(offset, majors - offset)) + [0]
    started = []
    pair_copies = {}
    for offset in order:
        target = lax.rem(major + offset, majors)
        copy = pltpu.make_async_remote_copy(
            src_ref=value_ref.at[target * 2 + 1 - minor],
            dst_ref=pair_in.at[offset],
            send_sem=pair_send.at[offset],
            recv_sem=pair_recv.at[offset],
            device_id=partner,
            device_id_type=MESH,
        )
        copy.start()
        pair_copies[offset] = copy
    for offset in order:
        target = lax.rem(major + offset, majors)
        pair_copies[offset].wait_recv()
        total[offset] = pair_in[offset] + value_ref[target * 2 + minor]
        if offset:
            copy = pltpu.make_async_remote_copy(
                src_ref=total.at[offset],
                dst_ref=major_in.at[offset - 1],
                send_sem=major_send.at[offset - 1],
                recv_sem=major_recv.at[offset - 1],
                device_id=peer(offset),
                device_id_type=MESH,
            )
            copy.start()
            started.append(copy)
    for copy in started:
        copy.wait_recv()
    result = total[0]
    for slot in range(majors - 1):
        result = result + major_in[slot]
    out_ref[...] = result
    for copy in started:
        copy.wait_send()
    for offset in order:
        pair_copies[offset].wait_send()


def scatter_rows(value, rows):
    chunk, width = value.shape[0] // rows, value.shape[1]
    majors = rows // 2
    dma = pltpu.SemaphoreType.DMA
    return pl.pallas_call(
        functools.partial(scatter_kernel, rows),
        out_shape=jax.ShapeDtypeStruct((chunk, width), jnp.float32),
        in_specs=[pl.BlockSpec(memory_space=pltpu.VMEM)],
        out_specs=pl.BlockSpec(memory_space=pltpu.VMEM),
        scratch_shapes=[
            pltpu.VMEM((majors, chunk, width), jnp.float32),
            pltpu.VMEM((majors, chunk, width), jnp.float32),
            pltpu.VMEM((majors - 1, chunk, width), jnp.float32),
            dma((majors,)),
            dma((majors,)),
            dma((majors - 1,)),
            dma((majors - 1,)),
        ],
        compiler_params=pltpu.CompilerParams(
            collective_id=0, has_side_effects=True, vmem_limit_bytes=40 * 2**20
        ),
    )(value.reshape(rows, chunk, width))


def sum_kernel(rows, cols, value_ref, out_ref, full, sum_a, sum_b, in_a, in_b, in_c, *sems):
    row = lax.axis_index("row")
    col = lax.axis_index("col")
    outer = cols // 2
    far, core = col // 2, col % 2
    half = outer * rows
    base_a = core * half
    base_b = base_a + far * rows
    base_c = base_b + row

    def pair_peer(offset):
        return (row, far * 2 + 1 - core)

    def far_peer(offset):
        return (row, lax.rem(far + offset, outer) * 2 + core)

    def row_peer(offset):
        return (lax.rem(row + offset, rows), col)

    greet(
        [pair_peer(1)]
        + [far_peer(offset) for offset in range(1, outer)]
        + [row_peer(offset) for offset in range(1, rows)]
    )

    def exchange(count, peer, source, landing, stage):
        copies = []
        for offset in range(1, count):
            copy = pltpu.make_async_remote_copy(
                src_ref=source(offset),
                dst_ref=landing(offset),
                send_sem=sems[2 * stage].at[offset - 1],
                recv_sem=sems[2 * stage + 1].at[offset - 1],
                device_id=peer(offset),
                device_id_type=MESH,
            )
            copy.start()
            copies.append(copy)
        for copy in copies:
            copy.wait_recv()
        return copies

    pending = []
    pending += exchange(
        2, pair_peer, lambda k: value_ref.at[pl.ds((1 - core) * half, half)], lambda k: in_a.at[k - 1], 0
    )
    sum_a[...] = value_ref[pl.ds(base_a, half)] + in_a[0]
    pending += exchange(
        outer, far_peer, lambda k: sum_a.at[pl.ds(lax.rem(far + k, outer) * rows, rows)], lambda k: in_b.at[k - 1], 1
    )
    total = sum_a[pl.ds(far * rows, rows)]
    for slot in range(outer - 1):
        total = total + in_b[slot]
    sum_b[...] = total
    pending += exchange(
        rows, row_peer, lambda k: sum_b.at[lax.rem(row + k, rows)], lambda k: in_c.at[k - 1], 2
    )
    total = sum_b[row]
    for slot in range(rows - 1):
        total = total + in_c[slot]
    full[base_c] = total
    pending += exchange(rows, row_peer, lambda k: full.at[base_c], lambda k: full.at[base_c], 3)
    pending += exchange(
        outer, far_peer, lambda k: full.at[pl.ds(base_b, rows)], lambda k: full.at[pl.ds(base_b, rows)], 4
    )
    pending += exchange(
        2, pair_peer, lambda k: full.at[pl.ds(base_a, half)], lambda k: full.at[pl.ds(base_a, half)], 5
    )
    out_ref[...] = full[...]
    for copy in pending:
        copy.wait_send()


def sum_everywhere(value, rows, cols):
    devices = rows * cols
    lanes = value.shape[1]
    depth = value.shape[0] // devices
    outer = cols // 2
    dma = pltpu.SemaphoreType.DMA
    vmem = lambda *lead: pltpu.VMEM(lead + (depth, lanes), jnp.float32)
    total = pl.pallas_call(
        functools.partial(sum_kernel, rows, cols),
        out_shape=jax.ShapeDtypeStruct((devices, depth, lanes), jnp.float32),
        in_specs=[pl.BlockSpec(memory_space=pltpu.VMEM)],
        out_specs=pl.BlockSpec(memory_space=pltpu.VMEM),
        scratch_shapes=[
            vmem(devices),
            vmem(devices // 2),
            vmem(rows),
            vmem(1, devices // 2),
            vmem(outer - 1, rows),
            vmem(rows - 1),
        ]
        + [dma((count - 1,)) for count in (2, outer, rows, rows, outer, 2) for _ in range(2)],
        compiler_params=pltpu.CompilerParams(
            collective_id=1, has_side_effects=True, vmem_limit_bytes=24 * 2**20
        ),
        cost_estimate=pl.CostEstimate(flops=0, bytes_accessed=100 * value.size * 4, transcendentals=0),
    )(value.reshape(devices, depth, lanes))
    return total.reshape(value.shape)


def deliver(values, tile_owner, col_count):
    tile_count = tile_owner.shape[0]
    tile_rows = values.shape[0] // tile_count
    all_tiles = values.reshape(tile_count, tile_rows, values.shape[1])
    owner_col = tile_owner[:, 0]
    col_ids = jnp.arange(col_count, dtype=jnp.int32)
    onehot = (owner_col[:, None] == col_ids[None, :]).astype(jnp.int32)
    tile_rank = jnp.sum((jnp.cumsum(onehot, axis=0) - onehot) * onehot, axis=1)
    slot_index = jnp.arange(CAP, dtype=jnp.int32)
    select = (
        (owner_col[None, None, :] == col_ids[:, None, None])
        & (tile_rank[None, None, :] == slot_index[None, :, None])
    ).astype(jnp.float32)
    outgoing = jnp.einsum("cks,srb->ckrb", select, all_tiles, precision=lax.Precision.HIGHEST)
    incoming = lax.all_to_all(outgoing, "col", split_axis=0, concat_axis=0, tiled=True)
    return incoming.reshape(col_count * CAP, tile_rows, values.shape[1])


ROWS, COLS, CHIPS = 8, 4, 16
CHUNKS = 4
LANES = 128


def fits_fused(matrix, panel, struct_one, struct_two, tile_owner, rows, cols):
    span, width = panel.shape
    return (
        (rows, cols) == (ROWS, COLS)
        and span % LANES == 0
        and width == 2 * LANES
        and matrix.shape == (cols * span, rows * span)
        and struct_one.shape[0] % LANES == 0
        and struct_two.shape[0] % LANES == 0
        and span % (8 * tile_owner.shape[0]) == 0
    )


def exact(left, right, contract):
    return lax.dot_general(
        left, right, (contract, ((), ())), precision=lax.Precision.HIGHEST, preferred_element_type=jnp.float32
    )


def fused_kernel(
    matrix, panel_one, panel_two, struct_one_in, struct_two_in, lower_one_in, above_in, lower_two_in, owner,
    inverse_one_out, diag_one_out, cross_two_out, diag_two_out, delivered,
    inverse_one, diag_one, cross_two, diag_two, tiles_here,
    struct_one, struct_two, lower_one, above, lower_two, window, high, low, own, land, left, other, mine, pair_in, major_in, masks, turned, resident, product,
    inv_one_t, part_two_t, panel_two_t, correction, packed, fold_in, fold, part_in, side, wide_sum, straight, full, outgoing,
    out_sem, small_sem, fetch_sem, own_sem, turn_sem, move_sem, flow_sem, gather_sem, pair_sem, major_sem, sum_sem, line_sem,
    direct_send, direct_recv, hand_send, hand_recv, tile_sem,
):
    row = lax.axis_index("row")
    col = lax.axis_index("col")
    z, y = row // 2, row % 2
    x, core = col // 2, col % 2
    upper, lower = z // 2, z % 2
    chip = (z * 2 + y) * 2 + x
    depth, total_columns = matrix.shape
    span, width = own.shape[1:]
    chunk = left.shape[1] // 2
    per_panel = width // chunk

    def device(z_at, y_at, x_at, core_at):
        return (z_at * 2 + y_at, x_at * 2 + core_at)

    partner = device(z, y, x, 1 - core)
    across = device(z, y, 1 - x, core)
    beside = device(z, 1 - y, x, core)
    near = device(upper * 2 + 1 - lower, y, x, core)
    inner = device(3 - z, y, x, core)
    ends = upper == lower
    middle = upper != lower

    def remote(source, target, sems, at, peer):
        return pltpu.make_async_remote_copy(
            src_ref=source,
            dst_ref=target,
            send_sem=sems.at[(0,) + at],
            recv_sem=sems.at[(1,) + at],
            device_id=peer,
            device_id_type=MESH,
        )

    own_copies = [
        pltpu.make_async_copy(panel, own.at[at], own_sem.at[at]) for at, panel in enumerate((panel_one, panel_two))
    ]
    for copy in own_copies:
        copy.start()

    def fetch(step, which):
        rank = jnp.where(ends, step, jnp.where(step == 0, 0, jnp.where(step == 3, 2, 5 - 2 * step)))
        target = jnp.where(upper == 0, 3 - rank, rank) * 2 + lax.rem(1 - y + which, 2)
        return pltpu.make_async_copy(
            matrix.at[:, pl.ds(pl.multiple_of(target * span, LANES), span)], window.at[which], fetch_sem.at[which]
        )

    small_pairs = (
        (struct_one_in, struct_one),
        (struct_two_in, struct_two),
        (lower_one_in, lower_one),
        (above_in, above),
        (lower_two_in, lower_two),
    )
    small_copies = [
        pltpu.make_async_copy(source, target, small_sem.at[at]) for at, (source, target) in enumerate(small_pairs)
    ]
    for copy in small_copies:
        copy.start()
    barrier = pltpu.get_barrier_semaphore()

    def greet_at(semaphore, peer):
        pl.semaphore_signal(semaphore, inc=1, device_id=peer, device_id_type=MESH)

    devices = ROWS * COLS
    for offset in range(1, devices):
        flat = lax.rem(row * COLS + col + offset, devices)
        greet_at(barrier, (flat // COLS, lax.rem(flat, COLS)))
    for which in range(2):
        fetch(0, which).start()
    pl.semaphore_wait(barrier, devices - 1)
    for copy in own_copies:
        copy.wait()

    def piece(at):
        return own.at[at // per_panel, :, pl.ds(at % per_panel * chunk, chunk)]

    def flow(kind, source, target, recv_sem, peer):
        return pltpu.make_async_remote_copy(
            src_ref=source,
            dst_ref=target,
            send_sem=flow_sem.at[kind],
            recv_sem=recv_sem,
            device_id=peer,
            device_id_type=MESH,
        )

    def take(like, semaphore):
        pltpu.make_async_copy(like, like, semaphore).wait()

    def far_copy(at, source=None):
        source = land.at[0, at] if source is None else source
        return flow(0, source, land.at[col, at], gather_sem.at[0, at], across)

    def near_copy(at, source=None):
        source = land.at[0, at] if source is None else source
        return flow(1, source, land.at[col, at], gather_sem.at[1, at], partner)

    def relay_copy(at):
        slot = (1 - x) * 2 + core
        return flow(2, land.at[slot, at], land.at[slot, at], gather_sem.at[2, at], partner)

    turns = core != y
    direct = jnp.where(x == upper, 0, 1)
    relays_move = lower == x

    def move_copy(source, slot, panel, at, peer):
        return pltpu.make_async_remote_copy(
            src_ref=source.at[panel],
            dst_ref=resident.at[slot, panel],
            send_sem=move_sem.at[0, panel, at],
            recv_sem=move_sem.at[1, panel, slot],
            device_id=peer,
            device_id_type=MESH,
        )

    def climb(source, panel, at, from_y):
        peer = device(2 * from_y + x, y, x, lower)
        return move_copy(source, direct, panel, at, peer), (peer[0] == row) & (peer[1] == col)

    def start_climb(source, panel, at, from_y):
        copy, stays = climb(source, panel, at, from_y)
        kept = pltpu.make_async_copy(source.at[panel], resident.at[direct, panel], move_sem.at[1, panel, direct])
        pl.when(stays)(lambda: kept.start())
        pl.when(jnp.logical_not(stays))(lambda: copy.start())

    def end_climb(source, panel, at, from_y):
        copy, stays = climb(source, panel, at, from_y)
        pl.when(jnp.logical_not(stays))(lambda: copy.wait_send())

    turn = [remote(own.at[panel], turned.at[panel], turn_sem, (panel,), beside) for panel in range(2)]
    passed = [move_copy(resident.at[1], 0, panel, 2, across) for panel in range(2)]

    def climb_turned(panel):
        @pl.when(jnp.logical_not(turns))
        def _():
            turn[panel].wait_recv()
            start_climb(turned, panel, 1, 1 - y)

    def pass_on(panel):
        @pl.when(relays_move)
        def _():
            move_copy(own, 1, panel, 0, beside).wait_recv()
            passed[panel].start()

    for at in range(CHUNKS):
        far_copy(at, piece(at)).start()
        near_copy(at, piece(at)).start()
        if at == 0:
            @pl.when(turns)
            def _():
                for copy in turn:
                    copy.start()

            @pl.when(jnp.logical_not(turns))
            def _():
                for panel in range(2):
                    start_climb(own, panel, 0, y)

    for at in range(CHUNKS):
        land[col, at] = piece(at)[...]

    for copy in small_copies:
        copy.wait()
    blocks = span // LANES
    slots_of = COLS * blocks
    mask_rows = masks.shape[1]
    place_rows = lax.broadcasted_iota(jnp.int32, (mask_rows, LANES), 0)
    block_base = row * slots_of
    result_base = (col * ROWS + row) * blocks
    wanted = jnp.where(place_rows < slots_of, block_base + place_rows, result_base + place_rows - slots_of)
    lane_ids = lax.broadcasted_iota(jnp.int32, (LANES, LANES), 0)
    for at, struct in enumerate((struct_one, struct_two)):
        count = struct.shape[0]
        group = max(size for size in range(1, 17) if count % size == 0)
        counts = jnp.zeros((mask_rows, LANES), jnp.float32)
        for begin in range(0, count, group):
            highs, lows = [], []
            for entry in range(begin, begin + group):
                value = struct[pl.ds(entry, 1), :]
                highs.append(jnp.where(wanted == value // LANES, 1.0, 0.0))
                lows.append(jnp.where(lane_ids == value % LANES, 1.0, 0.0))
            counts = counts + lax.dot_general(
                jnp.concatenate(highs, axis=1).astype(jnp.bfloat16),
                jnp.concatenate(lows, axis=1).astype(jnp.bfloat16),
                (((1,), (1,)), ((), ())),
                preferred_element_type=jnp.float32,
            )
        masks[at] = jnp.where(counts > 0.5, 1.0, 0.0)
    diag_one[...] = exact(lower_one[...].T, lower_one[...], ((1,), (0,)))
    diag_two[...] = exact(lower_two[...].T, lower_two[...], ((1,), (0,)))

    def mask_of(panel, begin):
        return jnp.concatenate([masks[panel, pl.ds(begin + at, 1), :] for at in range(blocks)], axis=1)

    def prepare(at):
        near_copy(at).wait_recv()
        far_copy(at).wait_recv()
        relay_copy(at).start()
        relay_copy(at).wait_recv()
        for slot in range(COLS):
            value = land[slot, at].T * mask_of(at // per_panel, slot * blocks)
            upper_part = value.astype(jnp.bfloat16)
            columns = pl.ds(slot * span, span)
            left[at, pl.ds(0, chunk), columns] = upper_part
            left[at, pl.ds(chunk, chunk), columns] = (value - upper_part.astype(jnp.float32)).astype(jnp.bfloat16)

    def pair_copy(at, step):
        return flow(3, other.at[at, step], pair_in.at[at, step], pair_sem.at[at, step], beside)

    def multiply(at, step, which):
        target = step * 2 + which
        both = jnp.dot(left[at], high[target], preferred_element_type=jnp.float32)
        rest = jnp.dot(left[at, pl.ds(0, chunk), :], low[target], preferred_element_type=jnp.float32)
        value = both[:chunk] + (both[chunk:] + rest)
        if which == 0:
            other[at, step] = value
            pair_copy(at, step).start()
        else:
            mine[at, step] = value

    def first_step(step, carry):
        for which in range(2):
            fetch(step, which).wait()
            target = step * 2 + which
            for begin in range(0, depth, 256):
                size = min(256, depth - begin)
                value = window[which, pl.ds(begin, size), :]
                upper_part = value.astype(jnp.bfloat16)
                high[target, pl.ds(begin, size), :] = upper_part
                low[target, pl.ds(begin, size), :] = (value - upper_part.astype(jnp.float32)).astype(jnp.bfloat16)

            @pl.when(step + 1 < 4)
            def _():
                fetch(step + 1, which).start()

            multiply(0, step, which)
        pl.when(step == 1)(lambda: climb_turned(1))
        return carry

    def later_steps(chunks, begin, end):
        def body(step, carry):
            for at in chunks:
                for which in range(2):
                    multiply(at, step, which)
            return carry

        lax.fori_loop(begin, end, body, 0)

    def major_copy(at, step):
        slot = jnp.where(ends, (0, 2, 3)[step], (1, 3, 4)[step])
        peer = near if step == 1 else (jnp.where(ends, near[0], inner[0]), col)
        return flow(4, mine.at[at, step], major_in.at[at, slot], major_sem.at[at, slot], peer)

    def arrived(at, slot):
        pltpu.make_async_copy(mine.at[at, 0], major_in.at[at, slot], major_sem.at[at, slot]).wait()
        return major_in[at, slot]

    def forward(at, step):
        pair_copy(at, step).wait_recv()
        mine[at, step] = mine[at, step] + pair_in[at, step]

        @pl.when(middle)
        def _():
            mine[at, step] = mine[at, step] + arrived(at, step)

        major_copy(at, step).start()

    def collect(at):
        pair_copy(at, 3).wait_recv()
        product[at] = (mine[at, 3] + pair_in[at, 3]) + arrived(at, 3)

        @pl.when(middle)
        def _():
            product[at] = product[at] + arrived(at, 4)

    half = width // 2
    plain, last = ((1,), (0,)), ((1,), (1,))
    def flipped(upper_at, lower_at, y_at, x_at):
        z_at = jnp.where(upper_at, 1 - upper, upper) * 2 + jnp.where(lower_at, 1 - lower, lower)
        return z_at, jnp.where(y_at, 1 - y, y), jnp.where(x_at, 1 - x, x)

    def bits_of(offset):
        return offset // 8, offset // 4 % 2, offset // 2 % 2, offset % 2

    far_chips = sorted(range(1, CHIPS), key=lambda offset: -sum(w * b for w, b in zip((2.2, 1, 1, 1), bits_of(offset))))

    side_here = lax.rem(x + y, 2)
    opposite = device(z, 1 - y, 1 - x, core)

    class LineTotal:
        share = 7 * half // 2
        wide = share // 2
        rows = wide // 4

        def __init__(self):
            self.base = core * self.share
            self.half_rows = pl.ds(self.base, self.share)
            self.wide_rows = pl.ds(self.base + side_here * self.wide, self.wide)
            self.mine_rows = pl.ds(self.base + side_here * self.wide + z * self.rows, self.rows)
            self.sent = []

        def launch(self, *copy):
            copy = remote(*copy)
            copy.start()
            self.sent.append(copy)
            return copy

        def begin(self, tiles):
            for at, tile in enumerate(tiles):
                packed[pl.ds(at * half, half), :] = tile
            theirs = pl.ds((1 - core) * self.share, self.share)
            self.first = self.launch(packed.at[theirs], fold_in, sum_sem, (0,), partner)

        def scatter(self):
            self.first.wait_recv()
            fold[...] = packed[self.half_rows, :] + fold_in[...]
            theirs = pl.ds((1 - side_here) * self.wide, self.wide)
            self.second = self.launch(fold.at[theirs], wide_sum.at[1], sum_sem, (3,), across)

        def line(self):
            for at, (upper_at, lower_at) in enumerate(((1, 1), (1, 0), (0, 1))):
                z_at = flipped(upper_at, lower_at, 0, 0)[0]
                yield at, z_at, device(z_at, y, x, core)

        def climb(self):
            self.second.wait_recv()
            wide_sum[0] = fold[pl.ds(side_here * self.wide, self.wide), :] + wide_sum[1]
            self.copies = [
                self.launch(wide_sum.at[0, pl.ds(z_at * self.rows, self.rows)], part_in.at[at], line_sem, (0, at), peer)
                for at, z_at, peer in self.line()
            ]

        def cross(self):
            for copy in self.copies:
                copy.wait_recv()
            side[0] = (wide_sum[0, pl.ds(z * self.rows, self.rows), :] + part_in[0]) + (part_in[1] + part_in[2])
            self.crossing = self.launch(side.at[0], side.at[1], sum_sem, (2,), opposite)

        def spread(self):
            self.crossing.wait_recv()
            full[self.mine_rows, :] = side[0] + side[1]
            target = full.at[self.mine_rows]
            self.copies = [self.launch(target, target, line_sem, (1, at), peer) for at, _, peer in self.line()]

        def widen(self):
            for copy in self.copies:
                copy.wait_recv()
            target = full.at[self.wide_rows]
            self.second = self.launch(target, target, sum_sem, (4,), across)

        def finish(self):
            self.second.wait_recv()
            target = full.at[self.half_rows]
            self.final = self.launch(target, target, sum_sem, (1,), partner)

        def tile(self, at):
            return full[pl.ds(at * half, half), :]

    owner_here = core == x

    class DirectTotal:
        def __init__(self, at, start, blocks):
            self.at, self.start, self.rows = at, start, blocks * half // CHIPS
            self.mine_rows = pl.ds(start + chip * self.rows, self.rows)

        def place(self, offset, core_at=None):
            z_at, y_at, x_at = flipped(*bits_of(offset))
            return (z_at * 2 + y_at) * 2 + x_at, device(z_at, y_at, x_at, x_at if core_at is None else core_at)

        def sending(self, offset):
            flat, peer = self.place(offset)
            return pltpu.make_async_remote_copy(
                src_ref=packed.at[pl.ds(self.start + flat * self.rows, self.rows)],
                dst_ref=straight.at[self.at, offset * 2 + core, pl.ds(0, self.rows)],
                send_sem=direct_send.at[self.at, 0 if offset else 1],
                recv_sem=direct_recv.at[self.at],
                device_id=peer,
                device_id_type=MESH,
            )

        def handing(self, offset, core_at):
            peer = partner if core_at is None else self.place(offset, core_at)[1]
            return pltpu.make_async_remote_copy(
                src_ref=full.at[self.mine_rows],
                dst_ref=full.at[self.mine_rows],
                send_sem=hand_send.at[self.at],
                recv_sem=hand_recv.at[self.at, 0 if offset else 1],
                device_id=peer,
                device_id_type=MESH,
            )

        def hands(self):
            return [self.handing(offset, core_at) for offset in far_chips for core_at in range(2)] + [
                self.handing(0, None)
            ]

        def begin(self, tiles):
            for at, tile in enumerate(tiles):
                packed[pl.ds(self.start + at * half, half), :] = tile
            for offset in far_chips:
                self.sending(offset).start()
            pl.when(jnp.logical_not(owner_here))(lambda: self.sending(0).start())

        def spread(self):
            @pl.when(owner_here)
            def _():
                rows = pl.ds(0, self.rows)
                take(straight.at[self.at, pl.ds(0, 2 * CHIPS - 1), rows], direct_recv.at[self.at])
                value = packed[self.mine_rows, :] + straight[self.at, 1 - core, rows, :]
                for slot in range(2, 2 * CHIPS):
                    value = value + straight[self.at, slot, rows, :]
                full[self.mine_rows, :] = value
                for copy in self.hands():
                    copy.start()

        def many(self, count):
            return packed.at[pl.ds(0, count * self.rows)]

        def finish(self):
            take(self.many(CHIPS - 1), hand_recv.at[self.at, 0])
            pl.when(jnp.logical_not(owner_here))(lambda: self.handing(0, None).wait_recv())

        def drain(self):
            take(self.many(CHIPS - 1), direct_send.at[self.at, 0])
            pl.when(jnp.logical_not(owner_here))(lambda: self.sending(0).wait_send())
            pl.when(owner_here)(lambda: take(self.many(2 * CHIPS - 1), hand_send.at[self.at]))

        def tile(self, at):
            return full[pl.ds(self.start + at * half, half), :]

    def quarters(value, places):
        return [value[i * half : (i + 1) * half, j * half : (j + 1) * half] for i, j in places]

    upper_places = ((0, 0), (0, 1), (1, 1))
    every_place = ((0, 0), (0, 1), (1, 0), (1, 1))
    tile_count = owner.shape[0]
    tile_rows = span // tile_count
    names = [owner[at] for at in range(tile_count)]
    ranks = [
        sum([jnp.where(names[before] == names[at], 1, 0) for before in range(at)], jnp.int32(0))
        for at in range(tile_count)
    ]
    tile_copies = []

    def send_tiles(part, values):
        columns = pl.ds(part * half, half)

        def slot_value(name, rank):
            value = jnp.zeros((tile_rows, half), jnp.float32)
            for at in range(tile_count):
                chosen = (names[at] == name) & (ranks[at] == rank)
                value = jnp.where(chosen, values[at * tile_rows : (at + 1) * tile_rows], value)
            return value

        for offset in range(1, COLS):
            name = lax.rem(col + offset, COLS)
            for rank in range(CAP):
                outgoing[offset - 1, rank, :, columns] = slot_value(name, rank)
            copy = remote(
                outgoing.at[offset - 1, :, :, columns],
                delivered.at[pl.ds(col * CAP, CAP), :, columns],
                tile_sem,
                (part, offset - 1),
                (row, name),
            )
            copy.start()
            tile_copies.append(copy)
        for rank in range(CAP):
            tiles_here[rank, :, columns] = slot_value(col, rank)

    first_total = LineTotal()
    middle_total, second_total = DirectTotal(0, 7 * half, 2), DirectTotal(1, 9 * half, 1)

    prepare(0)
    climb_turned(0)
    lax.fori_loop(0, 4, first_step, 0)
    prepare(1)
    def only(where, *steps):
        @pl.when(where)
        def _():
            for at, step in steps:
                forward(at, step)

    only(ends, (0, 0))
    later_steps((1,), 0, 4)
    only(middle, (0, 0))
    only(ends, (0, 1))
    prepare(2)
    prepare(3)
    only(ends, (0, 2))
    later_steps((2, 3), 0, 2)
    only(middle, (0, 1), (0, 2))
    only(ends, (1, 0))
    pass_on(0)
    pass_on(1)
    only(ends, (1, 1))
    collect(0)
    only(middle, (1, 0), (1, 1))
    forward(1, 2)
    only(ends, (2, 0))
    collect(1)
    only(ends, (3, 0))
    only(middle, (2, 0))
    one_row = mask_of(0, slots_of)
    two_row = mask_of(1, slots_of)
    inv_one_t[...] = -(jnp.concatenate([product[at] for at in range(per_panel)], axis=0) * one_row)
    for copy in passed:
        copy.wait_recv()
    panel_two_t[...] = resident[0, 1].T
    gram_one = exact(resident[0, 0].T, inv_one_t[...], last)
    cross_sum = exact(inv_one_t[...] * two_row, panel_two_t[...], last)
    first_total.begin(quarters(gram_one, upper_places) + quarters(cross_sum, every_place))
    above_t = above[...].T
    correction[...] = exact(above_t, inv_one_t[...], plain) * two_row
    inverse_one[...] = inv_one_t[...].T
    outs = [pltpu.make_async_copy(inverse_one, inverse_one_out, out_sem.at[0])]
    outs[0].start()
    first_total.scatter()
    later_steps((2, 3), 2, 3)
    only(ends, (2, 1))
    only(middle, (3, 0), (2, 1))
    later_steps((2, 3), 3, 4)
    first_total.climb()
    only(ends, (3, 1), (2, 2))
    only(middle, (2, 2), (3, 1))
    first_total.cross()
    forward(3, 2)
    first_total.spread()
    collect(2)
    low_half, high_half = pl.ds(0, half), pl.ds(half, half)
    part_two_t[low_half, :] = -(product[2] * two_row)
    gram_left = exact(panel_two_t[...], part_two_t[low_half, :], last)
    middle_total.begin([gram_left[:half], gram_left[half:]])
    send_tiles(0, (part_two_t[low_half, :] - correction[low_half, :]).T)
    collect(3)
    part_two_t[high_half, :] = -(product[3] * two_row)
    second_total.begin([exact(panel_two_t[high_half, :], part_two_t[high_half, :], last)])
    late = (part_two_t[high_half, :] - correction[high_half, :]).T
    first_total.widen()
    send_tiles(1, late)
    middle_total.spread()
    second_total.spread()
    first_total.finish()

    here = pltpu.make_async_copy(tiles_here, delivered.at[pl.ds(col * CAP, CAP)], out_sem.at[4])
    here.start()
    outs.append(here)

    def put(at, source, target):
        copy = pltpu.make_async_copy(source, target, out_sem.at[at])
        copy.start()
        outs.append(copy)

    def square(first, second, third, fourth):
        return jnp.concatenate(
            [jnp.concatenate([first, second], axis=1), jnp.concatenate([third, fourth], axis=1)], axis=0
        )

    for panel in range(2):

        @pl.when(turns)
        def _():
            turn[panel].wait_send()

        @pl.when(jnp.logical_not(turns))
        def _():
            end_climb(own, panel, 0, y)
            end_climb(turned, panel, 1, 1 - y)

        pl.when(relays_move)(lambda: passed[panel].wait_send())

    for copy in first_total.sent[:-1]:
        copy.wait_send()
    for kind, like in enumerate((own, own, land.at[0], other, mine.at[:, pl.ds(0, 3)])):
        take(like, flow_sem.at[kind])

    first_total.final.wait_recv()
    tile = first_total.tile
    diag_one_value = diag_one[...] - square(tile(0), tile(1), tile(1).T, tile(2))
    cross_total = square(tile(3), tile(4), tile(5), tile(6))
    diag_one[...] = diag_one_value
    put(1, diag_one, diag_one_out)
    cross_value = -(cross_total + exact(diag_one_value, above[...], plain))
    cross_two[...] = cross_value
    put(2, cross_two, cross_two_out)
    diag_two[...] = diag_two[...] + (exact(cross_total.T, above[...], plain) - exact(above_t, cross_value, plain))
    middle_total.finish()
    tile = middle_total.tile
    second_total.finish()
    diag_two[...] = diag_two[...] - square(tile(0), tile(1).T, tile(1), second_total.tile(0))
    put(3, diag_two, diag_two_out)

    for copy in tile_copies:
        copy.wait()
    for copy in outs:
        copy.wait()
    middle_total.drain()
    second_total.drain()
    first_total.final.wait_send()


def place_kernel(count, *refs):
    sources, targets, buffers, sems = refs[:count], refs[count : 2 * count], refs[2 * count : -1], refs[-1]
    loads = [pltpu.make_async_copy(sources[at], buffers[at], sems.at[0, at]) for at in range(count)]
    stores = [pltpu.make_async_copy(buffers[at], targets[at], sems.at[1, at]) for at in range(count)]
    for copy in loads:
        copy.start()
    for load, store in zip(loads, stores):
        load.wait()
        store.start()
    for copy in stores:
        copy.wait()


def fused(matrix, panel_one, panel_two, struct_one, struct_two, lower_one, above, lower_two, tile_owner):
    depth, _ = matrix.shape
    span, width = panel_one.shape
    chunk = 2 * width // CHUNKS
    tile_count = tile_owner.shape[0]
    share = 7 * (width // 2) // 2
    mask_rows = -(-(COLS + 1) * (span // LANES) // 8) * 8
    dma = pltpu.SemaphoreType.DMA
    vmem = lambda *shape: pltpu.VMEM(shape, jnp.float32)
    half_vmem = lambda *shape: pltpu.VMEM(shape, jnp.bfloat16)
    anywhere = pl.BlockSpec(memory_space=pl.ANY)
    scalars = pl.BlockSpec(memory_space=pltpu.SMEM)
    shape = lambda *dims: jax.ShapeDtypeStruct(dims, jnp.float32)
    results = pl.pallas_call(
        fused_kernel,
        out_shape=[
            shape(span, width),
            shape(width, width),
            shape(width, width),
            shape(width, width),
            shape(COLS * CAP, span // tile_count, width),
        ],
        in_specs=[anywhere] * 8 + [scalars],
        out_specs=[anywhere] * 5,
        scratch_shapes=[
            vmem(span, width),
            vmem(width, width),
            vmem(width, width),
            vmem(width, width),
            vmem(CAP, span // tile_count, width),
            pltpu.VMEM((struct_one.shape[0] // LANES, LANES), jnp.int32),
            pltpu.VMEM((struct_two.shape[0] // LANES, LANES), jnp.int32),
            vmem(width, width),
            vmem(width, width),
            vmem(width, width),
            vmem(2, depth, span),
            half_vmem(8, depth, span),
            half_vmem(8, depth, span),
            vmem(2, span, width),
            vmem(COLS, CHUNKS, span, chunk),
            half_vmem(CHUNKS, 2 * chunk, depth),
            vmem(CHUNKS, 4, chunk, span),
            vmem(CHUNKS, 4, chunk, span),
            vmem(CHUNKS, 4, chunk, span),
            vmem(CHUNKS, 5, chunk, span),
            vmem(2, mask_rows, LANES),
            vmem(2, span, width),
            vmem(2, 2, span, width),
            vmem(CHUNKS, chunk, span),
            vmem(width, span),
            vmem(width, span),
            vmem(width, span),
            vmem(width, span),
            vmem(10 * (width // 2), LANES),
            vmem(share, LANES),
            vmem(share, LANES),
            vmem(3, share // 8, LANES),
            vmem(2, share // 8, LANES),
            vmem(2, share // 2, LANES),
            vmem(2, 2 * CHIPS, width // CHIPS, LANES),
            vmem(10 * (width // 2), LANES),
            vmem(COLS - 1, CAP, span // tile_count, width),
            dma((5,)),
            dma((5,)),
            dma((2,)),
            dma((2,)),
            dma((2, 2)),
            dma((2, 2, 3)),
            dma((5,)),
            dma((3, CHUNKS)),
            dma((CHUNKS, 4)),
            dma((CHUNKS, 5)),
            dma((2, 5)),
            dma((2, 2, 3)),
            dma((2, 2)),
            dma((2,)),
            dma((2,)),
            dma((2, 2)),
            dma((2, 2, COLS - 1)),
        ],
        compiler_params=pltpu.CompilerParams(
            collective_id=3, has_side_effects=True, vmem_limit_bytes=58 * 2**20
        ),
        cost_estimate=pl.CostEstimate(
            flops=12 * matrix.size * width, bytes_accessed=4 * matrix.size, transcendentals=0
        ),
    )(
        matrix,
        panel_one,
        panel_two,
        struct_one.reshape(-1, LANES),
        struct_two.reshape(-1, LANES),
        lower_one,
        above,
        lower_two,
        tile_owner.reshape(-1),
    )
    return tuple(pl.pallas_call(
        functools.partial(place_kernel, len(results)),
        out_shape=[shape(*result.shape) for result in results],
        in_specs=[anywhere] * len(results),
        out_specs=[anywhere] * len(results),
        scratch_shapes=[vmem(*result.shape) for result in results] + [dma((2, len(results)))],
        compiler_params=pltpu.CompilerParams(vmem_limit_bytes=60 * 2**20),
    )(*results))


def local(
    ancestor_inverse,
    panel_one,
    struct_one,
    lower_one,
    panel_two,
    struct_two,
    panel_above,
    lower_two,
    tile_owner,
):
    row_count = lax.axis_size("row")
    col_count = lax.axis_size("col")
    row_index = lax.axis_index("row")
    col_index = lax.axis_index("col")
    local_rows = panel_one.shape[0]
    if fits_fused(ancestor_inverse, panel_one, struct_one, struct_two, tile_owner, row_count, col_count):
        return fused(
            ancestor_inverse,
            panel_one,
            panel_two,
            struct_one,
            struct_two,
            lower_one,
            panel_above,
            lower_two,
            tile_owner,
        )
    order = local_rows * row_count * col_count
    width = panel_one.shape[1]
    mask_one = row_mask(struct_one, order)
    mask_two = row_mask(struct_two, order)
    panel_start = (row_index * col_count + col_index) * local_rows
    result_start = (col_index * row_count + row_index) * local_rows
    local_one = panel_one * lax.dynamic_slice_in_dim(mask_one, panel_start, local_rows)[:, None]
    local_two = panel_two * lax.dynamic_slice_in_dim(mask_two, panel_start, local_rows)[:, None]
    result_mask_one = lax.dynamic_slice_in_dim(mask_one, result_start, local_rows)[:, None]
    result_mask_two = lax.dynamic_slice_in_dim(mask_two, result_start, local_rows)[:, None]

    both = jnp.concatenate([local_one, local_two], axis=1)
    gathered = lax.all_gather(both, "col", axis=0, tiled=True)
    product = scatter_rows(contract_rows(ancestor_inverse, gathered, lax.Precision.HIGH), row_count)
    moves = [(f, (f % row_count) * col_count + f // row_count) for f in range(row_count * col_count)]
    resident = lax.ppermute(both, ("row", "col"), moves)
    resident_one = resident[:, :width]
    resident_two = resident[:, width:]
    inverse_one = -product[:, :width] * result_mask_one
    inverse_two = -(product[:, width:] + matmul(inverse_one, panel_above)) * result_mask_two
    grams = (
        contract_rows(resident_one, inverse_one),
        contract_rows(inverse_one, resident_two),
        contract_rows(resident_two, inverse_two),
    )
    lanes = 128
    packed = jnp.concatenate(
        [gram[:, at : at + lanes] for gram in grams for at in range(0, width, lanes)], axis=0
    )
    sums = sum_everywhere(packed, row_count, col_count).reshape(len(grams), width // lanes, width, lanes)
    gram_one, cross_sum, gram_two = (
        jnp.concatenate([sums[at, block] for block in range(width // lanes)], axis=1) for at in range(len(grams))
    )
    diag_one = matmul(lower_one.T, lower_one) - gram_one
    cross_two = -(cross_sum + matmul(diag_one, panel_above))
    diag_two = matmul(lower_two.T, lower_two) - gram_two - matmul(panel_above.T, cross_two)
    delivered = deliver(inverse_two, tile_owner, col_count)
    return (inverse_one, diag_one, cross_two, diag_two, delivered)


def solution(mesh):
    return jax.shard_map(
        local,
        mesh=mesh,
        in_specs=(
            P("row", "col"),
            P(("row", "col"), None),
            P(),
            P(),
            P(("row", "col"), None),
            P(),
            P(),
            P(),
            P(("col", "row"), None),
        ),
        out_specs=(P(("col", "row"), None), P(), P(), P(), P(("row", "col"), None, None)),
        check_vma=False,
    )
```

```python
import functools

import jax
import jax.numpy as jnp
from jax import lax
from jax.experimental import pallas as pl
from jax.experimental.pallas import tpu as pltpu
from jax.sharding import PartitionSpec as P

CAP = 2


def matmul(left, right):
    return jnp.dot(left, right, precision=lax.Precision.HIGHEST, preferred_element_type=jnp.float32)


def contract_rows(left, right, precision=lax.Precision.HIGHEST):
    return lax.dot_general(
        left,
        right,
        (((0,), (0,)), ((), ())),
        precision=precision,
        preferred_element_type=jnp.float32,
    )


def row_mask(struct, count):
    lanes = 128
    high = struct // lanes
    low = struct % lanes
    high_hot = (jnp.arange(count // lanes, dtype=jnp.int32)[:, None] == high[None, :]).astype(jnp.bfloat16)
    low_hot = (jnp.arange(lanes, dtype=jnp.int32)[:, None] == low[None, :]).astype(jnp.bfloat16)
    counts = lax.dot_general(high_hot, low_hot, (((1,), (1,)), ((), ())), preferred_element_type=jnp.float32)
    return (counts > 0.5).astype(jnp.float32).reshape(count)


MESH = pl.DeviceIdType.MESH


def greet(peers):
    barrier = pltpu.get_barrier_semaphore()
    for peer in peers:
        pl.semaphore_signal(barrier, inc=1, device_id=peer, device_id_type=MESH)
    pl.semaphore_wait(barrier, len(peers))


def scatter_kernel(rows, value_ref, out_ref, pair_in, total, major_in, pair_send, pair_recv, major_send, major_recv):
    majors = rows // 2
    row = lax.axis_index("row")
    col = lax.axis_index("col")
    major, minor = row // 2, row % 2
    partner = (major * 2 + 1 - minor, col)

    def peer(offset):
        return (lax.rem(major + offset, majors) * 2 + minor, col)

    greet([partner] + [peer(offset) for offset in range(1, majors)])
    order = sorted(range(1, majors), key=lambda offset: -min(offset, majors - offset)) + [0]
    started = []
    pair_copies = {}
    for offset in order:
        target = lax.rem(major + offset, majors)
        copy = pltpu.make_async_remote_copy(
            src_ref=value_ref.at[target * 2 + 1 - minor],
            dst_ref=pair_in.at[offset],
            send_sem=pair_send.at[offset],
            recv_sem=pair_recv.at[offset],
            device_id=partner,
            device_id_type=MESH,
        )
        copy.start()
        pair_copies[offset] = copy
    for offset in order:
        target = lax.rem(major + offset, majors)
        pair_copies[offset].wait_recv()
        total[offset] = pair_in[offset] + value_ref[target * 2 + minor]
        if offset:
            copy = pltpu.make_async_remote_copy(
                src_ref=total.at[offset],
                dst_ref=major_in.at[offset - 1],
                send_sem=major_send.at[offset - 1],
                recv_sem=major_recv.at[offset - 1],
                device_id=peer(offset),
                device_id_type=MESH,
            )
            copy.start()
            started.append(copy)
    for copy in started:
        copy.wait_recv()
    result = total[0]
    for slot in range(majors - 1):
        result = result + major_in[slot]
    out_ref[...] = result
    for copy in started:
        copy.wait_send()
    for offset in order:
        pair_copies[offset].wait_send()


def scatter_rows(value, rows):
    chunk, width = value.shape[0] // rows, value.shape[1]
    majors = rows // 2
    dma = pltpu.SemaphoreType.DMA
    return pl.pallas_call(
        functools.partial(scatter_kernel, rows),
        out_shape=jax.ShapeDtypeStruct((chunk, width), jnp.float32),
        in_specs=[pl.BlockSpec(memory_space=pltpu.VMEM)],
        out_specs=pl.BlockSpec(memory_space=pltpu.VMEM),
        scratch_shapes=[
            pltpu.VMEM((majors, chunk, width), jnp.float32),
            pltpu.VMEM((majors, chunk, width), jnp.float32),
            pltpu.VMEM((majors - 1, chunk, width), jnp.float32),
            dma((majors,)),
            dma((majors,)),
            dma((majors - 1,)),
            dma((majors - 1,)),
        ],
        compiler_params=pltpu.CompilerParams(
            collective_id=0, has_side_effects=True, vmem_limit_bytes=40 * 2**20
        ),
    )(value.reshape(rows, chunk, width))


def sum_kernel(rows, cols, value_ref, out_ref, full, sum_a, sum_b, in_a, in_b, in_c, *sems):
    row = lax.axis_index("row")
    col = lax.axis_index("col")
    outer = cols // 2
    far, core = col // 2, col % 2
    half = outer * rows
    base_a = core * half
    base_b = base_a + far * rows
    base_c = base_b + row

    def pair_peer(offset):
        return (row, far * 2 + 1 - core)

    def far_peer(offset):
        return (row, lax.rem(far + offset, outer) * 2 + core)

    def row_peer(offset):
        return (lax.rem(row + offset, rows), col)

    greet(
        [pair_peer(1)]
        + [far_peer(offset) for offset in range(1, outer)]
        + [row_peer(offset) for offset in range(1, rows)]
    )

    def exchange(count, peer, source, landing, stage):
        copies = []
        for offset in range(1, count):
            copy = pltpu.make_async_remote_copy(
                src_ref=source(offset),
                dst_ref=landing(offset),
                send_sem=sems[2 * stage].at[offset - 1],
                recv_sem=sems[2 * stage + 1].at[offset - 1],
                device_id=peer(offset),
                device_id_type=MESH,
            )
            copy.start()
            copies.append(copy)
        for copy in copies:
            copy.wait_recv()
        return copies

    pending = []
    pending += exchange(
        2, pair_peer, lambda k: value_ref.at[pl.ds((1 - core) * half, half)], lambda k: in_a.at[k - 1], 0
    )
    sum_a[...] = value_ref[pl.ds(base_a, half)] + in_a[0]
    pending += exchange(
        outer, far_peer, lambda k: sum_a.at[pl.ds(lax.rem(far + k, outer) * rows, rows)], lambda k: in_b.at[k - 1], 1
    )
    total = sum_a[pl.ds(far * rows, rows)]
    for slot in range(outer - 1):
        total = total + in_b[slot]
    sum_b[...] = total
    pending += exchange(
        rows, row_peer, lambda k: sum_b.at[lax.rem(row + k, rows)], lambda k: in_c.at[k - 1], 2
    )
    total = sum_b[row]
    for slot in range(rows - 1):
        total = total + in_c[slot]
    full[base_c] = total
    pending += exchange(rows, row_peer, lambda k: full.at[base_c], lambda k: full.at[base_c], 3)
    pending += exchange(
        outer, far_peer, lambda k: full.at[pl.ds(base_b, rows)], lambda k: full.at[pl.ds(base_b, rows)], 4
    )
    pending += exchange(
        2, pair_peer, lambda k: full.at[pl.ds(base_a, half)], lambda k: full.at[pl.ds(base_a, half)], 5
    )
    out_ref[...] = full[...]
    for copy in pending:
        copy.wait_send()


def sum_everywhere(value, rows, cols):
    devices = rows * cols
    lanes = value.shape[1]
    depth = value.shape[0] // devices
    outer = cols // 2
    dma = pltpu.SemaphoreType.DMA
    vmem = lambda *lead: pltpu.VMEM(lead + (depth, lanes), jnp.float32)
    total = pl.pallas_call(
        functools.partial(sum_kernel, rows, cols),
        out_shape=jax.ShapeDtypeStruct((devices, depth, lanes), jnp.float32),
        in_specs=[pl.BlockSpec(memory_space=pltpu.VMEM)],
        out_specs=pl.BlockSpec(memory_space=pltpu.VMEM),
        scratch_shapes=[
            vmem(devices),
            vmem(devices // 2),
            vmem(rows),
            vmem(1, devices // 2),
            vmem(outer - 1, rows),
            vmem(rows - 1),
        ]
        + [dma((count - 1,)) for count in (2, outer, rows, rows, outer, 2) for _ in range(2)],
        compiler_params=pltpu.CompilerParams(
            collective_id=1, has_side_effects=True, vmem_limit_bytes=24 * 2**20
        ),
        cost_estimate=pl.CostEstimate(flops=0, bytes_accessed=100 * value.size * 4, transcendentals=0),
    )(value.reshape(devices, depth, lanes))
    return total.reshape(value.shape)


def deliver(values, tile_owner, col_count):
    tile_count = tile_owner.shape[0]
    tile_rows = values.shape[0] // tile_count
    all_tiles = values.reshape(tile_count, tile_rows, values.shape[1])
    owner_col = tile_owner[:, 0]
    col_ids = jnp.arange(col_count, dtype=jnp.int32)
    onehot = (owner_col[:, None] == col_ids[None, :]).astype(jnp.int32)
    tile_rank = jnp.sum((jnp.cumsum(onehot, axis=0) - onehot) * onehot, axis=1)
    slot_index = jnp.arange(CAP, dtype=jnp.int32)
    select = (
        (owner_col[None, None, :] == col_ids[:, None, None])
        & (tile_rank[None, None, :] == slot_index[None, :, None])
    ).astype(jnp.float32)
    outgoing = jnp.einsum("cks,srb->ckrb", select, all_tiles, precision=lax.Precision.HIGHEST)
    incoming = lax.all_to_all(outgoing, "col", split_axis=0, concat_axis=0, tiled=True)
    return incoming.reshape(col_count * CAP, tile_rows, values.shape[1])


ROWS, COLS, CHIPS = 8, 4, 16
CHUNKS = 4
LANES = 128


def fits_fused(matrix, panel, struct_one, struct_two, tile_owner, rows, cols):
    span, width = panel.shape
    return (
        (rows, cols) == (ROWS, COLS)
        and span % LANES == 0
        and width == 2 * LANES
        and matrix.shape == (cols * span, rows * span)
        and struct_one.shape[0] % LANES == 0
        and struct_two.shape[0] % LANES == 0
        and span % (8 * tile_owner.shape[0]) == 0
    )


def exact(left, right, contract):
    return lax.dot_general(
        left, right, (contract, ((), ())), precision=lax.Precision.HIGHEST, preferred_element_type=jnp.float32
    )


def fused_kernel(
    matrix, panel_one, panel_two, struct_one_in, struct_two_in, lower_one_in, above_in, lower_two_in, owner,
    inverse_one_out, diag_one_out, cross_two_out, diag_two_out, delivered,
    inverse_one, diag_one, cross_two, diag_two, tiles_here,
    struct_one, struct_two, lower_one, above, lower_two, window, high, low, own, land, left, other, mine, pair_in, major_in, masks, turned, resident, product,
    inv_one_t, part_two_t, panel_two_t, correction, packed, fold_in, fold, part_in, side, wide_sum, straight, full, outgoing,
    out_sem, small_sem, fetch_sem, own_sem, turn_sem, move_sem, flow_sem, gather_sem, pair_sem, major_sem, sum_sem, line_sem,
    direct_send, direct_recv, hand_send, hand_recv, tile_sem,
):
    row = lax.axis_index("row")
    col = lax.axis_index("col")
    z, y = row // 2, row % 2
    x, core = col // 2, col % 2
    upper, lower = z // 2, z % 2
    chip = (z * 2 + y) * 2 + x
    depth, total_columns = matrix.shape
    span, width = own.shape[1:]
    chunk = left.shape[1] // 2
    per_panel = width // chunk

    def device(z_at, y_at, x_at, core_at):
        return (z_at * 2 + y_at, x_at * 2 + core_at)

    partner = device(z, y, x, 1 - core)
    across = device(z, y, 1 - x, core)
    beside = device(z, 1 - y, x, core)
    near = device(upper * 2 + 1 - lower, y, x, core)
    inner = device(3 - z, y, x, core)
    ends = upper == lower
    middle = upper != lower

    def remote(source, target, sems, at, peer):
        return pltpu.make_async_remote_copy(
            src_ref=source,
            dst_ref=target,
            send_sem=sems.at[(0,) + at],
            recv_sem=sems.at[(1,) + at],
            device_id=peer,
            device_id_type=MESH,
        )

    own_copies = [
        pltpu.make_async_copy(panel, own.at[at], own_sem.at[at]) for at, panel in enumerate((panel_one, panel_two))
    ]
    for copy in own_copies:
        copy.start()

    def fetch(step, which):
        rank = jnp.where(ends, step, jnp.where(step == 0, 0, jnp.where(step == 3, 2, 5 - 2 * step)))
        target = jnp.where(upper == 0, 3 - rank, rank) * 2 + lax.rem(1 - y + which, 2)
        return pltpu.make_async_copy(
            matrix.at[:, pl.ds(pl.multiple_of(target * span, LANES), span)], window.at[which], fetch_sem.at[which]
        )

    small_pairs = (
        (struct_one_in, struct_one),
        (struct_two_in, struct_two),
        (lower_one_in, lower_one),
        (above_in, above),
        (lower_two_in, lower_two),
    )
    small_copies = [
        pltpu.make_async_copy(source, target, small_sem.at[at]) for at, (source, target) in enumerate(small_pairs)
    ]
    for copy in small_copies:
        copy.start()
    barrier = pltpu.get_barrier_semaphore()

    def greet_at(semaphore, peer):
        pl.semaphore_signal(semaphore, inc=1, device_id=peer, device_id_type=MESH)

    devices = ROWS * COLS
    for offset in range(devices - 1, 0, -1):
        up, below, over_y, over_x, over_core = (offset // size % 2 for size in (16, 8, 4, 2, 1))
        z_at = (1 - upper if up else upper) * 2 + (1 - lower if below else lower)
        there = (1 - y if over_y else y, 1 - x if over_x else x, 1 - core if over_core else core)
        greet_at(barrier, device(z_at, *there))
    for which in range(2):
        fetch(0, which).start()
    pl.semaphore_wait(barrier, devices - 1)
    for copy in own_copies:
        copy.wait()

    def piece(at):
        return own.at[at // per_panel, :, pl.ds(at % per_panel * chunk, chunk)]

    def flow(kind, source, target, recv_sem, peer):
        return pltpu.make_async_remote_copy(
            src_ref=source,
            dst_ref=target,
            send_sem=flow_sem.at[kind],
            recv_sem=recv_sem,
            device_id=peer,
            device_id_type=MESH,
        )

    def take(like, semaphore):
        pltpu.make_async_copy(like, like, semaphore).wait()

    def far_copy(at, source=None):
        source = land.at[0, at] if source is None else source
        return flow(0, source, land.at[col, at], gather_sem.at[0, at], across)

    def near_copy(at, source=None):
        source = land.at[0, at] if source is None else source
        return flow(1, source, land.at[col, at], gather_sem.at[1, at], partner)

    def relay_copy(at):
        slot = (1 - x) * 2 + core
        return flow(2, land.at[slot, at], land.at[slot, at], gather_sem.at[2, at], partner)

    turns = core != y
    direct = jnp.where(x == upper, 0, 1)
    relays_move = lower == x

    def move_copy(source, slot, panel, at, peer):
        return pltpu.make_async_remote_copy(
            src_ref=source.at[panel],
            dst_ref=resident.at[slot, panel],
            send_sem=move_sem.at[0, panel, at],
            recv_sem=move_sem.at[1, panel, slot],
            device_id=peer,
            device_id_type=MESH,
        )

    def climb(source, panel, at, from_y):
        peer = device(2 * from_y + x, y, x, lower)
        return move_copy(source, direct, panel, at, peer), (peer[0] == row) & (peer[1] == col)

    def start_climb(source, panel, at, from_y):
        copy, stays = climb(source, panel, at, from_y)
        kept = pltpu.make_async_copy(source.at[panel], resident.at[direct, panel], move_sem.at[1, panel, direct])
        pl.when(stays)(lambda: kept.start())
        pl.when(jnp.logical_not(stays))(lambda: copy.start())

    def end_climb(source, panel, at, from_y):
        copy, stays = climb(source, panel, at, from_y)
        pl.when(jnp.logical_not(stays))(lambda: copy.wait_send())

    turn = [remote(own.at[panel], turned.at[panel], turn_sem, (panel,), beside) for panel in range(2)]
    passed = [move_copy(resident.at[1], 0, panel, 2, across) for panel in range(2)]

    def climb_turned(panel):
        @pl.when(jnp.logical_not(turns))
        def _():
            turn[panel].wait_recv()
            start_climb(turned, panel, 1, 1 - y)

    def pass_on(panel):
        @pl.when(relays_move)
        def _():
            move_copy(own, 1, panel, 0, beside).wait_recv()
            passed[panel].start()

    for at in range(CHUNKS):
        far_copy(at, piece(at)).start()
        near_copy(at, piece(at)).start()
        if at == 0:
            @pl.when(turns)
            def _():
                for copy in turn:
                    copy.start()

            @pl.when(jnp.logical_not(turns))
            def _():
                for panel in range(2):
                    start_climb(own, panel, 0, y)

    for at in range(CHUNKS):
        land[col, at] = piece(at)[...]

    for copy in small_copies:
        copy.wait()
    blocks = span // LANES
    slots_of = COLS * blocks
    mask_rows = masks.shape[1]
    place_rows = lax.broadcasted_iota(jnp.int32, (mask_rows, LANES), 0)
    block_base = row * slots_of
    result_base = (col * ROWS + row) * blocks
    wanted = jnp.where(place_rows < slots_of, block_base + place_rows, result_base + place_rows - slots_of)
    lane_ids = lax.broadcasted_iota(jnp.int32, (LANES, LANES), 0)
    for at, struct in enumerate((struct_one, struct_two)):
        count = struct.shape[0]
        group = max(size for size in range(1, 17) if count % size == 0)
        counts = jnp.zeros((mask_rows, LANES), jnp.float32)
        for begin in range(0, count, group):
            highs, lows = [], []
            for entry in range(begin, begin + group):
                value = struct[pl.ds(entry, 1), :]
                highs.append(jnp.where(wanted == value // LANES, 1.0, 0.0))
                lows.append(jnp.where(lane_ids == value % LANES, 1.0, 0.0))
            counts = counts + lax.dot_general(
                jnp.concatenate(highs, axis=1).astype(jnp.bfloat16),
                jnp.concatenate(lows, axis=1).astype(jnp.bfloat16),
                (((1,), (1,)), ((), ())),
                preferred_element_type=jnp.float32,
            )
        masks[at] = jnp.where(counts > 0.5, 1.0, 0.0)
    diag_one[...] = exact(lower_one[...].T, lower_one[...], ((1,), (0,)))
    diag_two[...] = exact(lower_two[...].T, lower_two[...], ((1,), (0,)))

    def mask_of(panel, begin):
        return jnp.concatenate([masks[panel, pl.ds(begin + at, 1), :] for at in range(blocks)], axis=1)

    def prepare(at):
        near_copy(at).wait_recv()
        far_copy(at).wait_recv()
        relay_copy(at).start()
        relay_copy(at).wait_recv()
        for slot in range(COLS):
            value = land[slot, at].T * mask_of(at // per_panel, slot * blocks)
            upper_part = value.astype(jnp.bfloat16)
            columns = pl.ds(slot * span, span)
            left[at, pl.ds(0, chunk), columns] = upper_part
            left[at, pl.ds(chunk, chunk), columns] = (value - upper_part.astype(jnp.float32)).astype(jnp.bfloat16)

    def pair_copy(at, step):
        return flow(3, other.at[at, step], pair_in.at[at, step], pair_sem.at[at, step], beside)

    def multiply(at, step, which):
        target = step * 2 + which
        both = jnp.dot(left[at], high[target], preferred_element_type=jnp.float32)
        rest = jnp.dot(left[at, pl.ds(0, chunk), :], low[target], preferred_element_type=jnp.float32)
        value = both[:chunk] + (both[chunk:] + rest)
        if which == 0:
            other[at, step] = value
            pair_copy(at, step).start()
        else:
            mine[at, step] = value

    def first_step(step, carry):
        for which in range(2):
            fetch(step, which).wait()
            target = step * 2 + which
            for begin in range(0, depth, 256):
                size = min(256, depth - begin)
                value = window[which, pl.ds(begin, size), :]
                upper_part = value.astype(jnp.bfloat16)
                high[target, pl.ds(begin, size), :] = upper_part
                low[target, pl.ds(begin, size), :] = (value - upper_part.astype(jnp.float32)).astype(jnp.bfloat16)

            @pl.when(step + 1 < 4)
            def _():
                fetch(step + 1, which).start()

            multiply(0, step, which)
        pl.when(step == 1)(lambda: climb_turned(1))
        return carry

    def later_steps(chunks, begin, end):
        def body(step, carry):
            for at in chunks:
                for which in range(2):
                    multiply(at, step, which)
            return carry

        lax.fori_loop(begin, end, body, 0)

    def major_copy(at, step):
        slot = jnp.where(ends, (0, 2, 3)[step], (1, 3, 4)[step])
        peer = near if step == 1 else (jnp.where(ends, near[0], inner[0]), col)
        return flow(4, mine.at[at, step], major_in.at[at, slot], major_sem.at[at, slot], peer)

    def arrived(at, slot):
        pltpu.make_async_copy(mine.at[at, 0], major_in.at[at, slot], major_sem.at[at, slot]).wait()
        return major_in[at, slot]

    def forward(at, step):
        pair_copy(at, step).wait_recv()
        mine[at, step] = mine[at, step] + pair_in[at, step]

        @pl.when(middle)
        def _():
            mine[at, step] = mine[at, step] + arrived(at, step)

        major_copy(at, step).start()

    def collect(at):
        pair_copy(at, 3).wait_recv()
        product[at] = (mine[at, 3] + pair_in[at, 3]) + arrived(at, 3)

        @pl.when(middle)
        def _():
            product[at] = product[at] + arrived(at, 4)

    half = width // 2
    plain, last = ((1,), (0,)), ((1,), (1,))
    def flipped(upper_at, lower_at, y_at, x_at):
        z_at = jnp.where(upper_at, 1 - upper, upper) * 2 + jnp.where(lower_at, 1 - lower, lower)
        return z_at, jnp.where(y_at, 1 - y, y), jnp.where(x_at, 1 - x, x)

    def bits_of(offset):
        return offset // 8, offset // 4 % 2, offset // 2 % 2, offset % 2

    far_chips = sorted(range(1, CHIPS), key=lambda offset: -sum(w * b for w, b in zip((2.2, 1, 1, 1), bits_of(offset))))

    side_here = lax.rem(x + y, 2)
    opposite = device(z, 1 - y, 1 - x, core)

    class LineTotal:
        share = 7 * half // 2
        wide = share // 2
        rows = wide // 4

        def __init__(self):
            self.base = core * self.share
            self.half_rows = pl.ds(self.base, self.share)
            self.wide_rows = pl.ds(self.base + side_here * self.wide, self.wide)
            self.mine_rows = pl.ds(self.base + side_here * self.wide + z * self.rows, self.rows)
            self.sent = []

        def launch(self, *copy):
            copy = remote(*copy)
            copy.start()
            self.sent.append(copy)
            return copy

        def begin(self, tiles):
            for at, tile in enumerate(tiles):
                packed[pl.ds(at * half, half), :] = tile
            theirs = pl.ds((1 - core) * self.share, self.share)
            self.first = self.launch(packed.at[theirs], fold_in, sum_sem, (0,), partner)

        def scatter(self):
            self.first.wait_recv()
            fold[...] = packed[self.half_rows, :] + fold_in[...]
            theirs = pl.ds((1 - side_here) * self.wide, self.wide)
            self.second = self.launch(fold.at[theirs], wide_sum.at[1], sum_sem, (3,), across)

        def line(self):
            for at, (upper_at, lower_at) in enumerate(((1, 1), (1, 0), (0, 1))):
                z_at = flipped(upper_at, lower_at, 0, 0)[0]
                yield at, z_at, device(z_at, y, x, core)

        def climb(self):
            self.second.wait_recv()
            wide_sum[0] = fold[pl.ds(side_here * self.wide, self.wide), :] + wide_sum[1]
            self.copies = [
                self.launch(wide_sum.at[0, pl.ds(z_at * self.rows, self.rows)], part_in.at[at], line_sem, (0, at), peer)
                for at, z_at, peer in self.line()
            ]

        def cross(self):
            for copy in self.copies:
                copy.wait_recv()
            side[0] = (wide_sum[0, pl.ds(z * self.rows, self.rows), :] + part_in[0]) + (part_in[1] + part_in[2])
            self.crossing = self.launch(side.at[0], side.at[1], sum_sem, (2,), opposite)

        def spread(self):
            self.crossing.wait_recv()
            full[self.mine_rows, :] = side[0] + side[1]
            target = full.at[self.mine_rows]
            self.copies = [self.launch(target, target, line_sem, (1, at), peer) for at, _, peer in self.line()]

        def widen(self):
            for copy in self.copies:
                copy.wait_recv()
            target = full.at[self.wide_rows]
            self.second = self.launch(target, target, sum_sem, (4,), across)

        def finish(self):
            self.second.wait_recv()
            target = full.at[self.half_rows]
            self.final = self.launch(target, target, sum_sem, (1,), partner)

        def tile(self, at):
            return full[pl.ds(at * half, half), :]

    owner_here = core == x

    class DirectTotal:
        def __init__(self, at, start, blocks):
            self.at, self.start, self.rows = at, start, blocks * half // CHIPS
            self.mine_rows = pl.ds(start + chip * self.rows, self.rows)

        def place(self, offset, core_at=None):
            z_at, y_at, x_at = flipped(*bits_of(offset))
            return (z_at * 2 + y_at) * 2 + x_at, device(z_at, y_at, x_at, x_at if core_at is None else core_at)

        def sending(self, offset):
            flat, peer = self.place(offset)
            return pltpu.make_async_remote_copy(
                src_ref=packed.at[pl.ds(self.start + flat * self.rows, self.rows)],
                dst_ref=straight.at[self.at, offset * 2 + core, pl.ds(0, self.rows)],
                send_sem=direct_send.at[self.at, 0 if offset else 1],
                recv_sem=direct_recv.at[self.at],
                device_id=peer,
                device_id_type=MESH,
            )

        def handing(self, offset, core_at):
            peer = partner if core_at is None else self.place(offset, core_at)[1]
            return pltpu.make_async_remote_copy(
                src_ref=full.at[self.mine_rows],
                dst_ref=full.at[self.mine_rows],
                send_sem=hand_send.at[self.at],
                recv_sem=hand_recv.at[self.at, 0 if offset else 1],
                device_id=peer,
                device_id_type=MESH,
            )

        def hands(self):
            return [self.handing(offset, core_at) for offset in far_chips for core_at in range(2)] + [
                self.handing(0, None)
            ]

        def begin(self, tiles):
            for at, tile in enumerate(tiles):
                packed[pl.ds(self.start + at * half, half), :] = tile
            for offset in far_chips:
                self.sending(offset).start()
            pl.when(jnp.logical_not(owner_here))(lambda: self.sending(0).start())

        def spread(self):
            @pl.when(owner_here)
            def _():
                rows = pl.ds(0, self.rows)
                take(straight.at[self.at, pl.ds(0, 2 * CHIPS - 1), rows], direct_recv.at[self.at])
                value = packed[self.mine_rows, :] + straight[self.at, 1 - core, rows, :]
                for slot in range(2, 2 * CHIPS):
                    value = value + straight[self.at, slot, rows, :]
                full[self.mine_rows, :] = value
                for copy in self.hands():
                    copy.start()

        def many(self, count):
            return packed.at[pl.ds(0, count * self.rows)]

        def finish(self):
            take(self.many(CHIPS - 1), hand_recv.at[self.at, 0])
            pl.when(jnp.logical_not(owner_here))(lambda: self.handing(0, None).wait_recv())

        def drain(self):
            take(self.many(CHIPS - 1), direct_send.at[self.at, 0])
            pl.when(jnp.logical_not(owner_here))(lambda: self.sending(0).wait_send())
            pl.when(owner_here)(lambda: take(self.many(2 * CHIPS - 1), hand_send.at[self.at]))

        def tile(self, at):
            return full[pl.ds(self.start + at * half, half), :]

    def quarters(value, places):
        return [value[i * half : (i + 1) * half, j * half : (j + 1) * half] for i, j in places]

    upper_places = ((0, 0), (0, 1), (1, 1))
    every_place = ((0, 0), (0, 1), (1, 0), (1, 1))
    tile_count = owner.shape[0]
    tile_rows = span // tile_count
    names = [owner[at] for at in range(tile_count)]
    ranks = [
        sum([jnp.where(names[before] == names[at], 1, 0) for before in range(at)], jnp.int32(0))
        for at in range(tile_count)
    ]
    tile_copies = []

    def send_tiles(part, values):
        columns = pl.ds(part * half, half)

        def slot_value(name, rank):
            value = jnp.zeros((tile_rows, half), jnp.float32)
            for at in range(tile_count):
                chosen = (names[at] == name) & (ranks[at] == rank)
                value = jnp.where(chosen, values[at * tile_rows : (at + 1) * tile_rows], value)
            return value

        for offset in range(1, COLS):
            name = lax.rem(col + offset, COLS)
            for rank in range(CAP):
                outgoing[offset - 1, rank, :, columns] = slot_value(name, rank)
            copy = remote(
                outgoing.at[offset - 1, :, :, columns],
                delivered.at[pl.ds(col * CAP, CAP), :, columns],
                tile_sem,
                (part, offset - 1),
                (row, name),
            )
            copy.start()
            tile_copies.append(copy)
        for rank in range(CAP):
            tiles_here[rank, :, columns] = slot_value(col, rank)

    first_total = LineTotal()
    middle_total, second_total = DirectTotal(0, 7 * half, 2), DirectTotal(1, 9 * half, 1)

    prepare(0)
    climb_turned(0)
    lax.fori_loop(0, 4, first_step, 0)
    prepare(1)
    def only(where, *steps):
        @pl.when(where)
        def _():
            for at, step in steps:
                forward(at, step)

    only(ends, (0, 0))
    later_steps((1,), 0, 4)
    only(middle, (0, 0))
    only(ends, (0, 1))
    prepare(2)
    prepare(3)
    only(ends, (0, 2))
    later_steps((2, 3), 0, 2)
    only(middle, (0, 1), (0, 2))
    only(ends, (1, 0))
    pass_on(0)
    pass_on(1)
    only(ends, (1, 1))
    collect(0)
    only(middle, (1, 0), (1, 1))
    forward(1, 2)
    only(ends, (2, 0))
    collect(1)
    only(ends, (3, 0))
    only(middle, (2, 0))
    one_row = mask_of(0, slots_of)
    two_row = mask_of(1, slots_of)
    inv_one_t[...] = -(jnp.concatenate([product[at] for at in range(per_panel)], axis=0) * one_row)
    for copy in passed:
        copy.wait_recv()
    panel_two_t[...] = resident[0, 1].T
    gram_one = exact(resident[0, 0].T, inv_one_t[...], last)
    cross_sum = exact(inv_one_t[...] * two_row, panel_two_t[...], last)
    first_total.begin(quarters(gram_one, upper_places) + quarters(cross_sum, every_place))
    above_t = above[...].T
    correction[...] = exact(above_t, inv_one_t[...], plain) * two_row
    inverse_one[...] = inv_one_t[...].T
    outs = [pltpu.make_async_copy(inverse_one, inverse_one_out, out_sem.at[0])]
    outs[0].start()
    first_total.scatter()
    later_steps((2, 3), 2, 3)
    only(ends, (2, 1))
    only(middle, (3, 0), (2, 1))
    later_steps((2, 3), 3, 4)
    first_total.climb()
    only(ends, (3, 1), (2, 2))
    only(middle, (2, 2), (3, 1))
    first_total.cross()
    forward(3, 2)
    first_total.spread()
    collect(2)
    low_half, high_half = pl.ds(0, half), pl.ds(half, half)
    part_two_t[low_half, :] = -(product[2] * two_row)
    gram_left = exact(panel_two_t[...], part_two_t[low_half, :], last)
    middle_total.begin([gram_left[:half], gram_left[half:]])
    send_tiles(0, (part_two_t[low_half, :] - correction[low_half, :]).T)
    collect(3)
    part_two_t[high_half, :] = -(product[3] * two_row)
    second_total.begin([exact(panel_two_t[high_half, :], part_two_t[high_half, :], last)])
    late = (part_two_t[high_half, :] - correction[high_half, :]).T
    first_total.widen()
    send_tiles(1, late)
    middle_total.spread()
    second_total.spread()
    first_total.finish()

    here = pltpu.make_async_copy(tiles_here, delivered.at[pl.ds(col * CAP, CAP)], out_sem.at[4])
    here.start()
    outs.append(here)

    def put(at, source, target):
        copy = pltpu.make_async_copy(source, target, out_sem.at[at])
        copy.start()
        outs.append(copy)

    def square(first, second, third, fourth):
        return jnp.concatenate(
            [jnp.concatenate([first, second], axis=1), jnp.concatenate([third, fourth], axis=1)], axis=0
        )

    for panel in range(2):

        @pl.when(turns)
        def _():
            turn[panel].wait_send()

        @pl.when(jnp.logical_not(turns))
        def _():
            end_climb(own, panel, 0, y)
            end_climb(turned, panel, 1, 1 - y)

        pl.when(relays_move)(lambda: passed[panel].wait_send())

    for copy in first_total.sent[:-1]:
        copy.wait_send()
    for kind, like in enumerate((own, own, land.at[0], other, mine.at[:, pl.ds(0, 3)])):
        take(like, flow_sem.at[kind])

    first_total.final.wait_recv()
    tile = first_total.tile
    diag_one_value = diag_one[...] - square(tile(0), tile(1), tile(1).T, tile(2))
    cross_total = square(tile(3), tile(4), tile(5), tile(6))
    diag_one[...] = diag_one_value
    put(1, diag_one, diag_one_out)
    cross_value = -(cross_total + exact(diag_one_value, above[...], plain))
    cross_two[...] = cross_value
    put(2, cross_two, cross_two_out)
    diag_two[...] = diag_two[...] + (exact(cross_total.T, above[...], plain) - exact(above_t, cross_value, plain))
    middle_total.finish()
    tile = middle_total.tile
    second_total.finish()
    diag_two[...] = diag_two[...] - square(tile(0), tile(1).T, tile(1), second_total.tile(0))
    put(3, diag_two, diag_two_out)

    for copy in tile_copies:
        copy.wait()
    for copy in outs:
        copy.wait()
    middle_total.drain()
    second_total.drain()
    first_total.final.wait_send()


def place_kernel(count, *refs):
    sources, targets, buffers, sems = refs[:count], refs[count : 2 * count], refs[2 * count : -1], refs[-1]
    loads = [pltpu.make_async_copy(sources[at], buffers[at], sems.at[0, at]) for at in range(count)]
    stores = [pltpu.make_async_copy(buffers[at], targets[at], sems.at[1, at]) for at in range(count)]
    for copy in reversed(loads):
        copy.start()
    for load, store in reversed(list(zip(loads, stores))):
        load.wait()
        store.start()
    for copy in stores:
        copy.wait()


def fused(matrix, panel_one, panel_two, struct_one, struct_two, lower_one, above, lower_two, tile_owner):
    depth, _ = matrix.shape
    span, width = panel_one.shape
    chunk = 2 * width // CHUNKS
    tile_count = tile_owner.shape[0]
    share = 7 * (width // 2) // 2
    mask_rows = -(-(COLS + 1) * (span // LANES) // 8) * 8
    dma = pltpu.SemaphoreType.DMA
    vmem = lambda *shape: pltpu.VMEM(shape, jnp.float32)
    half_vmem = lambda *shape: pltpu.VMEM(shape, jnp.bfloat16)
    anywhere = pl.BlockSpec(memory_space=pl.ANY)
    scalars = pl.BlockSpec(memory_space=pltpu.SMEM)
    shape = lambda *dims: jax.ShapeDtypeStruct(dims, jnp.float32)
    results = pl.pallas_call(
        fused_kernel,
        out_shape=[
            shape(span, width),
            shape(width, width),
            shape(width, width),
            shape(width, width),
            shape(COLS * CAP, span // tile_count, width),
        ],
        in_specs=[anywhere] * 8 + [scalars],
        out_specs=[anywhere] * 5,
        scratch_shapes=[
            vmem(span, width),
            vmem(width, width),
            vmem(width, width),
            vmem(width, width),
            vmem(CAP, span // tile_count, width),
            pltpu.VMEM((struct_one.shape[0] // LANES, LANES), jnp.int32),
            pltpu.VMEM((struct_two.shape[0] // LANES, LANES), jnp.int32),
            vmem(width, width),
            vmem(width, width),
            vmem(width, width),
            vmem(2, depth, span),
            half_vmem(8, depth, span),
            half_vmem(8, depth, span),
            vmem(2, span, width),
            vmem(COLS, CHUNKS, span, chunk),
            half_vmem(CHUNKS, 2 * chunk, depth),
            vmem(CHUNKS, 4, chunk, span),
            vmem(CHUNKS, 4, chunk, span),
            vmem(CHUNKS, 4, chunk, span),
            vmem(CHUNKS, 5, chunk, span),
            vmem(2, mask_rows, LANES),
            vmem(2, span, width),
            vmem(2, 2, span, width),
            vmem(CHUNKS, chunk, span),
            vmem(width, span),
            vmem(width, span),
            vmem(width, span),
            vmem(width, span),
            vmem(10 * (width // 2), LANES),
            vmem(share, LANES),
            vmem(share, LANES),
            vmem(3, share // 8, LANES),
            vmem(2, share // 8, LANES),
            vmem(2, share // 2, LANES),
            vmem(2, 2 * CHIPS, width // CHIPS, LANES),
            vmem(10 * (width // 2), LANES),
            vmem(COLS - 1, CAP, span // tile_count, width),
            dma((5,)),
            dma((5,)),
            dma((2,)),
            dma((2,)),
            dma((2, 2)),
            dma((2, 2, 3)),
            dma((5,)),
            dma((3, CHUNKS)),
            dma((CHUNKS, 4)),
            dma((CHUNKS, 5)),
            dma((2, 5)),
            dma((2, 2, 3)),
            dma((2, 2)),
            dma((2,)),
            dma((2,)),
            dma((2, 2)),
            dma((2, 2, COLS - 1)),
        ],
        compiler_params=pltpu.CompilerParams(
            collective_id=3, has_side_effects=True, vmem_limit_bytes=58 * 2**20
        ),
        cost_estimate=pl.CostEstimate(
            flops=12 * matrix.size * width, bytes_accessed=4 * matrix.size, transcendentals=0
        ),
    )(
        matrix,
        panel_one,
        panel_two,
        struct_one.reshape(-1, LANES),
        struct_two.reshape(-1, LANES),
        lower_one,
        above,
        lower_two,
        tile_owner.reshape(-1),
    )
    return tuple(pl.pallas_call(
        functools.partial(place_kernel, len(results)),
        out_shape=[shape(*result.shape) for result in results],
        in_specs=[anywhere] * len(results),
        out_specs=[anywhere] * len(results),
        scratch_shapes=[vmem(*result.shape) for result in results] + [dma((2, len(results)))],
        compiler_params=pltpu.CompilerParams(vmem_limit_bytes=60 * 2**20),
    )(*results))


def local(
    ancestor_inverse,
    panel_one,
    struct_one,
    lower_one,
    panel_two,
    struct_two,
    panel_above,
    lower_two,
    tile_owner,
):
    row_count = lax.axis_size("row")
    col_count = lax.axis_size("col")
    row_index = lax.axis_index("row")
    col_index = lax.axis_index("col")
    local_rows = panel_one.shape[0]
    if fits_fused(ancestor_inverse, panel_one, struct_one, struct_two, tile_owner, row_count, col_count):
        return fused(
            ancestor_inverse,
            panel_one,
            panel_two,
            struct_one,
            struct_two,
            lower_one,
            panel_above,
            lower_two,
            tile_owner,
        )
    order = local_rows * row_count * col_count
    width = panel_one.shape[1]
    mask_one = row_mask(struct_one, order)
    mask_two = row_mask(struct_two, order)
    panel_start = (row_index * col_count + col_index) * local_rows
    result_start = (col_index * row_count + row_index) * local_rows
    local_one = panel_one * lax.dynamic_slice_in_dim(mask_one, panel_start, local_rows)[:, None]
    local_two = panel_two * lax.dynamic_slice_in_dim(mask_two, panel_start, local_rows)[:, None]
    result_mask_one = lax.dynamic_slice_in_dim(mask_one, result_start, local_rows)[:, None]
    result_mask_two = lax.dynamic_slice_in_dim(mask_two, result_start, local_rows)[:, None]

    both = jnp.concatenate([local_one, local_two], axis=1)
    gathered = lax.all_gather(both, "col", axis=0, tiled=True)
    product = scatter_rows(contract_rows(ancestor_inverse, gathered, lax.Precision.HIGH), row_count)
    moves = [(f, (f % row_count) * col_count + f // row_count) for f in range(row_count * col_count)]
    resident = lax.ppermute(both, ("row", "col"), moves)
    resident_one = resident[:, :width]
    resident_two = resident[:, width:]
    inverse_one = -product[:, :width] * result_mask_one
    inverse_two = -(product[:, width:] + matmul(inverse_one, panel_above)) * result_mask_two
    grams = (
        contract_rows(resident_one, inverse_one),
        contract_rows(inverse_one, resident_two),
        contract_rows(resident_two, inverse_two),
    )
    lanes = 128
    packed = jnp.concatenate(
        [gram[:, at : at + lanes] for gram in grams for at in range(0, width, lanes)], axis=0
    )
    sums = sum_everywhere(packed, row_count, col_count).reshape(len(grams), width // lanes, width, lanes)
    gram_one, cross_sum, gram_two = (
        jnp.concatenate([sums[at, block] for block in range(width // lanes)], axis=1) for at in range(len(grams))
    )
    diag_one = matmul(lower_one.T, lower_one) - gram_one
    cross_two = -(cross_sum + matmul(diag_one, panel_above))
    diag_two = matmul(lower_two.T, lower_two) - gram_two - matmul(panel_above.T, cross_two)
    delivered = deliver(inverse_two, tile_owner, col_count)
    return (inverse_one, diag_one, cross_two, diag_two, delivered)


def solution(mesh):
    return jax.shard_map(
        local,
        mesh=mesh,
        in_specs=(
            P("row", "col"),
            P(("row", "col"), None),
            P(),
            P(),
            P(("row", "col"), None),
            P(),
            P(),
            P(),
            P(("col", "row"), None),
        ),
        out_specs=(P(("col", "row"), None), P(), P(), P(), P(("row", "col"), None, None)),
        check_vma=False,
    )
```
